128 devices in a mesh: shaft: 16 (over y, z), lat: 8 (over x, core).
Axes of the slice: x: 4, y: 4, z: 4, core: 2. Of those that a mesh axis runs over, the one named last changes fastest.
Arguments:
- sphere_position: float32 [3, 16, 16, 8, 128], P(None, 'shaft', 'lat'), may hold values from 0 to 5
- sphere_velocity: float32 [3, 16, 16, 8, 128], P(None, 'shaft', 'lat'), may hold values from -6 to 6
- sphere_radius: float32 [16, 16, 8, 128], P('shaft', 'lat'), may hold values from 0.4 to 0.6
- sphere_offset: float32 [3, 16, 16, 8, 128], P(None, 'shaft', 'lat'), may hold values from -6 to 6
- sphere_piece: int32 [16, 8, 2048], P('shaft', 'lat'), may hold values from 0 to 511, never falling along the last dimension, each value on 1 to 64 neighbouring positions
- piece_route: int32 [16, 8, 512], P('shaft', 'lat'), may hold values from 0 to 8, as said below
- piece_clump: int32 [16, 8, 512], P('shaft', 'lat'), may hold values from 0 to 255
- blade_phase: int32 [1], replicated, may hold values from 0 to 63
- clump_centre: float32 [3, 16, 8, 256], P(None, 'shaft', 'lat'), may hold values from -6 to 6
- clump_motion: float32 [6, 16, 8, 256], P(None, 'shaft', 'lat'), may hold values from -6 to 6
- clump_angles: float32 [3, 16, 8, 256], P(None, 'shaft', 'lat'), may hold values from -3.140625 to 3.140625
- clump_inverse_mass: float32 [16, 8, 256], P('shaft', 'lat'), may hold values from 0.05 to 0.5
- clump_inverse_inertia: float32 [3, 16, 8, 256], P(None, 'shaft', 'lat'), may hold values from 0.01 to 0.1
Outputs:
- clump_next: float32 [9, 16, 8, 256], P(None, 'shaft', 'lat')
- sphere_next: float32 [6, 16, 16, 8, 128], P(None, 'shaft', 'lat')
The draws below stay inside these ranges and needn't reach their ends.
Inputs may be any that keep to these rules, and one draw needn't show every extreme that they name: `sphere_piece`: each device's spheres, in the order of the steps, form 512 runs of consecutive spheres numbered in order, each of 1 to 64 spheres; some run has exactly 64. `piece_route`: a code never names a lateral index outside the slabs; on every device no code is named by more than 128 pieces, and one code exactly 128 times.
All inputs are finite; a program needn't handle non-finite values.
Results may differ from the reference program's by a relative error of at most 0.0003.
Values sent between devices are 32-bit elements; how exact they have to be, the bound alone decides.
A program may use at most 128 MiB of HBM per device.

```python
import math
import jax
import jax.numpy as jnp
import numpy as np
from jax import lax

SHAFT_SIDE = 1
LAT_SIDE = 2
HEIGHT = 8
CELL_SPHERES = 128
PIECES_DEV = 512
CLUMPS_DEV = 256
PIECE_MOST = 64
PHASES = 64
SHAFT_CELLS = 16
LAT_CELLS = 16
SPHERES_DEV = 2048
CAPACITY = 128
N_SHAFT = 16
N_LAT = 8


def draw_piece_route(key, part):
    device_count = N_SHAFT * N_LAT
    slot_total = 9 * CAPACITY

    def one_device(device_key, lat_index):
        busy_key, shaft_key, rank_key, order_key = jax.random.split(device_key, 4)
        lowest = jnp.where(lat_index > 0, 0, 1)
        highest = jnp.where(lat_index < N_LAT - 1, 3, 2)
        busy_lat = jax.random.randint(busy_key, (), lowest, highest)
        busy_shaft = jax.random.randint(shaft_key, (), 0, 3)
        busy_code = busy_shaft * 3 + busy_lat
        slot_code = jnp.arange(slot_total, dtype=jnp.int32) // CAPACITY
        target_lat = lat_index + slot_code % 3 - 1
        allowed = (target_lat >= 0) & (target_lat < N_LAT)
        ranking = jax.random.permutation(rank_key, slot_total).astype(jnp.int32)
        level = jnp.where(slot_code == busy_code, 0, jnp.where(allowed, 1, 2)).astype(jnp.int32)
        score = ranking + slot_total * level
        picked = jnp.argsort(score, stable=True)[:PIECES_DEV]
        chosen = slot_code[picked]
        return jax.random.permutation(order_key, chosen).astype(jnp.int32)
    device_keys = jax.random.split(jax.random.fold_in(key, 23), device_count)
    lat_of = (jnp.arange(device_count, dtype=jnp.int32) % N_LAT).astype(jnp.int32)
    codes = jax.vmap(one_device)(device_keys, lat_of)
    return codes.reshape(N_SHAFT, N_LAT, PIECES_DEV).astype(jnp.int32)


def plant(values, rng, low, largest):
    longest = values.shape.index(max(values.shape))
    spots = []
    for shift in (0, 1):
        where = [jax.random.randint(jax.random.fold_in(rng, axis), (), 0, length) for axis, length in enumerate(values.shape)]
        where[longest] = (where[longest] + shift) % values.shape[longest]
        spots.append(tuple(where))
    return values.at[spots[0]].set(low).at[spots[1]].set(largest)


def shard_levels(stream_key, extent, shards, smallest, top_value):
    def one(axis_at, blocks):
        draws = jax.random.uniform(jax.random.fold_in(jax.random.fold_in(stream_key, 6), axis_at), (blocks,), jnp.float32, smallest / len(shards), top_value / len(shards))
        return jnp.repeat(jnp.exp(draws), extent[axis_at] // blocks).reshape((-1,) + (1,) * (len(extent) - axis_at - 1))

    loudness = one(*shards[0])
    for cut in shards[1:]:
        loudness = loudness * one(*cut)
    return loudness


def profile(amount, total, bound, slope):
    loads = [(1 << 20) // math.isqrt(standing ** slope) + 1 for standing in range(2, amount + 1)]
    surplus, holding = total - bound - (amount - 1), [1] * (amount - 1)
    while surplus > 0:
        movable = [i for i in range(amount - 1) if holding[i] < bound]
        mass, left = sum([loads[i] for i in movable]), surplus
        for i in movable:
            addition = min(bound - holding[i], max(1, left * loads[i] // mass), surplus)
            holding[i] = holding[i] + addition
            surplus = surplus - addition
    return np.array([bound] + holding)


def ragged_sizes(stream_key, amount, total, limit, skew):
    if amount == 2:
        one = jax.random.randint(stream_key, (), max(1, total - limit), min(limit, total - 1) + 1)
        return jnp.stack([one, total - one])
    sizes = jnp.asarray(profile(amount, total, limit, skew), jnp.int32)
    couples = (amount - 1) // 2
    giver, receiver = sizes[1:1 + 2 * couples:2], sizes[2:2 + 2 * couples:2]
    margin = jnp.minimum(giver - 1, limit - receiver)
    passed = jax.random.randint(jax.random.fold_in(stream_key, 1), (couples,), 0, 1 << 20) % (margin + 1)
    sizes = sizes.at[1:1 + 2 * couples:2].set(giver - passed).at[2:2 + 2 * couples:2].set(receiver + passed)
    return sizes[jax.random.permutation(jax.random.fold_in(stream_key, 2), amount)]


def normal_values(own_key, shape, scale, reach, shards=(), kind=jnp.bfloat16):
    gain = shard_levels(own_key, shape, shards, -0.22, 0.18) if shards else 1.0
    drawn = jax.random.normal(own_key, shape, jnp.float32) * scale * gain
    return jnp.minimum(jnp.maximum(drawn, -reach), reach).astype(kind)


def setup_inputs(seed: int = 0) -> dict:
    splits = jax.random.split(jax.random.key(seed), 14)
    sphere_position = jnp.clip(5.0 * jax.random.uniform(splits[0], (3, SHAFT_CELLS, LAT_CELLS, HEIGHT, CELL_SPHERES), jnp.float32) ** shard_levels(splits[0], (3, SHAFT_CELLS, LAT_CELLS, HEIGHT, CELL_SPHERES), ((1, 16), (2, 8)), -0.2, 0.2), 0.0, 5.0)
    sphere_velocity = normal_values(splits[1], (3, SHAFT_CELLS, LAT_CELLS, HEIGHT, CELL_SPHERES), 1.0, 6.0, ((1, 16), (2, 8)), jnp.float32)
    sphere_radius = jnp.clip(jnp.exp(math.log(0.6) - 0.40546513 * jax.random.uniform(splits[2], (SHAFT_CELLS, LAT_CELLS, HEIGHT, CELL_SPHERES), jnp.float32) ** shard_levels(splits[2], (SHAFT_CELLS, LAT_CELLS, HEIGHT, CELL_SPHERES), ((0, 16), (1, 8)), -0.2, 0.2)), 0.4, 0.6)
    sphere_offset = normal_values(splits[3], (3, SHAFT_CELLS, LAT_CELLS, HEIGHT, CELL_SPHERES), 1.5, 6.0, ((1, 16), (2, 8)), jnp.float32)
    sphere_piece = jax.vmap(lambda own: jnp.searchsorted(jnp.cumsum(ragged_sizes(own, PIECES_DEV, SPHERES_DEV, PIECE_MOST, 1)), jnp.arange(SPHERES_DEV), side="right"))(jax.random.split(splits[4], N_SHAFT * N_LAT)).reshape((N_SHAFT, N_LAT, SPHERES_DEV)).astype(jnp.int32)
    piece_route = draw_piece_route(jax.random.fold_in(splits[13], 71), 0)
    piece_clump = plant(jax.random.randint(splits[6], (N_SHAFT, N_LAT, PIECES_DEV), 0, CLUMPS_DEV), jax.random.fold_in(splits[6], 1), 0, CLUMPS_DEV - 1).astype(jnp.int32)
    blade_phase = jax.random.randint(splits[7], (1,), 0, PHASES).astype(jnp.int32)
    clump_centre = normal_values(splits[8], (3, N_SHAFT, N_LAT, CLUMPS_DEV), 1.0, 6.0, ((1, 16), (2, 8)), jnp.float32)
    clump_motion = normal_values(splits[9], (6, N_SHAFT, N_LAT, CLUMPS_DEV), 1.0, 6.0, ((1, 16), (2, 8)), jnp.float32)
    clump_angles = jnp.clip(jax.random.uniform(splits[10], (3, N_SHAFT, N_LAT, CLUMPS_DEV), jnp.float32, -3.140625, 3.140625), -3.140625, 3.140625)
    clump_inverse_mass = jnp.clip(jnp.exp(math.log(0.5) - 2.3025851 * jax.random.uniform(splits[11], (N_SHAFT, N_LAT, CLUMPS_DEV), jnp.float32) ** shard_levels(splits[11], (N_SHAFT, N_LAT, CLUMPS_DEV), ((0, 16), (1, 8)), -0.2, 0.2)), 0.05, 0.5)
    clump_inverse_inertia = jnp.clip(jnp.exp(math.log(0.1) - 2.3025851 * jax.random.uniform(splits[12], (3, N_SHAFT, N_LAT, CLUMPS_DEV), jnp.float32) ** shard_levels(splits[12], (3, N_SHAFT, N_LAT, CLUMPS_DEV), ((1, 16), (2, 8)), -0.2, 0.2)), 0.01, 0.1)
    return dict(sphere_position=sphere_position, sphere_velocity=sphere_velocity, sphere_radius=sphere_radius, sphere_offset=sphere_offset, sphere_piece=sphere_piece, piece_route=piece_route, piece_clump=piece_clump, blade_phase=blade_phase, clump_centre=clump_centre, clump_motion=clump_motion, clump_angles=clump_angles, clump_inverse_mass=clump_inverse_mass, clump_inverse_inertia=clump_inverse_inertia)


CELL_SIDE = 5.0
STIFFNESS = 10.0
NORMAL_DAMPING = 2.0
SHEAR_DAMPING = 2.0
COHESION = 0.5
FRICTION = 0.5
BLADE_STIFFNESS = 20.0
BLADE_THICKNESS = 1.0
TIME_STEP = 0.5
GRAVITY = 0.5

def offsets(tile_kind):
    packed = tile_kind + (tile_kind >= 13).astype(jnp.int32)
    return (packed // 9 - 1, packed // 3 % 3 - 1, packed % 3 - 1)

def cross_product(left, right):
    return jnp.stack([left[1] * right[2] - left[2] * right[1], left[2] * right[0] - left[0] * right[2], left[0] * right[1] - left[1] * right[0]], 0)

def pair_force(position_mine, velocity_mine, radius_mine, position_other, velocity_other, radius_other, keep_mask):
    separation = position_mine[:, :, :, None] - position_other[:, :, None, :]
    radius_sum = radius_mine[:, :, None] + radius_other[:, None, :]
    distance = jnp.sqrt(lax.optimization_barrier(jnp.sum(separation * separation, 0)))
    distance = jnp.maximum(distance, 0.25 * radius_sum)
    normal = separation / distance
    intersection = jnp.maximum(radius_sum - distance, 0.0)
    reduced = radius_mine[:, :, None] * radius_other[:, None, :] / radius_sum
    stiff_root = jnp.sqrt(reduced * intersection)
    relative = velocity_mine[:, :, :, None] - velocity_other[:, :, None, :]
    normal_speed = lax.optimization_barrier(jnp.sum(relative * normal, 0))
    sliding = relative - normal_speed * normal
    normal_force = stiff_root * (STIFFNESS * intersection - NORMAL_DAMPING * normal_speed - COHESION)
    friction_cap = FRICTION * STIFFNESS * stiff_root * intersection
    shear_force = -SHEAR_DAMPING * stiff_root * sliding
    factor = friction_cap / jnp.sqrt(lax.optimization_barrier(jnp.sum(shear_force * shear_force, 0)) + friction_cap * friction_cap + 1e-06)
    forces = (normal_force * normal + factor * shear_force) * keep_mask
    return lax.optimization_barrier(jnp.sum(forces, 3))

def tile_forces(source, mine, targets, shifts):
    tile_rows, per_cell = targets.shape
    cell_size = mine.shape[2]
    joined = tile_rows * per_cell
    others = jnp.take(source, targets.reshape(-1), axis=1)
    repeated = jnp.broadcast_to(mine[:, :, None, :], (7, tile_rows, per_cell, cell_size)).reshape(7, joined, cell_size)
    shifted = others[0:3] + shifts.reshape(3, joined)[:, :, None]
    first_kind = (jnp.arange(joined) % per_cell == 0).astype(jnp.float32)
    identity = jnp.eye(cell_size, dtype=jnp.float32)
    keep_mask = 1.0 - first_kind[:, None, None] * identity[None]
    forces = pair_force(repeated[0:3], repeated[3:6], repeated[6], shifted, others[3:6], others[6], keep_mask)
    return lax.optimization_barrier(jnp.sum(forces.reshape(3, tile_rows, per_cell, cell_size), 2))

def tile_lists(shaft_cell, lateral_cell, upward_cell, lat_cells, height_cells):
    cell_codes = jnp.broadcast_to(jnp.arange(26, dtype=jnp.int32)[None, :], (shaft_cell.shape[0], 26))
    step_shaft, step_lat, step_up = offsets(cell_codes)
    zero_col = jnp.zeros_like(cell_codes[:, :1])
    step_shaft = jnp.concatenate([zero_col, step_shaft], 1)
    step_lat = jnp.concatenate([zero_col, step_lat], 1)
    step_up = jnp.concatenate([zero_col, step_up], 1)
    targets = ((shaft_cell[:, None] + 1 + step_shaft) * (lat_cells + 2) + lateral_cell[:, None] + 1 + step_lat) * (height_cells + 2) + upward_cell[:, None] + 1 + step_up
    shifts = CELL_SIDE * jnp.stack([step_shaft, step_lat, step_up], 0).astype(jnp.float32)
    return (targets, shifts)

def blade_force(position, radius, shaft_cell, lateral_cell, upward_cell, blade_phase, lat_cells, height_cells, shaft_per_device):
    global_x = CELL_SIDE * shaft_cell.astype(jnp.float32) + position[0]
    global_y = CELL_SIDE * lateral_cell.astype(jnp.float32) + position[1]
    global_z = CELL_SIDE * upward_cell.astype(jnp.float32) + position[2]
    blade_angle = blade_phase[0].astype(jnp.float32) * (2.0 * math.pi / PHASES)
    blade_cos = jnp.cos(blade_angle)
    blade_sin = jnp.sin(blade_angle)
    centre_y = 0.5 * CELL_SIDE * lat_cells
    centre_z = 0.5 * CELL_SIDE * height_cells
    blade_reach = 0.45 * CELL_SIDE * min(lat_cells, height_cells)
    across = (global_y - centre_y) * blade_cos + (global_z - centre_z) * blade_sin
    radial = (global_z - centre_z) * blade_cos - (global_y - centre_y) * blade_sin
    contact_depth = jnp.maximum(jnp.minimum(radius - across, radius + BLADE_THICKNESS + across), 0.0)
    window = jnp.maximum(radial * (blade_reach - radial), 0.0) * (4.0 / (blade_reach * blade_reach))
    strip_gate = jnp.maximum(jnp.cos(global_x * (2.0 * math.pi / (2.0 * CELL_SIDE * shaft_per_device))), 0.0)
    magnitude = BLADE_STIFFNESS * contact_depth * window * strip_gate
    return jnp.stack([jnp.zeros_like(magnitude), magnitude * blade_cos, magnitude * blade_sin], 0)

def rigid_update(sums, centre, motion, angles, inverse_mass, inverse_inertia):
    gravity_vec = jnp.array([0.0, 0.0, -GRAVITY], dtype=jnp.float32)[:, None]
    velocity = motion[0:3] + TIME_STEP * (inverse_mass[None] * sums[0:3] + gravity_vec)
    cos_z, sin_z = (jnp.cos(angles[0]), jnp.sin(angles[0]))
    cos_y, sin_y = (jnp.cos(angles[1]), jnp.sin(angles[1]))
    cos_x, sin_x = (jnp.cos(angles[2]), jnp.sin(angles[2]))
    rotation = [[cos_z * cos_y, cos_z * sin_y * sin_x - sin_z * cos_x, cos_z * sin_y * cos_x + sin_z * sin_x], [sin_z * cos_y, sin_z * sin_y * sin_x + cos_z * cos_x, sin_z * sin_y * cos_x - cos_z * sin_x], [-sin_y, cos_y * sin_x, cos_y * cos_x]]
    torque = sums[3:6]
    body_torque = [sum((rotation[row_index][col_index] * torque[row_index] for row_index in range(3))) for col_index in range(3)]
    scaled = [inverse_inertia[col_index] * body_torque[col_index] for col_index in range(3)]
    world = jnp.stack([sum((rotation[row_index][col_index] * scaled[col_index] for col_index in range(3))) for row_index in range(3)], 0)
    spin = motion[3:6] + TIME_STEP * world
    centre_next = centre + TIME_STEP * velocity
    return (centre_next, velocity, spin)

def turn_offsets(offset, spin):
    half_turn = 0.5 * TIME_STEP * spin
    scale = 2.0 / (1.0 + lax.optimization_barrier(jnp.sum(half_turn * half_turn, 0)))
    first_cross = cross_product(half_turn, offset)
    return offset + scale * (first_cross + cross_product(half_turn, first_cross))

def per_device(whole_field):
    depth_count = whole_field.shape[0]
    divided = whole_field.reshape(depth_count, N_SHAFT, SHAFT_SIDE, N_LAT, LAT_SIDE, HEIGHT, CELL_SPHERES)
    return jnp.transpose(divided, (1, 3, 0, 2, 4, 5, 6)).reshape(N_SHAFT * N_LAT, depth_count, -1)

def from_device(flat_rows):
    depth_count = flat_rows.shape[0]
    divided = flat_rows.reshape(depth_count, N_SHAFT, N_LAT, SHAFT_SIDE, LAT_SIDE, HEIGHT, CELL_SPHERES)
    return jnp.transpose(divided, (0, 1, 3, 2, 4, 5, 6)).reshape(depth_count, SHAFT_CELLS, LAT_CELLS, HEIGHT, CELL_SPHERES)

def reference(sphere_position, sphere_velocity, sphere_radius, sphere_offset, sphere_piece, piece_route, piece_clump, blade_phase, clump_centre, clump_motion, clump_angles, clump_inverse_mass, clump_inverse_inertia):
    sphere_state = jnp.concatenate([sphere_position, sphere_velocity, sphere_radius[None]], 0)
    wrapped = jnp.concatenate([sphere_state[:, -1:], sphere_state, sphere_state[:, :1]], 1)
    extended = jnp.pad(wrapped, ((0, 0), (0, 0), (1, 1), (1, 1), (0, 0)))
    source = extended.reshape(7, -1, CELL_SPHERES)
    own_cells = sphere_state.reshape(7, -1, CELL_SPHERES)

    def cell_block(cell_ids):
        shaft_cell = cell_ids // (LAT_CELLS * HEIGHT)
        lateral_cell = cell_ids // HEIGHT % LAT_CELLS
        upward_cell = cell_ids % HEIGHT
        targets, shifts = tile_lists(shaft_cell, lateral_cell, upward_cell, LAT_CELLS, HEIGHT)
        return tile_forces(source, own_cells[:, cell_ids], targets, shifts)
    contact = lax.map(cell_block, jnp.arange(SHAFT_CELLS * LAT_CELLS * HEIGHT, dtype=jnp.int32).reshape(-1, 2 * HEIGHT))
    contact = jnp.transpose(contact, (1, 0, 2, 3)).reshape(3, SHAFT_CELLS, LAT_CELLS, HEIGHT, CELL_SPHERES)
    grid_shape = (SHAFT_CELLS, LAT_CELLS, HEIGHT, CELL_SPHERES)
    shaft_ids = lax.broadcasted_iota(jnp.int32, grid_shape, 0)
    lat_ids = lax.broadcasted_iota(jnp.int32, grid_shape, 1)
    height_ids = lax.broadcasted_iota(jnp.int32, grid_shape, 2)
    blade = blade_force(sphere_position, sphere_radius, shaft_ids, lat_ids, height_ids, blade_phase, LAT_CELLS, HEIGHT, SHAFT_SIDE)
    sphere_force = contact + blade
    moment = cross_product(sphere_offset, sphere_force)
    device_count = N_SHAFT * N_LAT
    terms = per_device(jnp.concatenate([sphere_force, moment], 0))
    piece_ids = (sphere_piece.reshape(device_count, SPHERES_DEV) + PIECES_DEV * jnp.arange(device_count, dtype=jnp.int32)[:, None]).reshape(-1)
    piece_sums = jax.ops.segment_sum(jnp.transpose(terms, (0, 2, 1)).reshape(-1, 6), piece_ids, num_segments=device_count * PIECES_DEV)
    device_ids = jnp.arange(device_count, dtype=jnp.int32)
    shaft_of = (device_ids // N_LAT)[:, None]
    lat_of = (device_ids % N_LAT)[:, None]
    codes = piece_route.reshape(device_count, PIECES_DEV)
    owner_device = (shaft_of + codes // 3 - 1) % N_SHAFT * N_LAT + lat_of + codes % 3 - 1
    owner_ids = (owner_device.reshape(-1) * CLUMPS_DEV + piece_clump.reshape(-1)).astype(jnp.int32)
    clump_sums = jax.ops.segment_sum(piece_sums, owner_ids, num_segments=device_count * CLUMPS_DEV).T
    centre_next, velocity, spin = rigid_update(clump_sums, clump_centre.reshape(3, -1), clump_motion.reshape(6, -1), clump_angles.reshape(3, -1), clump_inverse_mass.reshape(-1), clump_inverse_inertia.reshape(3, -1))
    clump_next = jnp.concatenate([centre_next, velocity, spin], 0).reshape(9, N_SHAFT, N_LAT, CLUMPS_DEV)
    motion_table = jnp.concatenate([velocity, spin], 0)
    sphere_pose = motion_table[:, owner_ids][:, piece_ids]
    offset_rows = jnp.transpose(per_device(sphere_offset), (1, 0, 2)).reshape(3, -1)
    turned = turn_offsets(offset_rows, sphere_pose[3:6])
    moving = sphere_pose[0:3] + cross_product(sphere_pose[3:6], turned)
    sphere_next = from_device(jnp.concatenate([turned, moving], 0))
    return (clump_next, sphere_next)
```

```python
import functools
import math

import jax
import jax.numpy as jnp
from jax import lax
from jax.experimental import pallas as pl
from jax.experimental.pallas import tpu as pltpu
from jax.sharding import PartitionSpec as P

PHASES = 64
CELL_SIDE = 5.0
BLADE_STIFFNESS = 20.0
BLADE_THICKNESS = 1.0
TIME_STEP = 0.5
GRAVITY = 0.5

REACH = 1.2001
CHUNK = 32
F32 = jnp.float32
BF16 = jnp.bfloat16
MESH = pl.DeviceIdType.MESH
LANES = (((1,), (1,)), ((), ()))
ROWS = (((1,), (0,)), ((), ()))
VMEM = pl.BlockSpec(memory_space=pltpu.VMEM)
SMEM = pl.BlockSpec(memory_space=pltpu.SMEM)
ANY = pl.BlockSpec(memory_space=pl.ANY)


def split3(x):
    high = x.astype(BF16)
    rest = x - high.astype(F32)
    middle = rest.astype(BF16)
    low = (rest - middle.astype(F32)).astype(BF16)
    return high, middle, low


def rows3(x):
    high = x.astype(BF16).astype(F32)
    rest = x - high
    middle = rest.astype(BF16).astype(F32)
    return jnp.concatenate([high, middle, rest - middle], 0).astype(BF16)


def sum3(x):
    return x[0:8] + x[8:16] + x[16:24]


def one_hot(rows, row):
    length = row.shape[-1]
    ids = lax.broadcasted_iota(jnp.int32, (rows, length), 0)
    return jnp.where(ids == row, 1.0, 0.0).astype(BF16)


class Place:
    def __init__(self, n_shaft, n_lat):
        self.n_shaft, self.n_lat = n_shaft, n_lat
        self.s, self.l = lax.axis_index("shaft"), lax.axis_index("lat")

    def at(self, ds, dl):
        return {"shaft": lax.rem(self.s + ds + self.n_shaft, self.n_shaft), "lat": self.l + dl}

    def lateral(self, act):
        act(0)
        pl.when(self.l > 0)(lambda: act(-1))
        pl.when(self.l < self.n_lat - 1)(lambda: act(1))

    def barrier(self):
        sem = pltpu.get_barrier_semaphore()

        def signal(dl):
            for ds in (-1, 0, 1):
                if (ds, dl) != (0, 0):
                    pl.semaphore_signal(
                        sem, inc=1, device_id=self.at(ds, dl), device_id_type=MESH
                    )

        self.lateral(signal)
        edge = jnp.logical_or(self.l == 0, self.l == self.n_lat - 1)
        pl.semaphore_wait(sem, jnp.where(edge, 5, 8))


def halo_kernel(n_shaft, n_lat, pos, vel, rad, ext, send_sem, recv_sem, own_sem):
    place = Place(n_shaft, n_lat)

    def parts(j, si, lj):
        return (
            (pos.at[:, 0, j], ext.at[si, lj, 0:3]),
            (vel.at[:, 0, j], ext.at[si, lj, 3:6]),
            (rad.at[0, pl.ds(j, 1)], ext.at[si, lj, 6:7]),
        )

    def remote(j, ds, dl, si, lj):
        return [
            pltpu.make_async_remote_copy(
                src_ref=src,
                dst_ref=dst,
                send_sem=send_sem.at[si, lj, t],
                recv_sem=recv_sem.at[si, lj, t],
                device_id=place.at(ds, dl),
                device_id_type=MESH,
            )
            for t, (src, dst) in enumerate(parts(j, si, lj))
        ]

    def outgoing(dl):
        found = []
        for ds in (-1, 0, 1):
            for j in (0, 1):
                lj = j - 2 * dl + 1
                if 0 <= lj <= 3 and (ds, dl) != (0, 0):
                    found += remote(j, ds, dl, 1 - ds, lj)
        return found

    def incoming(dl):
        found = []
        for ds in (-1, 0, 1):
            for lj in {0: (1, 2), -1: (0,), 1: (3,)}[dl]:
                if (ds, dl) != (0, 0):
                    found += remote(0, ds, dl, 1 + ds, lj)
        return found

    own = [
        pltpu.make_async_copy(src, dst, own_sem.at[j, t])
        for j in (0, 1)
        for t, (src, dst) in enumerate(parts(j, 1, 1 + j))
    ]
    place.barrier()
    place.lateral(lambda dl: [c.start() for c in outgoing(dl)] and None)
    for c in own:
        c.start()
    ext[:, :, 7] = jnp.zeros((3, 4, 8, 128), F32)

    @pl.when(place.l == 0)
    def _():
        ext[:, 0, 0:7] = jnp.zeros((3, 7, 8, 128), F32)

    @pl.when(place.l == n_lat - 1)
    def _():
        ext[:, 3, 0:7] = jnp.zeros((3, 7, 8, 128), F32)

    for c in own:
        c.wait()
    place.lateral(lambda dl: [c.wait_recv() for c in incoming(dl)] and None)
    place.lateral(lambda dl: [c.wait_send() for c in outgoing(dl)] and None)


def pair_sums(mine, other, acc):
    ax, ay, az, au, av, aw, ar, ar4 = mine
    bx, by, bz, bu, bv, bw, br = other
    dx, dy, dz = ax - bx, ay - by, az - bz
    square = dx * dx + dy * dy + dz * dz
    radii = ar + br
    clamped = jnp.maximum(square, radii * radii * 0.0625)
    inverse = lax.rsqrt(clamped)
    delta = jnp.maximum(radii - clamped * inverse, 0.0)
    du, dv, dw = au - bu, av - bv, aw - bw
    normal_speed = (du * dx + dv * dy + dw * dz) * inverse
    speed = du * du + dv * dv + dw * dw
    unit = square * (inverse * inverse)
    sliding = jnp.maximum(speed + normal_speed * normal_speed * (unit - 2.0), 0.0)
    load = ar4 * br * delta
    root = load * lax.rsqrt(jnp.maximum(load * radii, 1e-30))
    root2 = root * root
    cap = 2.5 * delta
    shear = root2 * cap * lax.rsqrt(root2 * (sliding + cap * cap) + 1e-06)
    push = root * (5.0 * delta - normal_speed - 0.25)
    along = (push + shear * normal_speed) * inverse
    return (
        acc[0] + (along * dx - shear * du),
        acc[1] + (along * dy - shear * dv),
        acc[2] + (along * dz - shear * dw),
    )


def contact_kernel(
    lat_cells,
    phase,
    ext,
    off,
    piece,
    route,
    clump,
    angles,
    inertia,
    part,
    turning,
    dest,
    count_v,
    count_s,
    bounds,
    picked,
    packed,
    force,
    copy_sem,
):
    sub = lax.broadcasted_iota(jnp.int32, (8, 128), 0)

    before = jnp.where(
        lax.broadcasted_iota(jnp.int32, (128, 128), 0)
        < lax.broadcasted_iota(jnp.int32, (128, 128), 1),
        1.0,
        0.0,
    ).astype(BF16)
    ones = jnp.ones((128, 128), BF16)
    for j in range(2):
        masks = []
        for c in range(9):
            di, dj = c // 3 - 1, c % 3 - 1
            base = ((1 + di) * 4 + 1 + j + dj) * 64
            x, y, z = (ext[base + 8 * t : base + 8 * t + 8, :] for t in range(3))
            keep = ext[base + 48 : base + 56, :] > 0.0
            if di:
                keep &= (x < REACH) if di > 0 else (x > CELL_SIDE - REACH)
            if dj:
                keep &= (y < REACH) if dj > 0 else (y > CELL_SIDE - REACH)
            low, high = z < REACH, z > CELL_SIDE - REACH
            kept = jnp.where(keep, 1.0, 0.0)
            low_f = jnp.where(low, kept, 0.0)
            high_f = jnp.where(high, kept, 0.0)
            masks += [low_f, kept - low_f - high_f, high_f]
        mask_f = jnp.concatenate(masks, 0)
        mask = mask_f.astype(BF16)
        prefix = lax.dot_general(mask, before, ROWS, preferred_element_type=F32)
        total = lax.dot_general(mask, ones, ROWS, preferred_element_type=F32)
        counts = lax.dot_general(ones[0:8], mask, LANES, preferred_element_type=F32)
        count_v[:, j * 256 : j * 256 + 216] = counts.astype(jnp.int32)
        for c in range(9):
            a = c * 24
            low_p, mid_p, high_p = (prefix[a + 8 * t : a + 8 * t + 8] for t in range(3))
            low_n, mid_n = total[a : a + 8], total[a + 8 : a + 16]
            spot = (
                masks[3 * c] * low_p
                + masks[3 * c + 1] * (low_n + mid_p)
                + masks[3 * c + 2] * (low_n + mid_n + high_p)
            )
            any_of = masks[3 * c] + masks[3 * c + 1] + masks[3 * c + 2]
            spot = jnp.where(any_of > 0.0, spot, -1.0).astype(jnp.int32)
            dest[(j * 9 + c) * 8 : (j * 9 + c) * 8 + 8, :] = spot
    copy = pltpu.make_async_copy(count_v, count_s, copy_sem)
    copy.start()
    copy.wait()

    for j in range(2):

        def count(c, part_id, k):
            return count_s[0, j * 256 + (c * 3 + part_id) * 8 + k]

        def gather_level(k, offset):
            rise = CELL_SIDE * k.astype(F32) - 20.0
            for c in range(9):
                di, dj = c // 3 - 1, c % 3 - 1
                base = ((1 + di) * 4 + 1 + j + dj) * 64
                value = ext[pl.ds(base + k, 8, stride=8), :]
                shift = jnp.where(
                    sub == 0,
                    CELL_SIDE * di,
                    jnp.where(sub == 1, CELL_SIDE * dj, jnp.where(sub == 2, rise, 0.0)),
                )
                value = jnp.concatenate(split3(value + shift), 1)
                spot = dest[pl.ds((j * 9 + c) * 8 + k, 1), :]

                def pick(first, last):
                    ids = lax.broadcasted_iota(jnp.int32, (last - first, 128), 0) + first
                    hot = jnp.where(ids == spot, 1.0, 0.0).astype(BF16)
                    picked[c, first:last, :] = lax.dot_general(
                        jnp.concatenate([hot, hot, hot], 1),
                        value,
                        LANES,
                        preferred_element_type=F32,
                    )

                if c == 4:
                    pick(0, 128)
                else:
                    pick(0, 64)
                    full = count(c, 0, k) + count(c, 1, k) + count(c, 2, k)
                    pl.when(full > 64)(lambda: pick(64, 128))
            for t in range(3):
                if t == 2:
                    bounds[0, k] = offset
                for c in range(9):
                    amount = count(c, t, k)
                    start = 0 if t == 0 else count(c, 0, k)
                    if t == 2:
                        start = start + count(c, 1, k)
                    short = (64 if t != 1 else 96) if c == 4 else 32

                    def move(first, length):
                        packed[pl.ds(offset + first, length), :] = picked[
                            c, pl.ds(start + first, length), :
                        ]

                    move(0, short)
                    pl.when(amount > short)(lambda: move(short, 128 - short))
                    offset = offset + amount
                if t == 0:
                    bounds[1, k] = offset
            return offset

        end = lax.fori_loop(0, 8, gather_level, jnp.int32(0))
        packed[pl.ds(end, 64), :] = jnp.zeros((64, 8), F32)
        bounds[1, 8] = end

        def cell(k, _):
            rise = CELL_SIDE * k.astype(F32) - 20.0
            base = (5 + j) * 64
            own = [ext[pl.ds(base + 8 * t + k, 1), :] for t in range(7)]
            own[2] = own[2] + rise
            own.append(4.0 * own[6])
            own = [jnp.broadcast_to(v, (8, 128)) for v in own]
            first = jnp.where(k == 0, 0, bounds[0, jnp.maximum(k - 1, 0)])
            first = (first // 8) * 8
            last = bounds[1, k + 1]

            def chunk(i, acc):
                for g in range(CHUNK // 8):
                    at = pl.multiple_of(first + i * CHUNK + g * 8, 8)
                    rows = packed[pl.ds(at, 8), :]
                    acc = pair_sums(own, [rows[:, t : t + 1] for t in range(7)], acc)
                return acc

            zero = jnp.zeros((8, 128), F32)
            sums = lax.fori_loop(
                0, (last - first + CHUNK - 1) // CHUNK, chunk, (zero, zero, zero)
            )
            for t in range(3):
                force[pl.ds((j * 8 + t) * 8 + k, 1), :] = jnp.sum(sums[t], 0, keepdims=True)
            return 0

        lax.fori_loop(0, 8, cell, 0)

    angle = jnp.full((8, 128), phase[0].astype(F32) * (2.0 * math.pi / PHASES), F32)
    cos_b, sin_b = jnp.cos(angle), jnp.sin(angle)
    height_cells = 8
    centre_y, centre_z = 0.5 * CELL_SIDE * lat_cells, 0.5 * CELL_SIDE * height_cells
    reach = 0.45 * CELL_SIDE * min(lat_cells, height_cells)
    shaft_id = lax.axis_index("shaft").astype(F32)
    lat_id = (lax.axis_index("lat") * 2).astype(F32)
    up_id = sub.astype(F32)
    terms = []
    for j in range(2):
        base = (5 + j) * 64
        x, y, z = (ext[base + 8 * t : base + 8 * t + 8, :] for t in range(3))
        radius = ext[base + 48 : base + 56, :]
        x = CELL_SIDE * shaft_id + x
        y = CELL_SIDE * (lat_id + j) + y - centre_y
        z = CELL_SIDE * up_id + z - centre_z
        across = y * cos_b + z * sin_b
        radial = z * cos_b - y * sin_b
        depth = jnp.maximum(jnp.minimum(radius - across, radius + BLADE_THICKNESS + across), 0.0)
        window = jnp.maximum(radial * (reach - radial), 0.0) * (4.0 / (reach * reach))
        gate = jnp.maximum(jnp.cos(x * (2.0 * math.pi / (2.0 * CELL_SIDE))), 0.0)
        size = BLADE_STIFFNESS * depth * window * gate
        fx, fy, fz = (force[(j * 8 + t) * 8 : (j * 8 + t) * 8 + 8, :] for t in range(3))
        fy, fz = fy + size * cos_b, fz + size * sin_b
        ox, oy, oz = (off[t, 0, j] for t in range(3))
        six = [fx, fy, fz, oy * fz - oz * fy, oz * fx - ox * fz, ox * fy - oy * fx]
        for t in range(8):
            force[(j * 8 + t) * 8 : (j * 8 + t) * 8 + 8, :] = (
                six[t] if t < 6 else jnp.zeros((8, 128), F32)
            )
        for k in range(8):
            terms.append(rows3(force[pl.ds(j * 64 + k, 8, stride=8), :]))
    n_piece = route.shape[-1]
    sums = jnp.zeros((24, n_piece), F32)
    for pair in range(8):
        row = piece[0, :, pair * 256 : pair * 256 + 256]
        sums = sums + lax.dot_general(
            jnp.concatenate([terms[2 * pair], terms[2 * pair + 1]], 1),
            one_hot(n_piece, row),
            LANES,
            preferred_element_type=F32,
        )
    sums = rows3(sum3(sums))
    n_clump = part.shape[-1]
    for c in range(9):
        key = jnp.where(route[0] == c, clump[0], -1)
        part[c] = sum3(
            lax.dot_general(sums, one_hot(n_clump, key), LANES, preferred_element_type=F32)
        )

    cos_z, cos_y, cos_x = (jnp.cos(angles[t, 0]) for t in range(3))
    sin_z, sin_y, sin_x = (jnp.sin(angles[t, 0]) for t in range(3))
    rotation = [
        [
            cos_z * cos_y,
            cos_z * sin_y * sin_x - sin_z * cos_x,
            cos_z * sin_y * cos_x + sin_z * sin_x,
        ],
        [
            sin_z * cos_y,
            sin_z * sin_y * sin_x + cos_z * cos_x,
            sin_z * sin_y * cos_x - cos_z * sin_x,
        ],
        [-sin_y, cos_y * sin_x, cos_y * cos_x],
    ]
    for t, (a, b) in enumerate(((0, 0), (0, 1), (0, 2), (1, 1), (1, 2), (2, 2))):
        turning[t : t + 1, :] = TIME_STEP * sum(
            rotation[a][i] * inertia[i, 0] * rotation[b][i] for i in range(3)
        )
    turning[6:8, :] = jnp.zeros((2, n_clump), F32)


def finish_kernel(
    n_shaft,
    n_lat,
    part_any,
    part,
    turning,
    centre,
    motion,
    inverse_mass,
    off,
    piece,
    route,
    clump,
    clump_out,
    sphere_out,
    got,
    table,
    hot_piece,
    hot_clump,
    pose,
    send_sem,
    recv_sem,
):
    place = Place(n_shaft, n_lat)
    n_piece, n_clump = route.shape[-1], part.shape[-1]

    def sums_copy(ds, dl, slot):
        c = (ds + 1) * 3 + dl + 1
        return pltpu.make_async_remote_copy(
            src_ref=part_any.at[c],
            dst_ref=got.at[slot],
            send_sem=send_sem.at[0, slot],
            recv_sem=recv_sem.at[0, slot],
            device_id=place.at(ds, dl),
            device_id_type=MESH,
        )

    def table_copy(ds, dl, slot):
        return pltpu.make_async_remote_copy(
            src_ref=table.at[4],
            dst_ref=table.at[slot],
            send_sem=send_sem.at[1, slot],
            recv_sem=recv_sem.at[1, slot],
            device_id=place.at(ds, dl),
            device_id_type=MESH,
        )

    def around(act, dl):
        for ds in (-1, 0, 1):
            if (ds, dl) != (0, 0):
                act(ds, dl)

    place.barrier()
    place.lateral(
        lambda dl: around(lambda ds, d: sums_copy(ds, d, (ds + 1) * 3 + d + 1).start(), dl)
    )

    def clear(edge, column):
        @pl.when(place.l == edge)
        def _():
            for row in range(3):
                table[row * 3 + column] = jnp.zeros((8, n_clump), F32)
                got[row * 3 + 2 - column] = jnp.zeros((8, n_clump), F32)

    clear(0, 0)
    clear(n_lat - 1, 2)
    for m in range(16):
        hot_piece[:, m * 128 : m * 128 + 128] = one_hot(
            n_piece, piece[0, :, m * 128 : m * 128 + 128]
        )
    for c in range(9):
        hot_clump[c * n_clump : (c + 1) * n_clump, :] = one_hot(
            n_clump, jnp.where(route[0] == c, clump[0], -1)
        )
    place.lateral(
        lambda dl: around(lambda ds, d: sums_copy(ds, d, 8 - (ds + 1) * 3 - d - 1).wait_recv(), dl)
    )
    sums = part[4]
    for c in range(9):
        if c != 4:
            sums = sums + got[c]
    rows = []
    for t in range(3):
        pull = -GRAVITY if t == 2 else 0.0
        rows.append(motion[t, 0] + TIME_STEP * (inverse_mass[0] * sums[t : t + 1] + pull))
    torque = [sums[3 + t : 4 + t] for t in range(3)]
    order = ((0, 1, 2), (1, 3, 4), (2, 4, 5))
    for t in range(3):
        change = sum(turning[order[t][i] : order[t][i] + 1, :] * torque[i] for i in range(3))
        rows.append(motion[3 + t, 0] + change)
    table[4] = jnp.concatenate(rows + [jnp.zeros((2, n_clump), F32)], 0)
    for t in range(3):
        clump_out[t, 0] = centre[t, 0] + TIME_STEP * rows[t]
    for t in range(6):
        clump_out[3 + t, 0] = rows[t]
    place.lateral(
        lambda dl: around(lambda ds, d: table_copy(ds, d, 8 - (ds + 1) * 3 - d - 1).start(), dl)
    )
    place.lateral(
        lambda dl: around(lambda ds, d: table_copy(ds, d, (ds + 1) * 3 + d + 1).wait_recv(), dl)
    )
    tables = jnp.concatenate([rows3(table[c]) for c in range(9)], 1)
    by_piece = lax.dot_general(tables, hot_clump[...], ROWS, preferred_element_type=F32)
    by_piece = by_piece.astype(BF16)
    by_sphere = sum3(
        lax.dot_general(by_piece, hot_piece[...], ROWS, preferred_element_type=F32)
    )
    for m in range(16):
        pose[m * 8 : m * 8 + 8, :] = by_sphere[:, m * 128 : m * 128 + 128]
    for j in range(2):
        vx, vy, vz, sx, sy, sz = (
            pose[pl.ds(j * 64 + t, 8, stride=8), :] for t in range(6)
        )
        bx, by, bz = (off[t, 0, j] for t in range(3))
        hx, hy, hz = (0.5 * TIME_STEP * s for s in (sx, sy, sz))
        scale = 2.0 / (1.0 + (hx * hx + hy * hy + hz * hz))
        cx, cy, cz = hy * bz - hz * by, hz * bx - hx * bz, hx * by - hy * bx
        tx = bx + scale * (cx + hy * cz - hz * cy)
        ty = by + scale * (cy + hz * cx - hx * cz)
        tz = bz + scale * (cz + hx * cy - hy * cx)
        sphere_out[0, 0, j], sphere_out[1, 0, j], sphere_out[2, 0, j] = tx, ty, tz
        sphere_out[3, 0, j] = vx + (sy * tz - sz * ty)
        sphere_out[4, 0, j] = vy + (sz * tx - sx * tz)
        sphere_out[5, 0, j] = vz + (sx * ty - sy * tx)
    place.lateral(
        lambda dl: around(lambda ds, d: sums_copy(ds, d, (ds + 1) * 3 + d + 1).wait_send(), dl)
    )
    place.lateral(
        lambda dl: around(lambda ds, d: table_copy(ds, d, 8 - (ds + 1) * 3 - d - 1).wait_send(), dl)
    )


def contact_call(lat_cells, blade_phase, ext, off, piece, route, clump, angles, inertia, **extra):
    n_clump = angles.shape[-1]
    return pl.pallas_call(
        functools.partial(contact_kernel, lat_cells),
        out_shape=(
            jax.ShapeDtypeStruct((9, 8, n_clump), F32),
            jax.ShapeDtypeStruct((8, n_clump), F32),
        ),
        in_specs=[SMEM] + [VMEM] * 7,
        out_specs=(VMEM, VMEM),
        scratch_shapes=[
            pltpu.VMEM((144, 128), jnp.int32),
            pltpu.VMEM((8, 512), jnp.int32),
            pltpu.SMEM((8, 512), jnp.int32),
            pltpu.SMEM((2, 16), jnp.int32),
            pltpu.VMEM((9, 256, 8), F32),
            pltpu.VMEM((9 * 1024 + 256, 8), F32),
            pltpu.VMEM((128, 128), F32),
            pltpu.SemaphoreType.DMA,
        ],
        compiler_params=pltpu.CompilerParams(vmem_limit_bytes=48 << 20),
        name="contact",
        **extra,
    )(blade_phase, ext, off, piece, route, clump, angles, inertia)


def on_device(
    n_shaft,
    n_lat,
    sphere_position,
    sphere_velocity,
    sphere_radius,
    sphere_offset,
    sphere_piece,
    piece_route,
    piece_clump,
    blade_phase,
    clump_centre,
    clump_motion,
    clump_angles,
    clump_inverse_mass,
    clump_inverse_inertia,
):
    n_piece, n_clump = piece_route.shape[-1], clump_angles.shape[-1]
    ext = pl.pallas_call(
        functools.partial(halo_kernel, n_shaft, n_lat),
        out_shape=jax.ShapeDtypeStruct((3, 4, 8, 8, 128), F32),
        in_specs=[ANY] * 3,
        out_specs=VMEM,
        scratch_shapes=[
            pltpu.SemaphoreType.DMA((3, 4, 3)),
            pltpu.SemaphoreType.DMA((3, 4, 3)),
            pltpu.SemaphoreType.DMA((2, 3)),
        ],
        compiler_params=pltpu.CompilerParams(collective_id=0, has_side_effects=True),
        name="halo",
    )(sphere_position, sphere_velocity, sphere_radius)
    part, turning = contact_call(
        2 * n_lat,
        blade_phase,
        ext.reshape(768, 128),
        sphere_offset,
        sphere_piece,
        piece_route,
        piece_clump,
        clump_angles,
        clump_inverse_inertia,
    )
    return pl.pallas_call(
        functools.partial(finish_kernel, n_shaft, n_lat),
        out_shape=(
            jax.ShapeDtypeStruct((9, 1, 1, n_clump), F32),
            jax.ShapeDtypeStruct((6, 1, 2, 8, 128), F32),
        ),
        in_specs=[ANY] + [VMEM] * 9,
        out_specs=(VMEM, VMEM),
        scratch_shapes=[
            pltpu.VMEM((9, 8, n_clump), F32),
            pltpu.VMEM((9, 8, n_clump), F32),
            pltpu.VMEM((n_piece, 2048), BF16),
            pltpu.VMEM((9 * n_clump, n_piece), BF16),
            pltpu.VMEM((128, 128), F32),
            pltpu.SemaphoreType.DMA((2, 9)),
            pltpu.SemaphoreType.DMA((2, 9)),
        ],
        compiler_params=pltpu.CompilerParams(
            collective_id=1, has_side_effects=True, vmem_limit_bytes=48 << 20
        ),
        name="finish",
    )(
        part,
        part,
        turning,
        clump_centre,
        clump_motion,
        clump_inverse_mass,
        sphere_offset,
        sphere_piece,
        piece_route,
        piece_clump,
    )


def solution(mesh):
    placed = (
        P(None, "shaft", "lat", None, None),
        P(None, "shaft", "lat", None, None),
        P("shaft", "lat", None, None),
        P(None, "shaft", "lat", None, None),
        P("shaft", "lat", None),
        P("shaft", "lat", None),
        P("shaft", "lat", None),
        P(),
        P(None, "shaft", "lat", None),
        P(None, "shaft", "lat", None),
        P(None, "shaft", "lat", None),
        P("shaft", "lat", None),
        P(None, "shaft", "lat", None),
    )
    return jax.shard_map(
        functools.partial(on_device, mesh.shape["shaft"], mesh.shape["lat"]),
        mesh=mesh,
        in_specs=placed,
        out_specs=(P(None, "shaft", "lat", None), P(None, "shaft", "lat", None, None)),
        check_vma=False,
    )
```

```python
import functools
import math

import jax
import jax.numpy as jnp
from jax import lax
from jax.experimental import pallas as pl
from jax.experimental.pallas import tpu as pltpu
from jax.sharding import PartitionSpec as P

PHASES = 64
CELL_SIDE = 5.0
BLADE_STIFFNESS = 20.0
BLADE_THICKNESS = 1.0
TIME_STEP = 0.5
GRAVITY = 0.5

REACH = 1.2001
CHUNK = 32
F32 = jnp.float32
BF16 = jnp.bfloat16
MESH = pl.DeviceIdType.MESH
LANES = (((1,), (1,)), ((), ()))
ROWS = (((1,), (0,)), ((), ()))
VMEM = pl.BlockSpec(memory_space=pltpu.VMEM)
SMEM = pl.BlockSpec(memory_space=pltpu.SMEM)
ANY = pl.BlockSpec(memory_space=pl.ANY)


def split3(x):
    high = x.astype(BF16)
    rest = x - high.astype(F32)
    middle = rest.astype(BF16)
    low = (rest - middle.astype(F32)).astype(BF16)
    return high, middle, low


def rows3(x):
    high = x.astype(BF16).astype(F32)
    rest = x - high
    middle = rest.astype(BF16).astype(F32)
    return jnp.concatenate([high, middle, rest - middle], 0).astype(BF16)


def sum3(x):
    return x[0:8] + x[8:16] + x[16:24]


def one_hot(rows, row):
    length = row.shape[-1]
    ids = lax.broadcasted_iota(jnp.int32, (rows, length), 0)
    return jnp.where(ids == row, 1.0, 0.0).astype(BF16)


class Place:
    def __init__(self, n_shaft, n_lat):
        self.n_shaft, self.n_lat = n_shaft, n_lat
        self.s, self.l = lax.axis_index("shaft"), lax.axis_index("lat")

    def at(self, ds, dl):
        return {"shaft": lax.rem(self.s + ds + self.n_shaft, self.n_shaft), "lat": self.l + dl}

    def lateral(self, act):
        act(0)
        pl.when(self.l > 0)(lambda: act(-1))
        pl.when(self.l < self.n_lat - 1)(lambda: act(1))

    def barrier(self):
        sem = pltpu.get_barrier_semaphore()

        def signal(dl):
            for ds in (-1, 0, 1):
                if (ds, dl) != (0, 0):
                    pl.semaphore_signal(
                        sem, inc=1, device_id=self.at(ds, dl), device_id_type=MESH
                    )

        self.lateral(signal)
        edge = jnp.logical_or(self.l == 0, self.l == self.n_lat - 1)
        pl.semaphore_wait(sem, jnp.where(edge, 5, 8))


def halo_kernel(
    n_shaft,
    n_lat,
    pos,
    vel,
    rad,
    piece,
    route,
    clump,
    ext,
    hot_piece,
    hot_clump,
    send_sem,
    recv_sem,
    own_sem,
):
    place = Place(n_shaft, n_lat)

    def parts(j, si, lj):
        return (
            (pos.at[:, 0, j], ext.at[si, lj, 0:3]),
            (vel.at[:, 0, j], ext.at[si, lj, 3:6]),
            (rad.at[0, pl.ds(j, 1)], ext.at[si, lj, 6:7]),
        )

    def remote(j, ds, dl, si, lj):
        return [
            pltpu.make_async_remote_copy(
                src_ref=src,
                dst_ref=dst,
                send_sem=send_sem.at[si, lj, t],
                recv_sem=recv_sem.at[si, lj, t],
                device_id=place.at(ds, dl),
                device_id_type=MESH,
            )
            for t, (src, dst) in enumerate(parts(j, si, lj))
        ]

    def outgoing(dl):
        found = []
        for ds in (-1, 0, 1):
            for j in (0, 1):
                lj = j - 2 * dl + 1
                if 0 <= lj <= 3 and (ds, dl) != (0, 0):
                    found += remote(j, ds, dl, 1 - ds, lj)
        return found

    def incoming(dl):
        found = []
        for ds in (-1, 0, 1):
            for lj in {0: (1, 2), -1: (0,), 1: (3,)}[dl]:
                if (ds, dl) != (0, 0):
                    found += remote(0, ds, dl, 1 + ds, lj)
        return found

    own = [
        pltpu.make_async_copy(src, dst, own_sem.at[j, t])
        for j in (0, 1)
        for t, (src, dst) in enumerate(parts(j, 1, 1 + j))
    ]
    place.barrier()
    place.lateral(lambda dl: [c.start() for c in outgoing(dl)] and None)
    for c in own:
        c.start()
    ext[:, :, 7] = jnp.zeros((3, 4, 8, 128), F32)

    @pl.when(place.l == 0)
    def _():
        ext[:, 0, 0:7] = jnp.zeros((3, 7, 8, 128), F32)

    @pl.when(place.l == n_lat - 1)
    def _():
        ext[:, 3, 0:7] = jnp.zeros((3, 7, 8, 128), F32)

    for m in range(16):
        hot_piece[:, m * 128 : m * 128 + 128] = one_hot(
            hot_piece.shape[0], piece[0, :, m * 128 : m * 128 + 128]
        )
    n_clump = hot_clump.shape[0] // 9
    for c in range(9):
        hot_clump[c * n_clump : (c + 1) * n_clump, :] = one_hot(
            n_clump, jnp.where(route[0] == c, clump[0], -1)
        )
    for c in own:
        c.wait()
    place.lateral(lambda dl: [c.wait_recv() for c in incoming(dl)] and None)
    place.lateral(lambda dl: [c.wait_send() for c in outgoing(dl)] and None)


USUAL = {0: (128, 64, 96, 64), 1: (64, 24, 40, 24), 2: (32, 16, 24, 16)}
KEYS = 32
TERMS = 9


def kind(c):
    return (c // 3 != 1) + (c % 3 != 1)


def keyed(value, sub):
    radius = value[6:7]
    value = jnp.where(sub == 7, radius * radius * 0.0625, value)
    high = value.astype(BF16).astype(F32)
    rest = value - high
    middle = rest.astype(BF16).astype(F32)
    more = jnp.where(
        sub < 3,
        1.0,
        jnp.where(sub < 5, high[6:7], jnp.where(sub == 5, middle[6:7], 0.0)),
    )
    return jnp.concatenate([high, middle, rest - middle, more], 0).astype(BF16)


def own_table(own, sub, table):
    zero = jnp.zeros((8, 128), F32)

    def split(row):
        return [p.astype(F32) for p in split3(jnp.broadcast_to(row, (8, 128)))]

    def constants(row):
        high, middle, low = split(row)
        return jnp.where(sub == 0, high, jnp.where(sub == 1, middle, jnp.where(sub == 2, low, 0.0)))

    def put(t, same, more):
        block = jnp.concatenate([same, same, same, more], 0)
        table[:, t * 128 : t * 128 + 128] = block.astype(BF16)

    for t in range(7):
        put(t, jnp.where(sub == t, 1.0 if t == 6 else -1.0, zero), constants(own[t]))
    high, middle, low = split(4.0 * own[6])
    same = jnp.where(sub == 6, high, 0.0)
    more = jnp.where(sub == 4, low, jnp.where((sub == 3) | (sub == 5), middle, 0.0))
    put(7, same, more)
    put(
        8,
        jnp.where(sub == 7, 1.0, same * 0.03125),
        more * 0.03125 + constants(own[6] * own[6] * 0.0625),
    )


def pair_sums(pair, acc):
    dx, dy, dz, du, dv, dw, radii, product, least = pair
    square = dx * dx + dy * dy + dz * dz
    clamped = jnp.maximum(square, least)
    inverse = lax.rsqrt(clamped)
    delta = jnp.maximum(radii - clamped * inverse, 0.0)
    normal_speed = (du * dx + dv * dy + dw * dz) * inverse
    speed = du * du + dv * dv + dw * dw
    unit = square * (inverse * inverse)
    sliding = speed + normal_speed * normal_speed * (unit - 2.0)
    load = product * delta
    root = load * lax.rsqrt(jnp.maximum(load * radii, 1e-30))
    root2 = root * root
    cap = 2.5 * delta
    shear = root2 * cap * lax.rsqrt(jnp.maximum(root2 * (sliding + cap * cap), 0.0) + 1e-06)
    push = root * (cap + cap - normal_speed - 0.25)
    along = (push + shear * normal_speed) * inverse
    return (
        acc[0] + (along * dx - shear * du),
        acc[1] + (along * dy - shear * dv),
        acc[2] + (along * dz - shear * dw),
    )


def contact_kernel(
    lat_cells,
    phase,
    ext,
    off,
    hot_piece,
    hot_clump,
    angles,
    inertia,
    part,
    turning,
    dest,
    count_v,
    count_s,
    bounds,
    picked,
    packed,
    table,
    pairs_a,
    pairs_b,
    force,
    copy_sem,
):
    sub = lax.broadcasted_iota(jnp.int32, (8, 128), 0)

    before = jnp.where(
        lax.broadcasted_iota(jnp.int32, (128, 128), 0)
        < lax.broadcasted_iota(jnp.int32, (128, 128), 1),
        1.0,
        0.0,
    ).astype(BF16)
    ones = jnp.ones((128, 128), BF16)
    for j in range(2):
        masks = []
        for c in range(9):
            di, dj = c // 3 - 1, c % 3 - 1
            base = ((1 + di) * 4 + 1 + j + dj) * 64
            x, y, z = (ext[base + 8 * t : base + 8 * t + 8, :] for t in range(3))
            keep = ext[base + 48 : base + 56, :] > 0.0
            if di:
                keep &= (x < REACH) if di > 0 else (x > CELL_SIDE - REACH)
            if dj:
                keep &= (y < REACH) if dj > 0 else (y > CELL_SIDE - REACH)
            low, high = z < REACH, z > CELL_SIDE - REACH
            kept = jnp.where(keep, 1.0, 0.0)
            low_f = jnp.where(low, kept, 0.0)
            high_f = jnp.where(high, kept, 0.0)
            masks += [low_f, kept - low_f - high_f, high_f]
        mask = jnp.concatenate(masks, 0).astype(BF16)
        prefix = lax.dot_general(mask, before, ROWS, preferred_element_type=F32)
        total = lax.dot_general(mask, ones, ROWS, preferred_element_type=F32)
        counts = lax.dot_general(ones[0:8], mask, LANES, preferred_element_type=F32)
        count_v[0:8, j * 256 : j * 256 + 216] = counts.astype(jnp.int32)
        over = jnp.full((8, 128), -1.0, F32)
        for c in range(9):
            a = c * 24
            low_p, mid_p, high_p = (prefix[a + 8 * t : a + 8 * t + 8] for t in range(3))
            low_n, mid_n, high_n = (total[a + 8 * t : a + 8 * t + 8] for t in range(3))
            spot = (
                masks[3 * c] * low_p
                + masks[3 * c + 1] * (low_n + mid_p)
                + masks[3 * c + 2] * (low_n + mid_n + high_p)
            )
            any_of = masks[3 * c] + masks[3 * c + 1] + masks[3 * c + 2]
            spot = jnp.where(any_of > 0.0, spot, -1.0).astype(jnp.int32)
            dest[(j * 9 + c) * 8 : (j * 9 + c) * 8 + 8, :] = spot
            sizes = (low_n + mid_n + high_n, low_n, mid_n, high_n)
            for size, usual in zip(sizes, USUAL[kind(c)]):
                over = jnp.maximum(over, size - usual)
        count_v[8:16, j * 128 : j * 128 + 128] = over.astype(jnp.int32)
    copy = pltpu.make_async_copy(count_v, count_s, copy_sem)
    copy.start()
    copy.wait()

    for j in range(2):

        def count(c, t, k):
            return count_s[0, j * 256 + (c * 3 + t) * 8 + k]

        def gather_level(k, offset, sizes):
            rise = CELL_SIDE * k.astype(F32) - 20.0
            for c in range(9):
                di, dj = c // 3 - 1, c % 3 - 1
                base = ((1 + di) * 4 + 1 + j + dj) * 64
                value = ext[pl.ds(base + k, 8, stride=8), :]
                shift = jnp.where(
                    sub == 0,
                    CELL_SIDE * di,
                    jnp.where(sub == 1, CELL_SIDE * dj, jnp.where(sub == 2, rise, 0.0)),
                )
                spot = dest[pl.ds((j * 9 + c) * 8 + k, 1), :]
                rows = sizes[kind(c)][0]
                picked[c, 0:rows, :] = lax.dot_general(
                    one_hot(rows, spot),
                    keyed(value + shift, sub),
                    LANES,
                    preferred_element_type=F32,
                )
            for t in range(3):
                if t == 2:
                    bounds[0, k] = offset
                for c in range(9):
                    start = 0 if t == 0 else count(c, 0, k)
                    if t == 2:
                        start = start + count(c, 1, k)
                    length = sizes[kind(c)][1 + t]
                    packed[pl.ds(offset, length), :] = picked[c, pl.ds(start, length), :]
                    offset = offset + count(c, t, k)
                if t == 0:
                    bounds[1, k] = offset
            return offset

        def level(k, offset):
            return lax.cond(
                count_s[8 + k, j * 128] > 0,
                lambda: gather_level(k, offset, {t: (128,) * 4 for t in range(3)}),
                lambda: gather_level(k, offset, USUAL),
            )

        end = lax.fori_loop(0, 8, level, jnp.int32(0))
        lane = lax.broadcasted_iota(jnp.int32, (64, KEYS), 1)
        packed[pl.ds(end, 64), :] = jnp.where((lane >= 24) & (lane < 27), 1.0, 0.0)
        bounds[1, 8] = end

        def cell(k, _):
            rise = CELL_SIDE * k.astype(F32) - 20.0
            base = (5 + j) * 64
            own = [ext[pl.ds(base + 8 * t + k, 1), :] for t in range(7)]
            own[2] = own[2] + rise
            own_table(own, sub, table)
            first = jnp.where(k == 0, 0, bounds[0, jnp.maximum(k - 1, 0)])
            first = (first // 8) * 8
            last = bounds[1, k + 1]

            def fill(i, pairs):
                at = pl.multiple_of(first + i * CHUNK, 8)
                pairs[...] = lax.dot_general(
                    packed[pl.ds(at, CHUNK), :].astype(BF16),
                    table[...],
                    ROWS,
                    preferred_element_type=F32,
                )

            def use(pairs, acc):
                for g in range(CHUNK // 8):
                    pair = [
                        pairs[g * 8 : g * 8 + 8, t * 128 : t * 128 + 128] for t in range(TERMS)
                    ]
                    acc = pair_sums(pair, acc)
                return acc

            def chunks(i, acc):
                fill(2 * i + 1, pairs_b)
                acc = use(pairs_a, acc)
                fill(2 * i + 2, pairs_a)
                return use(pairs_b, acc)

            fill(0, pairs_a)
            zero = jnp.zeros((8, 128), F32)
            sums = lax.fori_loop(
                0, (last - first + 2 * CHUNK - 1) // (2 * CHUNK), chunks, (zero, zero, zero)
            )
            for t in range(3):
                force[pl.ds((j * 8 + t) * 8 + k, 1), :] = jnp.sum(sums[t], 0, keepdims=True)
            return 0

        lax.fori_loop(0, 8, cell, 0)

    angle = jnp.full((8, 128), phase[0].astype(F32) * (2.0 * math.pi / PHASES), F32)
    cos_b, sin_b = jnp.cos(angle), jnp.sin(angle)
    height_cells = 8
    centre_y, centre_z = 0.5 * CELL_SIDE * lat_cells, 0.5 * CELL_SIDE * height_cells
    reach = 0.45 * CELL_SIDE * min(lat_cells, height_cells)
    shaft_id = lax.axis_index("shaft").astype(F32)
    lat_id = (lax.axis_index("lat") * 2).astype(F32)
    up_id = sub.astype(F32)
    terms = []
    for j in range(2):
        base = (5 + j) * 64
        x, y, z = (ext[base + 8 * t : base + 8 * t + 8, :] for t in range(3))
        radius = ext[base + 48 : base + 56, :]
        x = CELL_SIDE * shaft_id + x
        y = CELL_SIDE * (lat_id + j) + y - centre_y
        z = CELL_SIDE * up_id + z - centre_z
        across = y * cos_b + z * sin_b
        radial = z * cos_b - y * sin_b
        depth = jnp.maximum(jnp.minimum(radius - across, radius + BLADE_THICKNESS + across), 0.0)
        window = jnp.maximum(radial * (reach - radial), 0.0) * (4.0 / (reach * reach))
        gate = jnp.maximum(jnp.cos(x * (2.0 * math.pi / (2.0 * CELL_SIDE))), 0.0)
        size = BLADE_STIFFNESS * depth * window * gate
        fx, fy, fz = (force[(j * 8 + t) * 8 : (j * 8 + t) * 8 + 8, :] for t in range(3))
        fy, fz = fy + size * cos_b, fz + size * sin_b
        ox, oy, oz = (off[t, 0, j] for t in range(3))
        six = [fx, fy, fz, oy * fz - oz * fy, oz * fx - ox * fz, ox * fy - oy * fx]
        for t in range(8):
            force[(j * 8 + t) * 8 : (j * 8 + t) * 8 + 8, :] = (
                six[t] if t < 6 else jnp.zeros((8, 128), F32)
            )
        for k in range(8):
            terms.append(rows3(force[pl.ds(j * 64 + k, 8, stride=8), :]))
    sums = lax.dot_general(
        jnp.concatenate(terms, 1), hot_piece[...], LANES, preferred_element_type=F32
    )
    sums = sum3(
        lax.dot_general(rows3(sum3(sums)), hot_clump[...], LANES, preferred_element_type=F32)
    )
    n_clump = part.shape[-1]
    for c in range(9):
        part[c] = sums[:, c * n_clump : (c + 1) * n_clump]

    cos_z, cos_y, cos_x = (jnp.cos(angles[t, 0]) for t in range(3))
    sin_z, sin_y, sin_x = (jnp.sin(angles[t, 0]) for t in range(3))
    rotation = [
        [
            cos_z * cos_y,
            cos_z * sin_y * sin_x - sin_z * cos_x,
            cos_z * sin_y * cos_x + sin_z * sin_x,
        ],
        [
            sin_z * cos_y,
            sin_z * sin_y * sin_x + cos_z * cos_x,
            sin_z * sin_y * cos_x - cos_z * sin_x,
        ],
        [-sin_y, cos_y * sin_x, cos_y * cos_x],
    ]
    for t, (a, b) in enumerate(((0, 0), (0, 1), (0, 2), (1, 1), (1, 2), (2, 2))):
        turning[t : t + 1, :] = TIME_STEP * sum(
            rotation[a][i] * inertia[i, 0] * rotation[b][i] for i in range(3)
        )
    turning[6:8, :] = jnp.zeros((2, n_clump), F32)


def finish_kernel(
    n_shaft,
    n_lat,
    part_any,
    part,
    turning,
    centre,
    motion,
    inverse_mass,
    off,
    hot_piece,
    hot_clump,
    clump_out,
    sphere_out,
    got,
    table,
    pose,
    send_sem,
    recv_sem,
):
    place = Place(n_shaft, n_lat)
    n_clump = part.shape[-1]

    def sums_copy(ds, dl, slot):
        c = (ds + 1) * 3 + dl + 1
        return pltpu.make_async_remote_copy(
            src_ref=part_any.at[c],
            dst_ref=got.at[slot],
            send_sem=send_sem.at[0, slot],
            recv_sem=recv_sem.at[0, slot],
            device_id=place.at(ds, dl),
            device_id_type=MESH,
        )

    def table_copy(ds, dl, slot):
        return pltpu.make_async_remote_copy(
            src_ref=table.at[4],
            dst_ref=table.at[slot],
            send_sem=send_sem.at[1, slot],
            recv_sem=recv_sem.at[1, slot],
            device_id=place.at(ds, dl),
            device_id_type=MESH,
        )

    def around(act, dl):
        for ds in (-1, 0, 1):
            if (ds, dl) != (0, 0):
                act(ds, dl)

    place.barrier()
    place.lateral(
        lambda dl: around(lambda ds, d: sums_copy(ds, d, (ds + 1) * 3 + d + 1).start(), dl)
    )

    def clear(edge, column):
        @pl.when(place.l == edge)
        def _():
            for row in range(3):
                table[row * 3 + column] = jnp.zeros((8, n_clump), F32)
                got[row * 3 + 2 - column] = jnp.zeros((8, n_clump), F32)

    clear(0, 0)
    clear(n_lat - 1, 2)
    place.lateral(
        lambda dl: around(lambda ds, d: sums_copy(ds, d, 8 - (ds + 1) * 3 - d - 1).wait_recv(), dl)
    )
    sums = part[4]
    for c in range(9):
        if c != 4:
            sums = sums + got[c]
    rows = []
    for t in range(3):
        pull = -GRAVITY if t == 2 else 0.0
        rows.append(motion[t, 0] + TIME_STEP * (inverse_mass[0] * sums[t : t + 1] + pull))
    torque = [sums[3 + t : 4 + t] for t in range(3)]
    order = ((0, 1, 2), (1, 3, 4), (2, 4, 5))
    for t in range(3):
        change = sum(turning[order[t][i] : order[t][i] + 1, :] * torque[i] for i in range(3))
        rows.append(motion[3 + t, 0] + change)
    table[4] = jnp.concatenate(rows + [jnp.zeros((2, n_clump), F32)], 0)
    for t in range(3):
        clump_out[t, 0] = centre[t, 0] + TIME_STEP * rows[t]
    for t in range(6):
        clump_out[3 + t, 0] = rows[t]
    place.lateral(
        lambda dl: around(lambda ds, d: table_copy(ds, d, 8 - (ds + 1) * 3 - d - 1).start(), dl)
    )
    place.lateral(
        lambda dl: around(lambda ds, d: table_copy(ds, d, (ds + 1) * 3 + d + 1).wait_recv(), dl)
    )
    tables = jnp.concatenate([rows3(table[c]) for c in range(9)], 1)
    by_piece = lax.dot_general(tables, hot_clump[...], ROWS, preferred_element_type=F32)
    by_piece = by_piece.astype(BF16)
    by_sphere = sum3(
        lax.dot_general(by_piece, hot_piece[...], ROWS, preferred_element_type=F32)
    )
    for m in range(16):
        pose[m * 8 : m * 8 + 8, :] = by_sphere[:, m * 128 : m * 128 + 128]
    for j in range(2):
        vx, vy, vz, sx, sy, sz = (
            pose[pl.ds(j * 64 + t, 8, stride=8), :] for t in range(6)
        )
        bx, by, bz = (off[t, 0, j] for t in range(3))
        hx, hy, hz = (0.5 * TIME_STEP * s for s in (sx, sy, sz))
        scale = 2.0 / (1.0 + (hx * hx + hy * hy + hz * hz))
        cx, cy, cz = hy * bz - hz * by, hz * bx - hx * bz, hx * by - hy * bx
        tx = bx + scale * (cx + hy * cz - hz * cy)
        ty = by + scale * (cy + hz * cx - hx * cz)
        tz = bz + scale * (cz + hx * cy - hy * cx)
        sphere_out[0, 0, j], sphere_out[1, 0, j], sphere_out[2, 0, j] = tx, ty, tz
        sphere_out[3, 0, j] = vx + (sy * tz - sz * ty)
        sphere_out[4, 0, j] = vy + (sz * tx - sx * tz)
        sphere_out[5, 0, j] = vz + (sx * ty - sy * tx)
    place.lateral(
        lambda dl: around(lambda ds, d: sums_copy(ds, d, (ds + 1) * 3 + d + 1).wait_send(), dl)
    )
    place.lateral(
        lambda dl: around(lambda ds, d: table_copy(ds, d, 8 - (ds + 1) * 3 - d - 1).wait_send(), dl)
    )


def contact_call(lat_cells, blade_phase, ext, off, hot_piece, hot_clump, angles, inertia, **extra):
    n_clump = angles.shape[-1]
    return pl.pallas_call(
        functools.partial(contact_kernel, lat_cells),
        out_shape=(
            jax.ShapeDtypeStruct((9, 8, n_clump), F32),
            jax.ShapeDtypeStruct((8, n_clump), F32),
        ),
        in_specs=[SMEM] + [VMEM] * 6,
        out_specs=(VMEM, VMEM),
        scratch_shapes=[
            pltpu.VMEM((144, 128), jnp.int32),
            pltpu.VMEM((16, 512), jnp.int32),
            pltpu.SMEM((16, 512), jnp.int32),
            pltpu.SMEM((2, 16), jnp.int32),
            pltpu.VMEM((9, 256, KEYS), F32),
            pltpu.VMEM((9 * 1024 + 256, KEYS), F32),
            pltpu.VMEM((KEYS, TERMS * 128), BF16),
            pltpu.VMEM((CHUNK, TERMS * 128), F32),
            pltpu.VMEM((CHUNK, TERMS * 128), F32),
            pltpu.VMEM((128, 128), F32),
            pltpu.SemaphoreType.DMA,
        ],
        compiler_params=pltpu.CompilerParams(vmem_limit_bytes=20 << 20),
        name="contact",
        **extra,
    )(blade_phase, ext, off, hot_piece, hot_clump, angles, inertia)


def on_device(
    n_shaft,
    n_lat,
    sphere_position,
    sphere_velocity,
    sphere_radius,
    sphere_offset,
    sphere_piece,
    piece_route,
    piece_clump,
    blade_phase,
    clump_centre,
    clump_motion,
    clump_angles,
    clump_inverse_mass,
    clump_inverse_inertia,
):
    n_piece, n_clump = piece_route.shape[-1], clump_angles.shape[-1]
    ext, hot_piece, hot_clump = pl.pallas_call(
        functools.partial(halo_kernel, n_shaft, n_lat),
        out_shape=(
            jax.ShapeDtypeStruct((3, 4, 8, 8, 128), F32),
            jax.ShapeDtypeStruct((n_piece, 2048), BF16),
            jax.ShapeDtypeStruct((9 * n_clump, n_piece), BF16),
        ),
        in_specs=[ANY] * 3 + [VMEM] * 3,
        out_specs=(VMEM,) * 3,
        scratch_shapes=[
            pltpu.SemaphoreType.DMA((3, 4, 3)),
            pltpu.SemaphoreType.DMA((3, 4, 3)),
            pltpu.SemaphoreType.DMA((2, 3)),
        ],
        compiler_params=pltpu.CompilerParams(
            collective_id=0, has_side_effects=True, vmem_limit_bytes=16 << 20
        ),
        name="halo",
    )(
        sphere_position,
        sphere_velocity,
        sphere_radius,
        sphere_piece,
        piece_route,
        piece_clump,
    )
    part, turning = contact_call(
        2 * n_lat,
        blade_phase,
        ext.reshape(768, 128),
        sphere_offset,
        hot_piece,
        hot_clump,
        clump_angles,
        clump_inverse_inertia,
    )
    return pl.pallas_call(
        functools.partial(finish_kernel, n_shaft, n_lat),
        out_shape=(
            jax.ShapeDtypeStruct((9, 1, 1, n_clump), F32),
            jax.ShapeDtypeStruct((6, 1, 2, 8, 128), F32),
        ),
        in_specs=[ANY] + [VMEM] * 8,
        out_specs=(VMEM, VMEM),
        scratch_shapes=[
            pltpu.VMEM((9, 8, n_clump), F32),
            pltpu.VMEM((9, 8, n_clump), F32),
            pltpu.VMEM((128, 128), F32),
            pltpu.SemaphoreType.DMA((2, 9)),
            pltpu.SemaphoreType.DMA((2, 9)),
        ],
        compiler_params=pltpu.CompilerParams(
            collective_id=1, has_side_effects=True, vmem_limit_bytes=16 << 20
        ),
        name="finish",
    )(
        part,
        part,
        turning,
        clump_centre,
        clump_motion,
        clump_inverse_mass,
        sphere_offset,
        hot_piece,
        hot_clump,
    )


def solution(mesh):
    placed = (
        P(None, "shaft", "lat", None, None),
        P(None, "shaft", "lat", None, None),
        P("shaft", "lat", None, None),
        P(None, "shaft", "lat", None, None),
        P("shaft", "lat", None),
        P("shaft", "lat", None),
        P("shaft", "lat", None),
        P(),
        P(None, "shaft", "lat", None),
        P(None, "shaft", "lat", None),
        P(None, "shaft", "lat", None),
        P("shaft", "lat", None),
        P(None, "shaft", "lat", None),
    )
    return jax.shard_map(
        functools.partial(on_device, mesh.shape["shaft"], mesh.shape["lat"]),
        mesh=mesh,
        in_specs=placed,
        out_specs=(P(None, "shaft", "lat", None), P(None, "shaft", "lat", None, None)),
        check_vma=False,
    )
```

```python
import functools
import math

import jax
import jax.numpy as jnp
from jax import lax
from jax.experimental import pallas as pl
from jax.experimental.pallas import tpu as pltpu
from jax.sharding import PartitionSpec as P

PHASES = 64
CELL_SIDE = 5.0
BLADE_STIFFNESS = 20.0
BLADE_THICKNESS = 1.0
TIME_STEP = 0.5
GRAVITY = 0.5

REACH = 1.2001
CHUNK = 32
F32 = jnp.float32
BF16 = jnp.bfloat16
MESH = pl.DeviceIdType.MESH
LANES = (((1,), (1,)), ((), ()))
ROWS = (((1,), (0,)), ((), ()))
VMEM = pl.BlockSpec(memory_space=pltpu.VMEM)
SMEM = pl.BlockSpec(memory_space=pltpu.SMEM)
HBM = pl.BlockSpec(memory_space=pltpu.HBM)


def split3(x):
    high = x.astype(BF16)
    rest = x - high.astype(F32)
    middle = rest.astype(BF16)
    low = (rest - middle.astype(F32)).astype(BF16)
    return high, middle, low


def rows3(x):
    high = x.astype(BF16).astype(F32)
    rest = x - high
    middle = rest.astype(BF16).astype(F32)
    return jnp.concatenate([high, middle, rest - middle], 0).astype(BF16)


def sum3(x):
    return x[0:8] + x[8:16] + x[16:24]


def one_hot(rows, row):
    length = row.shape[-1]
    ids = lax.broadcasted_iota(jnp.int32, (rows, length), 0)
    return jnp.where(ids == row, 1.0, 0.0).astype(BF16)


class Place:
    def __init__(self, n_shaft, n_lat):
        self.n_shaft, self.n_lat = n_shaft, n_lat
        self.s, self.l = lax.axis_index("shaft"), lax.axis_index("lat")

    def at(self, ds, dl):
        return {"shaft": lax.rem(self.s + ds + self.n_shaft, self.n_shaft), "lat": self.l + dl}

    def lateral(self, act):
        act(0)
        pl.when(self.l > 0)(lambda: act(-1))
        pl.when(self.l < self.n_lat - 1)(lambda: act(1))

    def barrier(self):
        sem = pltpu.get_barrier_semaphore()

        def signal(dl):
            for ds in (-1, 0, 1):
                if (ds, dl) != (0, 0):
                    pl.semaphore_signal(
                        sem, inc=1, device_id=self.at(ds, dl), device_id_type=MESH
                    )

        self.lateral(signal)
        edge = jnp.logical_or(self.l == 0, self.l == self.n_lat - 1)
        pl.semaphore_wait(sem, jnp.where(edge, 5, 8))


def halo_kernel(
    n_shaft,
    n_lat,
    pos,
    vel,
    rad,
    piece_hbm,
    route_hbm,
    clump_hbm,
    ext,
    hot_piece,
    hot_clump,
    inside,
    piece,
    route,
    clump,
    table,
    pairs_a,
    pairs_b,
    send_sem,
    recv_sem,
    own_sem,
    load_sem,
):
    place = Place(n_shaft, n_lat)

    def parts(j, si, lj):
        return (
            (pos.at[:, 0, j], ext.at[si, lj, 0:3]),
            (vel.at[:, 0, j], ext.at[si, lj, 3:6]),
            (rad.at[0, pl.ds(j, 1)], ext.at[si, lj, 6:7]),
        )

    def remote(j, ds, dl, si, lj):
        return [
            pltpu.make_async_remote_copy(
                src_ref=src,
                dst_ref=dst,
                send_sem=send_sem.at[si, lj, t],
                recv_sem=recv_sem.at[si, lj, t],
                device_id=place.at(ds, dl),
                device_id_type=MESH,
            )
            for t, (src, dst) in enumerate(parts(j, si, lj))
        ]

    def outgoing(dl):
        found = []
        for ds in (-1, 0, 1):
            for j in (0, 1):
                lj = j - 2 * dl + 1
                if 0 <= lj <= 3 and (ds, dl) != (0, 0):
                    found += remote(j, ds, dl, 1 - ds, lj)
        return found

    def incoming(dl):
        found = []
        for ds in (-1, 0, 1):
            for lj in {0: (1, 2), -1: (0,), 1: (3,)}[dl]:
                if (ds, dl) != (0, 0):
                    found += remote(0, ds, dl, 1 + ds, lj)
        return found

    own = [
        pltpu.make_async_copy(src, dst, own_sem.at[j, t])
        for j in (0, 1)
        for t, (src, dst) in enumerate(parts(j, 1, 1 + j))
    ]
    own += [
        pltpu.make_async_copy(src, dst, load_sem.at[t])
        for t, (src, dst) in enumerate(
            ((piece_hbm, piece), (route_hbm, route), (clump_hbm, clump))
        )
    ]
    for c in own:
        c.start()
    place.barrier()
    place.lateral(lambda dl: [c.start() for c in outgoing(dl)] and None)
    ext[:, :, 7] = jnp.zeros((3, 4, 8, 128), F32)

    @pl.when(place.l == 0)
    def _():
        ext[:, 0, 0:7] = jnp.zeros((3, 7, 8, 128), F32)

    @pl.when(place.l == n_lat - 1)
    def _():
        ext[:, 3, 0:7] = jnp.zeros((3, 7, 8, 128), F32)

    for c in own:
        c.wait()
    sub = lax.broadcasted_iota(jnp.int32, (8, 128), 0)
    every = one_hot(128, lax.broadcasted_iota(jnp.int32, (1, 128), 1))
    inside[...] = jnp.zeros((128, 128), F32)

    def cell(m, _):
        j, k = m // 8, m % 8
        mine = [ext[1, 1 + j, t, pl.ds(k, 1), :] for t in range(7)]
        own_table(mine, sub, table)
        value = jnp.concatenate(mine + [mine[6]], 0)
        rows = lax.dot_general(every, keyed(value, sub), LANES, preferred_element_type=F32)
        zero = jnp.zeros((8, 128), F32)
        acc = (zero, zero, zero)
        for i in range(128 // CHUNK):
            pairs = (pairs_a, pairs_b)[i % 2]
            fill(rows[i * CHUNK : (i + 1) * CHUNK], table, pairs)
            acc = use(pairs, acc)
        for t in range(3):
            inside[pl.ds((j * 8 + t) * 8 + k, 1), :] = jnp.sum(acc[t], 0, keepdims=True)
        return 0

    lax.fori_loop(0, 16, cell, 0)
    for m in range(16):
        hot_piece[:, m * 128 : m * 128 + 128] = one_hot(
            hot_piece.shape[0], piece[0, :, m * 128 : m * 128 + 128]
        )
    n_clump = hot_clump.shape[0] // 9
    for c in range(9):
        hot_clump[c * n_clump : (c + 1) * n_clump, :] = one_hot(
            n_clump, jnp.where(route[0] == c, clump[0], -1)
        )
    place.lateral(lambda dl: [c.wait_recv() for c in incoming(dl)] and None)
    place.lateral(lambda dl: [c.wait_send() for c in outgoing(dl)] and None)


USUAL = {0: (128, 64, 64, 64), 1: (64, 24, 40, 24), 2: (32, 16, 24, 16)}
KEYS = 32
TERMS = 9


def kind(c):
    return (c // 3 != 1) + (c % 3 != 1)


def keyed(value, sub):
    radius = value[6:7]
    value = jnp.where(sub == 7, radius * radius * 0.0625, value)
    high = value.astype(BF16).astype(F32)
    rest = value - high
    middle = rest.astype(BF16).astype(F32)
    more = jnp.where(
        sub < 3,
        1.0,
        jnp.where(sub < 5, high[6:7], jnp.where(sub == 5, middle[6:7], 0.0)),
    )
    return jnp.concatenate([high, middle, rest - middle, more], 0).astype(BF16)


def own_table(own, sub, table):
    zero = jnp.zeros((8, 128), F32)

    def split(row):
        return [p.astype(F32) for p in split3(jnp.broadcast_to(row, (8, 128)))]

    def constants(row):
        high, middle, low = split(row)
        return jnp.where(sub == 0, high, jnp.where(sub == 1, middle, jnp.where(sub == 2, low, 0.0)))

    def put(t, same, more):
        block = jnp.concatenate([same, same, same, more], 0)
        table[:, t * 128 : t * 128 + 128] = block.astype(BF16)

    for t in range(7):
        put(t, jnp.where(sub == t, 1.0 if t == 6 else -1.0, zero), constants(own[t]))
    high, middle, low = split(4.0 * own[6])
    same = jnp.where(sub == 6, high, 0.0)
    more = jnp.where(sub == 4, low, jnp.where((sub == 3) | (sub == 5), middle, 0.0))
    put(7, same, more)
    put(
        8,
        jnp.where(sub == 7, 1.0, same * 0.03125),
        more * 0.03125 + constants(own[6] * own[6] * 0.0625),
    )


def pair_sums(pair, acc):
    dx, dy, dz, du, dv, dw, radii, product, least = pair
    square = dx * dx + dy * dy + dz * dz
    clamped = jnp.maximum(square, least)
    inverse = lax.rsqrt(clamped)
    delta = jnp.maximum(radii - clamped * inverse, 0.0)
    normal_speed = (du * dx + dv * dy + dw * dz) * inverse
    speed = du * du + dv * dv + dw * dw
    unit = square * (inverse * inverse)
    sliding = speed + normal_speed * normal_speed * (unit - 2.0)
    load = product * delta
    root = load * lax.rsqrt(jnp.maximum(load * radii, 1e-30))
    root2 = root * root
    cap = 2.5 * delta
    shear = root2 * cap * lax.rsqrt(jnp.maximum(root2 * (sliding + cap * cap), 0.0) + 1e-06)
    push = root * (cap + cap - normal_speed - 0.25)
    along = (push + shear * normal_speed) * inverse
    return (
        acc[0] + (along * dx - shear * du),
        acc[1] + (along * dy - shear * dv),
        acc[2] + (along * dz - shear * dw),
    )


def fill(rows, table, pairs):
    pairs[...] = lax.dot_general(
        rows.astype(BF16), table[...], ROWS, preferred_element_type=F32
    )


def use(pairs, acc):
    for g in range(CHUNK // 8):
        acc = pair_sums(
            [pairs[g * 8 : g * 8 + 8, t * 128 : t * 128 + 128] for t in range(TERMS)], acc
        )
    return acc


def contact_kernel(
    lat_cells,
    phase,
    ext,
    hot_piece,
    hot_clump,
    inside,
    off_hbm,
    angles_hbm,
    inertia_hbm,
    part,
    turning,
    off,
    angles,
    inertia,
    dest,
    count_v,
    count_s,
    bounds,
    picked,
    picked_own,
    packed,
    table,
    pairs_a,
    pairs_b,
    force,
    copy_sem,
):
    loads = [
        pltpu.make_async_copy(src, dst, copy_sem.at[1 + t])
        for t, (src, dst) in enumerate(
            ((angles_hbm, angles), (inertia_hbm, inertia), (off_hbm, off))
        )
    ]
    for load in loads:
        load.start()
    sub = lax.broadcasted_iota(jnp.int32, (8, 128), 0)

    before = jnp.where(
        lax.broadcasted_iota(jnp.int32, (128, 128), 0)
        < lax.broadcasted_iota(jnp.int32, (128, 128), 1),
        1.0,
        0.0,
    ).astype(BF16)
    ones = jnp.ones((128, 128), BF16)
    for j in range(2):
        masks = []
        for c in range(9):
            di, dj = c // 3 - 1, c % 3 - 1
            base = ((1 + di) * 4 + 1 + j + dj) * 64
            x, y, z = (ext[base + 8 * t : base + 8 * t + 8, :] for t in range(3))
            keep = ext[base + 48 : base + 56, :] > 0.0
            if di:
                keep &= (x < REACH) if di > 0 else (x > CELL_SIDE - REACH)
            if dj:
                keep &= (y < REACH) if dj > 0 else (y > CELL_SIDE - REACH)
            low, high = z < REACH, z > CELL_SIDE - REACH
            kept = jnp.where(keep, 1.0, 0.0)
            low_f = jnp.where(low, kept, 0.0)
            high_f = jnp.where(high, kept, 0.0)
            mid_f = jnp.zeros((8, 128), F32) if c == 4 else kept - low_f - high_f
            masks += [low_f, mid_f, high_f]
        mask = jnp.concatenate(masks, 0).astype(BF16)
        prefix = lax.dot_general(mask, before, ROWS, preferred_element_type=F32)
        total = lax.dot_general(mask, ones, ROWS, preferred_element_type=F32)
        counts = lax.dot_general(ones[0:8], mask, LANES, preferred_element_type=F32)
        count_v[0:8, j * 256 : j * 256 + 216] = counts.astype(jnp.int32)
        over = jnp.full((8, 128), -1.0, F32)
        for c in range(9):
            a = c * 24
            low_p, mid_p, high_p = (prefix[a + 8 * t : a + 8 * t + 8] for t in range(3))
            low_n, mid_n, high_n = (total[a + 8 * t : a + 8 * t + 8] for t in range(3))
            spot = (
                masks[3 * c] * low_p
                + masks[3 * c + 1] * (low_n + mid_p)
                + masks[3 * c + 2] * (low_n + mid_n + high_p)
            )
            any_of = masks[3 * c] + masks[3 * c + 1] + masks[3 * c + 2]
            spot = jnp.where(any_of > 0.0, spot, -1.0).astype(jnp.int32)
            dest[(j * 9 + c) * 8 : (j * 9 + c) * 8 + 8, :] = spot
            sizes = (low_n + mid_n + high_n, low_n, mid_n, high_n)
            for size, usual in zip(sizes, USUAL[kind(c)]):
                excess = size - usual
                if c == 4:
                    excess = jnp.max(excess, 0, keepdims=True)
                over = jnp.maximum(over, excess)
        count_v[8:16, j * 128 : j * 128 + 128] = over.astype(jnp.int32)
    copy = pltpu.make_async_copy(count_v, count_s, copy_sem.at[0])
    copy.start()

    angle = jnp.full((8, 128), phase[0].astype(F32) * (2.0 * math.pi / PHASES), F32)
    cos_b, sin_b = jnp.cos(angle), jnp.sin(angle)
    height_cells = 8
    centre_y, centre_z = 0.5 * CELL_SIDE * lat_cells, 0.5 * CELL_SIDE * height_cells
    reach = 0.45 * CELL_SIDE * min(lat_cells, height_cells)
    shaft_id = lax.axis_index("shaft").astype(F32)
    lat_id = (lax.axis_index("lat") * 2).astype(F32)
    up_id = sub.astype(F32)
    blade = []
    for j in range(2):
        base = (5 + j) * 64
        x, y, z = (ext[base + 8 * t : base + 8 * t + 8, :] for t in range(3))
        radius = ext[base + 48 : base + 56, :]
        x = CELL_SIDE * shaft_id + x
        y = CELL_SIDE * (lat_id + j) + y - centre_y
        z = CELL_SIDE * up_id + z - centre_z
        across = y * cos_b + z * sin_b
        radial = z * cos_b - y * sin_b
        depth = jnp.maximum(jnp.minimum(radius - across, radius + BLADE_THICKNESS + across), 0.0)
        window = jnp.maximum(radial * (reach - radial), 0.0) * (4.0 / (reach * reach))
        gate = jnp.maximum(jnp.cos(x * (2.0 * math.pi / (2.0 * CELL_SIDE))), 0.0)
        size = BLADE_STIFFNESS * depth * window * gate
        blade.append(size)

    loads[0].wait()
    loads[1].wait()
    n_clump = part.shape[-1]
    cos_z, cos_y, cos_x = (jnp.cos(angles[t, 0]) for t in range(3))
    sin_z, sin_y, sin_x = (jnp.sin(angles[t, 0]) for t in range(3))
    rotation = [
        [
            cos_z * cos_y,
            cos_z * sin_y * sin_x - sin_z * cos_x,
            cos_z * sin_y * cos_x + sin_z * sin_x,
        ],
        [
            sin_z * cos_y,
            sin_z * sin_y * sin_x + cos_z * cos_x,
            sin_z * sin_y * cos_x - cos_z * sin_x,
        ],
        [-sin_y, cos_y * sin_x, cos_y * cos_x],
    ]
    for t, (a, b) in enumerate(((0, 0), (0, 1), (0, 2), (1, 1), (1, 2), (2, 2))):
        turning[t : t + 1, :] = TIME_STEP * sum(
            rotation[a][i] * inertia[i, 0] * rotation[b][i] for i in range(3)
        )
    turning[6:8, :] = jnp.zeros((2, n_clump), F32)
    copy.wait()

    lane = lax.broadcasted_iota(jnp.int32, (64, KEYS), 1)
    inert = jnp.where((lane >= 24) & (lane < 27), 1.0, 0.0)
    for j in range(2):

        def count(c, t, k):
            return count_s[0, j * 256 + (c * 3 + t) * 8 + k]

        def pick(c, k, rows, into):
            di, dj = c // 3 - 1, c % 3 - 1
            base = ((1 + di) * 4 + 1 + j + dj) * 64
            rise = CELL_SIDE * k.astype(F32) - 20.0
            shift = jnp.where(
                sub == 0,
                CELL_SIDE * di,
                jnp.where(sub == 1, CELL_SIDE * dj, jnp.where(sub == 2, rise, 0.0)),
            )
            value = ext[pl.ds(base + k, 8, stride=8), :] + shift
            spot = dest[pl.ds((j * 9 + c) * 8 + k, 1), :]
            into[0:rows, :] = lax.dot_general(
                one_hot(rows, spot), keyed(value, sub), LANES, preferred_element_type=F32
            )

        def pick_own(k, _):
            pick(4, k, 128, picked_own.at[k])
            return 0

        lax.fori_loop(0, 8, pick_own, 0)

        def gather_level(k, offset, sizes):
            sides = [c for c in range(9) if c != 4]
            for c in sides:
                pick(c, k, sizes[kind(c)][0], picked.at[c])
            for t in range(3):
                start_of_part = offset
                if t == 2:
                    bounds[0, k] = offset
                for c in sides:
                    start = 0 if t == 0 else count(c, 0, k)
                    if t == 2:
                        start = start + count(c, 1, k)
                    length = sizes[kind(c)][1 + t]
                    packed[pl.ds(offset, length), :] = picked[c, pl.ds(start, length), :]
                    offset = offset + count(c, t, k)
                if t == 0:
                    bounds[1, k] = offset
                if t == 1:
                    packed[pl.ds(offset, 64), :] = inert
                    offset = jnp.maximum(offset, start_of_part + 64)
                    below, above = jnp.maximum(k - 1, 0), jnp.minimum(k + 1, 7)
                    length = sizes[0][1]
                    start = count(4, 0, below)
                    packed[pl.ds(offset, length), :] = picked_own[below, pl.ds(start, length), :]
                    offset = offset + jnp.where(k > 0, count(4, 2, below), 0)
                    packed[pl.ds(offset, length), :] = picked_own[above, pl.ds(0, length), :]
                    offset = offset + jnp.where(k < 7, count(4, 0, above), 0)
                    packed[pl.ds(offset, 8), :] = inert[0:8]
                    offset = (offset + 7) // 8 * 8
            return offset

        def level(k, offset):
            return lax.cond(
                count_s[8 + k, j * 128] > 0,
                lambda: gather_level(k, offset, {t: (128,) * 4 for t in range(3)}),
                lambda: gather_level(k, offset, USUAL),
            )

        end = lax.fori_loop(0, 8, level, jnp.int32(0))
        packed[pl.ds(end, 64), :] = inert
        bounds[1, 8] = end

        def cell(k, _):
            rise = CELL_SIDE * k.astype(F32) - 20.0
            base = (5 + j) * 64
            own = [ext[pl.ds(base + 8 * t + k, 1), :] for t in range(7)]
            own[2] = own[2] + rise
            own_table(own, sub, table)
            first = jnp.where(k == 0, 0, bounds[0, jnp.maximum(k - 1, 0)])
            last = bounds[1, k + 1]

            def rows(i):
                return packed[pl.ds(pl.multiple_of(first + i * CHUNK, 8), CHUNK), :]

            def chunks(i, acc):
                acc = use(pairs_a, acc)
                fill(rows(2 * i + 2), table, pairs_a)
                acc = use(pairs_b, acc)
                fill(rows(2 * i + 3), table, pairs_b)
                return acc

            fill(rows(0), table, pairs_a)
            fill(rows(1), table, pairs_b)
            zero = jnp.zeros((8, 128), F32)
            sums = lax.fori_loop(
                0, (last - first + 2 * CHUNK - 1) // (2 * CHUNK), chunks, (zero, zero, zero)
            )
            for t in range(3):
                force[pl.ds((j * 8 + t) * 8 + k, 1), :] = jnp.sum(sums[t], 0, keepdims=True)
            return 0

        lax.fori_loop(0, 8, cell, 0)

    loads[2].wait()
    terms = []
    for j in range(2):
        fx, fy, fz = (
            force[(j * 8 + t) * 8 : (j * 8 + t) * 8 + 8, :]
            + inside[(j * 8 + t) * 8 : (j * 8 + t) * 8 + 8, :]
            for t in range(3)
        )
        fy, fz = fy + blade[j] * cos_b, fz + blade[j] * sin_b
        ox, oy, oz = (off[t, 0, j] for t in range(3))
        six = [fx, fy, fz, oy * fz - oz * fy, oz * fx - ox * fz, ox * fy - oy * fx]
        for t in range(8):
            force[(j * 8 + t) * 8 : (j * 8 + t) * 8 + 8, :] = (
                six[t] if t < 6 else jnp.zeros((8, 128), F32)
            )
        for k in range(8):
            terms.append(rows3(force[pl.ds(j * 64 + k, 8, stride=8), :]))
    sums = lax.dot_general(
        jnp.concatenate(terms, 1), hot_piece[...], LANES, preferred_element_type=F32
    )
    sums = sum3(
        lax.dot_general(rows3(sum3(sums)), hot_clump[...], LANES, preferred_element_type=F32)
    )
    for c in range(9):
        part[c] = sums[:, c * n_clump : (c + 1) * n_clump]


def finish_kernel(
    n_shaft,
    n_lat,
    part_any,
    part,
    turning,
    hot_piece,
    hot_clump,
    centre_hbm,
    motion_hbm,
    inverse_mass_hbm,
    off_hbm,
    clump_out,
    sphere_out,
    centre,
    motion,
    inverse_mass,
    off,
    got,
    table,
    pose,
    send_sem,
    recv_sem,
    load_sem,
):
    place = Place(n_shaft, n_lat)
    n_clump = part.shape[-1]
    loads = [
        pltpu.make_async_copy(src, dst, load_sem.at[t])
        for t, (src, dst) in enumerate(
            (
                (centre_hbm, centre),
                (motion_hbm, motion),
                (inverse_mass_hbm, inverse_mass),
                (off_hbm, off),
            )
        )
    ]
    for load in loads:
        load.start()

    def sums_copy(ds, dl, slot):
        c = (ds + 1) * 3 + dl + 1
        return pltpu.make_async_remote_copy(
            src_ref=part_any.at[c],
            dst_ref=got.at[slot],
            send_sem=send_sem.at[0, slot],
            recv_sem=recv_sem.at[0, slot],
            device_id=place.at(ds, dl),
            device_id_type=MESH,
        )

    def table_copy(ds, dl, slot):
        return pltpu.make_async_remote_copy(
            src_ref=table.at[4],
            dst_ref=table.at[slot],
            send_sem=send_sem.at[1, slot],
            recv_sem=recv_sem.at[1, slot],
            device_id=place.at(ds, dl),
            device_id_type=MESH,
        )

    def around(act, dl):
        for ds in (-1, 0, 1):
            if (ds, dl) != (0, 0):
                act(ds, dl)

    place.barrier()
    place.lateral(
        lambda dl: around(lambda ds, d: sums_copy(ds, d, (ds + 1) * 3 + d + 1).start(), dl)
    )

    def clear(edge, column):
        @pl.when(place.l == edge)
        def _():
            for row in range(3):
                table[row * 3 + column] = jnp.zeros((8, n_clump), F32)
                got[row * 3 + 2 - column] = jnp.zeros((8, n_clump), F32)

    clear(0, 0)
    clear(n_lat - 1, 2)
    for load in loads:
        load.wait()
    place.lateral(
        lambda dl: around(lambda ds, d: sums_copy(ds, d, 8 - (ds + 1) * 3 - d - 1).wait_recv(), dl)
    )
    sums = part[4]
    for c in range(9):
        if c != 4:
            sums = sums + got[c]
    rows = []
    for t in range(3):
        pull = -GRAVITY if t == 2 else 0.0
        rows.append(motion[t, 0] + TIME_STEP * (inverse_mass[0] * sums[t : t + 1] + pull))
    torque = [sums[3 + t : 4 + t] for t in range(3)]
    order = ((0, 1, 2), (1, 3, 4), (2, 4, 5))
    for t in range(3):
        change = sum(turning[order[t][i] : order[t][i] + 1, :] * torque[i] for i in range(3))
        rows.append(motion[3 + t, 0] + change)
    table[4] = jnp.concatenate(rows + [jnp.zeros((2, n_clump), F32)], 0)
    for t in range(3):
        clump_out[t, 0] = centre[t, 0] + TIME_STEP * rows[t]
    for t in range(6):
        clump_out[3 + t, 0] = rows[t]
    place.lateral(
        lambda dl: around(lambda ds, d: table_copy(ds, d, 8 - (ds + 1) * 3 - d - 1).start(), dl)
    )
    place.lateral(
        lambda dl: around(lambda ds, d: table_copy(ds, d, (ds + 1) * 3 + d + 1).wait_recv(), dl)
    )
    tables = jnp.concatenate([rows3(table[c]) for c in range(9)], 1)
    by_piece = lax.dot_general(tables, hot_clump[...], ROWS, preferred_element_type=F32)
    by_piece = by_piece.astype(BF16)
    by_sphere = sum3(
        lax.dot_general(by_piece, hot_piece[...], ROWS, preferred_element_type=F32)
    )
    for m in range(16):
        pose[m * 8 : m * 8 + 8, :] = by_sphere[:, m * 128 : m * 128 + 128]
    for j in range(2):
        vx, vy, vz, sx, sy, sz = (
            pose[pl.ds(j * 64 + t, 8, stride=8), :] for t in range(6)
        )
        bx, by, bz = (off[t, 0, j] for t in range(3))
        hx, hy, hz = (0.5 * TIME_STEP * s for s in (sx, sy, sz))
        scale = 2.0 / (1.0 + (hx * hx + hy * hy + hz * hz))
        cx, cy, cz = hy * bz - hz * by, hz * bx - hx * bz, hx * by - hy * bx
        tx = bx + scale * (cx + hy * cz - hz * cy)
        ty = by + scale * (cy + hz * cx - hx * cz)
        tz = bz + scale * (cz + hx * cy - hy * cx)
        sphere_out[0, 0, j], sphere_out[1, 0, j], sphere_out[2, 0, j] = tx, ty, tz
        sphere_out[3, 0, j] = vx + (sy * tz - sz * ty)
        sphere_out[4, 0, j] = vy + (sz * tx - sx * tz)
        sphere_out[5, 0, j] = vz + (sx * ty - sy * tx)
    place.lateral(
        lambda dl: around(lambda ds, d: sums_copy(ds, d, (ds + 1) * 3 + d + 1).wait_send(), dl)
    )
    place.lateral(
        lambda dl: around(lambda ds, d: table_copy(ds, d, 8 - (ds + 1) * 3 - d - 1).wait_send(), dl)
    )


def contact_call(
    lat_cells, blade_phase, ext, hot_piece, hot_clump, inside, off, angles, inertia, **extra
):
    n_clump = angles.shape[-1]
    return pl.pallas_call(
        functools.partial(contact_kernel, lat_cells),
        out_shape=(
            jax.ShapeDtypeStruct((9, 8, n_clump), F32),
            jax.ShapeDtypeStruct((8, n_clump), F32),
        ),
        in_specs=[SMEM] + [VMEM] * 4 + [HBM] * 3,
        out_specs=(VMEM, VMEM),
        scratch_shapes=[
            pltpu.VMEM(off.shape, F32),
            pltpu.VMEM(angles.shape, F32),
            pltpu.VMEM(inertia.shape, F32),
            pltpu.VMEM((144, 128), jnp.int32),
            pltpu.VMEM((16, 512), jnp.int32),
            pltpu.SMEM((16, 512), jnp.int32),
            pltpu.SMEM((2, 16), jnp.int32),
            pltpu.VMEM((9, 256, KEYS), F32),
            pltpu.VMEM((8, 256, KEYS), F32),
            pltpu.VMEM((9 * 1024 + 8 * 72 + 256, KEYS), F32),
            pltpu.VMEM((KEYS, TERMS * 128), BF16),
            pltpu.VMEM((CHUNK, TERMS * 128), F32),
            pltpu.VMEM((CHUNK, TERMS * 128), F32),
            pltpu.VMEM((128, 128), F32),
            pltpu.SemaphoreType.DMA((4,)),
        ],
        compiler_params=pltpu.CompilerParams(vmem_limit_bytes=20 << 20),
        name="contact",
        **extra,
    )(blade_phase, ext, hot_piece, hot_clump, inside, off, angles, inertia)


def on_device(
    n_shaft,
    n_lat,
    sphere_position,
    sphere_velocity,
    sphere_radius,
    sphere_offset,
    sphere_piece,
    piece_route,
    piece_clump,
    blade_phase,
    clump_centre,
    clump_motion,
    clump_angles,
    clump_inverse_mass,
    clump_inverse_inertia,
):
    n_piece, n_clump = piece_route.shape[-1], clump_angles.shape[-1]
    sphere_position, sphere_velocity, sphere_radius, sphere_piece, piece_route, piece_clump = (
        pltpu.with_memory_space_constraint(v, pltpu.HBM)
        for v in (
            sphere_position,
            sphere_velocity,
            sphere_radius,
            sphere_piece,
            piece_route,
            piece_clump,
        )
    )
    sphere_offset, clump_centre, clump_motion = (
        pltpu.with_memory_space_constraint(v, pltpu.HBM)
        for v in (sphere_offset, clump_centre, clump_motion)
    )
    clump_angles, clump_inverse_mass, clump_inverse_inertia = (
        pltpu.with_memory_space_constraint(v, pltpu.HBM)
        for v in (clump_angles, clump_inverse_mass, clump_inverse_inertia)
    )
    ext, hot_piece, hot_clump, inside = pl.pallas_call(
        functools.partial(halo_kernel, n_shaft, n_lat),
        out_shape=(
            jax.ShapeDtypeStruct((3, 4, 8, 8, 128), F32),
            jax.ShapeDtypeStruct((n_piece, 2048), BF16),
            jax.ShapeDtypeStruct((9 * n_clump, n_piece), BF16),
            jax.ShapeDtypeStruct((128, 128), F32),
        ),
        in_specs=[HBM] * 6,
        out_specs=(VMEM,) * 4,
        scratch_shapes=[
            pltpu.VMEM(sphere_piece.shape, jnp.int32),
            pltpu.VMEM(piece_route.shape, jnp.int32),
            pltpu.VMEM(piece_clump.shape, jnp.int32),
            pltpu.VMEM((KEYS, TERMS * 128), BF16),
            pltpu.VMEM((CHUNK, TERMS * 128), F32),
            pltpu.VMEM((CHUNK, TERMS * 128), F32),
            pltpu.SemaphoreType.DMA((3, 4, 3)),
            pltpu.SemaphoreType.DMA((3, 4, 3)),
            pltpu.SemaphoreType.DMA((2, 3)),
            pltpu.SemaphoreType.DMA((3,)),
        ],
        compiler_params=pltpu.CompilerParams(
            collective_id=0, has_side_effects=True, vmem_limit_bytes=16 << 20
        ),
        name="halo",
    )(
        sphere_position,
        sphere_velocity,
        sphere_radius,
        sphere_piece,
        piece_route,
        piece_clump,
    )
    part, turning = contact_call(
        2 * n_lat,
        blade_phase,
        ext.reshape(768, 128),
        hot_piece,
        hot_clump,
        inside,
        sphere_offset,
        clump_angles,
        clump_inverse_inertia,
    )
    return pl.pallas_call(
        functools.partial(finish_kernel, n_shaft, n_lat),
        out_shape=(
            jax.ShapeDtypeStruct((9, 1, 1, n_clump), F32),
            jax.ShapeDtypeStruct((6, 1, 2, 8, 128), F32),
        ),
        in_specs=[VMEM] * 5 + [HBM] * 4,
        out_specs=(VMEM, VMEM),
        scratch_shapes=[
            pltpu.VMEM(clump_centre.shape, F32),
            pltpu.VMEM(clump_motion.shape, F32),
            pltpu.VMEM(clump_inverse_mass.shape, F32),
            pltpu.VMEM(sphere_offset.shape, F32),
            pltpu.VMEM((9, 8, n_clump), F32),
            pltpu.VMEM((9, 8, n_clump), F32),
            pltpu.VMEM((128, 128), F32),
            pltpu.SemaphoreType.DMA((2, 9)),
            pltpu.SemaphoreType.DMA((2, 9)),
            pltpu.SemaphoreType.DMA((4,)),
        ],
        compiler_params=pltpu.CompilerParams(
            collective_id=1, has_side_effects=True, vmem_limit_bytes=16 << 20
        ),
        name="finish",
    )(
        part,
        part,
        turning,
        hot_piece,
        hot_clump,
        clump_centre,
        clump_motion,
        clump_inverse_mass,
        sphere_offset,
    )


def solution(mesh):
    placed = (
        P(None, "shaft", "lat", None, None),
        P(None, "shaft", "lat", None, None),
        P("shaft", "lat", None, None),
        P(None, "shaft", "lat", None, None),
        P("shaft", "lat", None),
        P("shaft", "lat", None),
        P("shaft", "lat", None),
        P(),
        P(None, "shaft", "lat", None),
        P(None, "shaft", "lat", None),
        P(None, "shaft", "lat", None),
        P("shaft", "lat", None),
        P(None, "shaft", "lat", None),
    )
    return jax.shard_map(
        functools.partial(on_device, mesh.shape["shaft"], mesh.shape["lat"]),
        mesh=mesh,
        in_specs=placed,
        out_specs=(P(None, "shaft", "lat", None), P(None, "shaft", "lat", None, None)),
        check_vma=False,
    )
```

```python
import functools
import math

import jax
import jax.numpy as jnp
from jax import lax
from jax.experimental import pallas as pl
from jax.experimental.pallas import tpu as pltpu
from jax.sharding import PartitionSpec as P

PHASES = 64
CELL_SIDE = 5.0
BLADE_STIFFNESS = 20.0
BLADE_THICKNESS = 1.0
TIME_STEP = 0.5
GRAVITY = 0.5

REACH = 0.6001
CHUNK = 64
F32 = jnp.float32
BF16 = jnp.bfloat16
MESH = pl.DeviceIdType.MESH
LANES = (((1,), (1,)), ((), ()))
ROWS = (((1,), (0,)), ((), ()))
VMEM = pl.BlockSpec(memory_space=pltpu.VMEM)
SMEM = pl.BlockSpec(memory_space=pltpu.SMEM)
HBM = pl.BlockSpec(memory_space=pltpu.HBM)


def split3(x):
    high = x.astype(BF16)
    rest = x - high.astype(F32)
    middle = rest.astype(BF16)
    low = (rest - middle.astype(F32)).astype(BF16)
    return high, middle, low


def rows3(x):
    high = x.astype(BF16).astype(F32)
    rest = x - high
    middle = rest.astype(BF16).astype(F32)
    return jnp.concatenate([high, middle, rest - middle], 0).astype(BF16)


def sum3(x):
    return x[0:8] + x[8:16] + x[16:24]


def one_hot(rows, row):
    length = row.shape[-1]
    ids = lax.broadcasted_iota(jnp.int32, (rows, length), 0)
    return jnp.where(ids == row, 1.0, 0.0).astype(BF16)


class Place:
    def __init__(self, n_shaft, n_lat):
        self.n_shaft, self.n_lat = n_shaft, n_lat
        self.s, self.l = lax.axis_index("shaft"), lax.axis_index("lat")

    def at(self, ds, dl):
        return {"shaft": lax.rem(self.s + ds + self.n_shaft, self.n_shaft), "lat": self.l + dl}

    def lateral(self, act):
        act(0)
        pl.when(self.l > 0)(lambda: act(-1))
        pl.when(self.l < self.n_lat - 1)(lambda: act(1))

    def greet(self):
        sem = pltpu.get_barrier_semaphore()

        def signal(dl):
            for ds in (-1, 0, 1):
                if (ds, dl) != (0, 0):
                    pl.semaphore_signal(
                        sem, inc=1, device_id=self.at(ds, dl), device_id_type=MESH
                    )

        self.lateral(signal)

    def meet(self):
        sem = pltpu.get_barrier_semaphore()
        edge = jnp.logical_or(self.l == 0, self.l == self.n_lat - 1)
        pl.semaphore_wait(sem, jnp.where(edge, 5, 8))


def halo_kernel(
    n_shaft,
    n_lat,
    pos,
    vel,
    rad,
    piece_hbm,
    route_hbm,
    clump_hbm,
    ext,
    hot_piece,
    hot_clump,
    inside,
    tables,
    piece,
    route,
    clump,
    send_sem,
    recv_sem,
    own_sem,
    load_sem,
):
    place = Place(n_shaft, n_lat)

    def parts(j, si, lj):
        return (
            (pos.at[:, 0, j], ext.at[si, lj, 0:3]),
            (vel.at[:, 0, j], ext.at[si, lj, 3:6]),
            (rad.at[0, pl.ds(j, 1)], ext.at[si, lj, 6:7]),
        )

    def remote(j, ds, dl, si, lj):
        return [
            pltpu.make_async_remote_copy(
                src_ref=src,
                dst_ref=dst,
                send_sem=send_sem.at[si, lj, t],
                recv_sem=recv_sem.at[si, lj, t],
                device_id=place.at(ds, dl),
                device_id_type=MESH,
            )
            for t, (src, dst) in enumerate(parts(j, si, lj))
        ]

    def outgoing(dl):
        found = []
        for ds in (-1, 0, 1):
            for j in (0, 1):
                lj = j - 2 * dl + 1
                if 0 <= lj <= 3 and (ds, dl) != (0, 0):
                    found += remote(j, ds, dl, 1 - ds, lj)
        return found

    def incoming(dl):
        found = []
        for ds in (-1, 0, 1):
            for lj in {0: (1, 2), -1: (0,), 1: (3,)}[dl]:
                if (ds, dl) != (0, 0):
                    found += remote(0, ds, dl, 1 + ds, lj)
        return found

    own = [
        pltpu.make_async_copy(src, dst, own_sem.at[j, t])
        for j in (0, 1)
        for t, (src, dst) in enumerate(parts(j, 1, 1 + j))
    ]
    own += [
        pltpu.make_async_copy(src, dst, load_sem.at[t])
        for t, (src, dst) in enumerate(
            ((piece_hbm, piece), (route_hbm, route), (clump_hbm, clump))
        )
    ]
    for c in own:
        c.start()
    place.greet()
    place.meet()
    place.lateral(lambda dl: [c.start() for c in outgoing(dl)] and None)
    ext[:, :, 7] = jnp.zeros((3, 4, 8, 128), F32)

    @pl.when(place.l == 0)
    def _():
        ext[:, 0, 0:7] = jnp.zeros((3, 7, 8, 128), F32)

    @pl.when(place.l == n_lat - 1)
    def _():
        ext[:, 3, 0:7] = jnp.zeros((3, 7, 8, 128), F32)

    for c in own:
        c.wait()
    sub = lax.broadcasted_iota(jnp.int32, (8, 128), 0)
    every = one_hot(128, lax.broadcasted_iota(jnp.int32, (1, 128), 1))
    inside[...] = jnp.zeros((128, 128), F32)

    def cell(m, _):
        j, k = m // 8, m % 8
        mine = [ext[1, 1 + j, t, pl.ds(k, 1), :] for t in range(7)]
        mine[2] = mine[2] + (CELL_SIDE * k.astype(F32) - 20.0)
        own_table(mine, sub, tables.at[m])
        value = jnp.concatenate(mine + [mine[6]], 0)
        rows = lax.dot_general(every, keyed(value, sub), LANES, preferred_element_type=F32)
        zero = jnp.zeros((8, 128), F32)
        acc = (zero, zero, zero)
        for i in range(0, 128, CHUNK):
            acc = add_pairs(rows[i : i + CHUNK], tables.at[m], acc)
        for t in range(3):
            inside[pl.ds((j * 8 + t) * 8 + k, 1), :] = jnp.sum(acc[t], 0, keepdims=True)
        return 0

    lax.fori_loop(0, 16, cell, 0)
    for m in range(16):
        hot_piece[:, m * 128 : m * 128 + 128] = one_hot(
            hot_piece.shape[0], piece[0, :, m * 128 : m * 128 + 128]
        )
    n_clump = hot_clump.shape[0] // 9
    for c in range(9):
        hot_clump[c * n_clump : (c + 1) * n_clump, :] = one_hot(
            n_clump, jnp.where(route[0] == c, clump[0], -1)
        )
    place.lateral(lambda dl: [c.wait_recv() for c in incoming(dl)] and None)
    place.lateral(lambda dl: [c.wait_send() for c in outgoing(dl)] and None)


USUAL = {0: (128, 64, 64, 64), 1: (64, 24, 40, 24), 2: (32, 16, 24, 16)}
KEYS = 32
TERMS = 9


def kind(c):
    return (c // 3 != 1) + (c % 3 != 1)


def keyed(value, sub):
    radius = value[6:7]
    value = jnp.where(sub == 7, radius * radius * 0.0625, value)
    high = value.astype(BF16).astype(F32)
    rest = value - high
    middle = rest.astype(BF16).astype(F32)
    more = jnp.where(
        sub < 3,
        1.0,
        jnp.where(sub < 5, high[6:7], jnp.where(sub == 5, middle[6:7], 0.0)),
    )
    return jnp.concatenate([high, middle, rest - middle, more], 0).astype(BF16)


def own_table(own, sub, table):
    zero = jnp.zeros((8, 128), F32)

    def split(row):
        return [p.astype(F32) for p in split3(jnp.broadcast_to(row, (8, 128)))]

    def constants(row):
        high, middle, low = split(row)
        return jnp.where(sub == 0, high, jnp.where(sub == 1, middle, jnp.where(sub == 2, low, 0.0)))

    def put(t, same, more):
        block = jnp.concatenate([same, same, same, more], 0)
        table[:, t * 128 : t * 128 + 128] = block.astype(BF16)

    for t in range(7):
        put(t, jnp.where(sub == t, 1.0 if t == 6 else -1.0, zero), constants(own[t]))
    high, middle, low = split(4.0 * own[6])
    same = jnp.where(sub == 6, high, 0.0)
    more = jnp.where(sub == 4, low, jnp.where((sub == 3) | (sub == 5), middle, 0.0))
    put(7, same, more)
    put(
        8,
        jnp.where(sub == 7, 1.0, same * 0.03125),
        more * 0.03125 + constants(own[6] * own[6] * 0.0625),
    )


def pair_sums(pair, acc):
    dx, dy, dz, du, dv, dw, radii, product, least = pair
    square = dx * dx + dy * dy + dz * dz
    clamped = jnp.maximum(square, least)
    inverse = lax.rsqrt(clamped)
    delta = jnp.maximum(radii - clamped * inverse, 0.0)
    normal_speed = (du * dx + dv * dy + dw * dz) * inverse
    speed = du * du + dv * dv + dw * dw
    unit = square * (inverse * inverse)
    sliding = speed + normal_speed * normal_speed * (unit - 2.0)
    load = product * delta
    root = load * lax.rsqrt(jnp.maximum(load * radii, 1e-30))
    root2 = root * root
    cap = 2.5 * delta
    shear = root2 * cap * lax.rsqrt(jnp.maximum(root2 * (sliding + cap * cap), 0.0) + 1e-06)
    push = root * (cap + cap - normal_speed - 0.25)
    along = (push + shear * normal_speed) * inverse
    return (
        acc[0] + (along * dx - shear * du),
        acc[1] + (along * dy - shear * dv),
        acc[2] + (along * dz - shear * dw),
    )


def add_pairs(rows, table, acc):
    pairs = lax.dot_general(rows.astype(BF16), table[...], ROWS, preferred_element_type=F32)
    for g in range(0, CHUNK, 8):
        acc = pair_sums([pairs[g : g + 8, t * 128 : t * 128 + 128] for t in range(TERMS)], acc)
    return acc


def contact_kernel(
    lat_cells,
    phase,
    ext,
    inside,
    tables,
    off_hbm,
    angles_hbm,
    inertia_hbm,
    force,
    turning,
    off,
    angles,
    inertia,
    dest,
    count_v,
    count_s,
    bounds,
    picked,
    packed,
    copy_sem,
):
    loads = [
        pltpu.make_async_copy(src, dst, copy_sem.at[1 + t])
        for t, (src, dst) in enumerate(
            ((angles_hbm, angles), (inertia_hbm, inertia), (off_hbm, off))
        )
    ]
    for load in loads:
        load.start()
    sub = lax.broadcasted_iota(jnp.int32, (8, 128), 0)

    before = jnp.where(
        lax.broadcasted_iota(jnp.int32, (128, 128), 0)
        < lax.broadcasted_iota(jnp.int32, (128, 128), 1),
        1.0,
        0.0,
    ).astype(BF16)
    ones = jnp.ones((128, 128), BF16)
    for j in range(2):
        masks = []
        for c in range(9):
            di, dj = c // 3 - 1, c % 3 - 1
            base = ((1 + di) * 4 + 1 + j + dj) * 64
            x, y, z = (ext[base + 8 * t : base + 8 * t + 8, :] for t in range(3))
            radius = ext[base + 48 : base + 56, :]
            keep = radius > 0.0
            near = radius + REACH
            away = [v if d > 0 else CELL_SIDE - v for v, d in ((x, di), (y, dj)) if d]
            if len(away) == 1:
                keep &= away[0] < near
            if len(away) == 2:
                keep &= away[0] * away[0] + away[1] * away[1] < near * near
            low, high = z < near, CELL_SIDE - z < near
            kept = jnp.where(keep, 1.0, 0.0)
            low_f = jnp.where(low, kept, 0.0)
            high_f = jnp.where(high, kept, 0.0)
            mid_f = jnp.zeros((8, 128), F32) if c == 4 else kept - low_f - high_f
            masks += [low_f, mid_f, high_f]
        mask = jnp.concatenate(masks, 0).astype(BF16)
        prefix = lax.dot_general(mask, before, ROWS, preferred_element_type=F32)
        total = lax.dot_general(mask, ones, ROWS, preferred_element_type=F32)
        counts = lax.dot_general(ones[0:8], mask, LANES, preferred_element_type=F32)
        count_v[0:8, j * 256 : j * 256 + 216] = counts.astype(jnp.int32)
        over = jnp.full((8, 128), -1.0, F32)
        for c in range(9):
            a = c * 24
            low_p, mid_p, high_p = (prefix[a + 8 * t : a + 8 * t + 8] for t in range(3))
            low_n, mid_n, high_n = (total[a + 8 * t : a + 8 * t + 8] for t in range(3))
            spot = (
                masks[3 * c] * low_p
                + masks[3 * c + 1] * (low_n + mid_p)
                + masks[3 * c + 2] * (low_n + mid_n + high_p)
            )
            any_of = masks[3 * c] + masks[3 * c + 1] + masks[3 * c + 2]
            spot = jnp.where(any_of > 0.0, spot, -1.0).astype(jnp.int32)
            dest[(j * 9 + c) * 8 : (j * 9 + c) * 8 + 8, :] = spot
            sizes = (low_n + mid_n + high_n, low_n, mid_n, high_n)
            for size, usual in zip(sizes, USUAL[kind(c)]):
                excess = size - usual
                if c == 4:
                    excess = jnp.max(excess, 0, keepdims=True)
                over = jnp.maximum(over, excess)
        count_v[8:16, j * 128 : j * 128 + 128] = over.astype(jnp.int32)
    copy = pltpu.make_async_copy(count_v, count_s, copy_sem.at[0])
    copy.start()

    angle = jnp.full((8, 128), phase[0].astype(F32) * (2.0 * math.pi / PHASES), F32)
    cos_b, sin_b = jnp.cos(angle), jnp.sin(angle)
    height_cells = 8
    centre_y, centre_z = 0.5 * CELL_SIDE * lat_cells, 0.5 * CELL_SIDE * height_cells
    reach = 0.45 * CELL_SIDE * min(lat_cells, height_cells)
    shaft_id = lax.axis_index("shaft").astype(F32)
    lat_id = (lax.axis_index("lat") * 2).astype(F32)
    up_id = sub.astype(F32)
    blade = []
    for j in range(2):
        base = (5 + j) * 64
        x, y, z = (ext[base + 8 * t : base + 8 * t + 8, :] for t in range(3))
        radius = ext[base + 48 : base + 56, :]
        x = CELL_SIDE * shaft_id + x
        y = CELL_SIDE * (lat_id + j) + y - centre_y
        z = CELL_SIDE * up_id + z - centre_z
        across = y * cos_b + z * sin_b
        radial = z * cos_b - y * sin_b
        depth = jnp.maximum(jnp.minimum(radius - across, radius + BLADE_THICKNESS + across), 0.0)
        window = jnp.maximum(radial * (reach - radial), 0.0) * (4.0 / (reach * reach))
        gate = jnp.maximum(jnp.cos(x * (2.0 * math.pi / (2.0 * CELL_SIDE))), 0.0)
        size = BLADE_STIFFNESS * depth * window * gate
        blade.append(size)

    loads[0].wait()
    loads[1].wait()
    n_clump = turning.shape[-1]
    cos_z, cos_y, cos_x = (jnp.cos(angles[t, 0]) for t in range(3))
    sin_z, sin_y, sin_x = (jnp.sin(angles[t, 0]) for t in range(3))
    rotation = [
        [
            cos_z * cos_y,
            cos_z * sin_y * sin_x - sin_z * cos_x,
            cos_z * sin_y * cos_x + sin_z * sin_x,
        ],
        [
            sin_z * cos_y,
            sin_z * sin_y * sin_x + cos_z * cos_x,
            sin_z * sin_y * cos_x - cos_z * sin_x,
        ],
        [-sin_y, cos_y * sin_x, cos_y * cos_x],
    ]
    for t, (a, b) in enumerate(((0, 0), (0, 1), (0, 2), (1, 1), (1, 2), (2, 2))):
        turning[t : t + 1, :] = TIME_STEP * sum(
            rotation[a][i] * inertia[i, 0] * rotation[b][i] for i in range(3)
        )
    turning[6:8, :] = jnp.zeros((2, n_clump), F32)
    copy.wait()

    lane = lax.broadcasted_iota(jnp.int32, (64, KEYS), 1)
    inert = jnp.where((lane >= 24) & (lane < 27), 1.0, 0.0)
    for j in range(2):

        def count(c, t, k):
            return count_s[0, j * 256 + (c * 3 + t) * 8 + k]

        def pick(c, k, rows, into):
            di, dj = c // 3 - 1, c % 3 - 1
            base = ((1 + di) * 4 + 1 + j + dj) * 64
            rise = CELL_SIDE * k.astype(F32) - 20.0
            shift = jnp.where(
                sub == 0,
                CELL_SIDE * di,
                jnp.where(sub == 1, CELL_SIDE * dj, jnp.where(sub == 2, rise, 0.0)),
            )
            value = ext[pl.ds(base + k, 8, stride=8), :] + shift
            spot = dest[pl.ds((j * 9 + c) * 8 + k, 1), :]
            into[k, 0:rows, :] = lax.dot_general(
                one_hot(rows, spot), keyed(value, sub), LANES, preferred_element_type=F32
            )

        sides = [c for c in range(9) if c != 4]

        def pick_two(i, _):
            for k in (2 * i, 2 * i + 1):
                for c in range(9):
                    pick(c, k, USUAL[kind(c)][0], picked.at[c])
            return 0

        lax.fori_loop(0, 4, pick_two, 0)

        def gather_level(k, offset, sizes):
            for t in range(3):
                start_of_part = offset
                if t == 2:
                    bounds[0, k] = offset
                for c in sides:
                    start = 0 if t == 0 else count(c, 0, k)
                    if t == 2:
                        start = start + count(c, 1, k)
                    length = sizes[kind(c)][1 + t]
                    packed[pl.ds(offset, length), :] = picked[c, k, pl.ds(start, length), :]
                    offset = offset + count(c, t, k)
                if t == 0:
                    bounds[1, k] = offset
                if t == 1:
                    packed[pl.ds(offset, 64), :] = inert
                    offset = jnp.maximum(offset, start_of_part + 64)
                    below, above = jnp.maximum(k - 1, 0), jnp.minimum(k + 1, 7)
                    length = sizes[0][1]
                    start = count(4, 0, below)
                    packed[pl.ds(offset, length), :] = picked[4, below, pl.ds(start, length), :]
                    offset = offset + jnp.where(k > 0, count(4, 2, below), 0)
                    packed[pl.ds(offset, length), :] = picked[4, above, pl.ds(0, length), :]
                    offset = offset + jnp.where(k < 7, count(4, 0, above), 0)
                    packed[pl.ds(offset, 8), :] = inert[0:8]
                    offset = (offset + 7) // 8 * 8
            return offset

        def gather_all(k, offset):
            for c in sides:
                pick(c, k, 128, picked.at[c])
            return gather_level(k, offset, {t: (128,) * 4 for t in range(3)})

        def level(k, offset):
            return lax.cond(
                count_s[8 + k, j * 128] > 0,
                lambda: gather_all(k, offset),
                lambda: gather_level(k, offset, USUAL),
            )

        end = lax.fori_loop(0, 8, level, jnp.int32(0))
        packed[pl.ds(end, 64), :] = inert
        bounds[1, 8] = end

        def cell(k, _):
            first = jnp.where(k == 0, 0, bounds[0, jnp.maximum(k - 1, 0)])
            last = bounds[1, k + 1]
            table = tables.at[j * 8 + k]

            def chunk(i, acc):
                at = pl.multiple_of(first + i * CHUNK, 8)
                return add_pairs(packed[pl.ds(at, CHUNK), :], table, acc)

            zero = jnp.zeros((8, 128), F32)
            sums = lax.fori_loop(0, (last - first + CHUNK - 1) // CHUNK, chunk, (zero, zero, zero))
            for t in range(3):
                force[pl.ds((j * 8 + t) * 8 + k, 1), :] = jnp.sum(sums[t], 0, keepdims=True)
            return 0

        lax.fori_loop(0, 8, cell, 0)

    loads[2].wait()
    for j in range(2):
        fx, fy, fz = (
            force[(j * 8 + t) * 8 : (j * 8 + t) * 8 + 8, :]
            + inside[(j * 8 + t) * 8 : (j * 8 + t) * 8 + 8, :]
            for t in range(3)
        )
        fy, fz = fy + blade[j] * cos_b, fz + blade[j] * sin_b
        ox, oy, oz = (off[t, 0, j] for t in range(3))
        six = [fx, fy, fz, oy * fz - oz * fy, oz * fx - ox * fz, ox * fy - oy * fx]
        for t in range(8):
            force[(j * 8 + t) * 8 : (j * 8 + t) * 8 + 8, :] = (
                six[t] if t < 6 else jnp.zeros((8, 128), F32)
            )


def exchange_kernel(
    n_shaft,
    n_lat,
    force,
    hot_piece,
    hot_clump,
    turning,
    motion_hbm,
    inverse_mass_hbm,
    table,
    motion,
    inverse_mass,
    part,
    got,
    send_sem,
    recv_sem,
    load_sem,
):
    place = Place(n_shaft, n_lat)
    n_clump = turning.shape[-1]
    place.greet()
    loads = [
        pltpu.make_async_copy(motion_hbm, motion, load_sem.at[0]),
        pltpu.make_async_copy(inverse_mass_hbm, inverse_mass, load_sem.at[1]),
    ]
    for load in loads:
        load.start()

    def sums_copy(ds, dl, slot):
        c = (ds + 1) * 3 + dl + 1
        return pltpu.make_async_remote_copy(
            src_ref=part.at[c],
            dst_ref=got.at[slot],
            send_sem=send_sem.at[0, slot],
            recv_sem=recv_sem.at[0, slot],
            device_id=place.at(ds, dl),
            device_id_type=MESH,
        )

    def table_copy(ds, dl, slot):
        return pltpu.make_async_remote_copy(
            src_ref=table.at[4],
            dst_ref=table.at[slot],
            send_sem=send_sem.at[1, slot],
            recv_sem=recv_sem.at[1, slot],
            device_id=place.at(ds, dl),
            device_id_type=MESH,
        )

    def around(act, dl):
        for ds in (-1, 0, 1):
            if (ds, dl) != (0, 0):
                act(ds, dl)

    terms = [
        rows3(force[pl.ds(j * 64 + k, 8, stride=8), :]) for j in range(2) for k in range(8)
    ]
    sums = lax.dot_general(
        jnp.concatenate(terms, 1), hot_piece[...], LANES, preferred_element_type=F32
    )
    sums = sum3(
        lax.dot_general(rows3(sum3(sums)), hot_clump[...], LANES, preferred_element_type=F32)
    )
    for c in range(9):
        part[c] = sums[:, c * n_clump : (c + 1) * n_clump]

    def clear(edge, column):
        @pl.when(place.l == edge)
        def _():
            for row in range(3):
                table[row * 3 + column] = jnp.zeros((8, n_clump), F32)
                got[row * 3 + 2 - column] = jnp.zeros((8, n_clump), F32)

    clear(0, 0)
    clear(n_lat - 1, 2)
    place.meet()
    place.lateral(
        lambda dl: around(lambda ds, d: sums_copy(ds, d, (ds + 1) * 3 + d + 1).start(), dl)
    )
    for load in loads:
        load.wait()
    place.lateral(
        lambda dl: around(lambda ds, d: sums_copy(ds, d, 8 - (ds + 1) * 3 - d - 1).wait_recv(), dl)
    )
    sums = part[4]
    for c in range(9):
        if c != 4:
            sums = sums + got[c]
    rows = []
    for t in range(3):
        pull = -GRAVITY if t == 2 else 0.0
        rows.append(motion[t, 0] + TIME_STEP * (inverse_mass[0] * sums[t : t + 1] + pull))
    torque = [sums[3 + t : 4 + t] for t in range(3)]
    order = ((0, 1, 2), (1, 3, 4), (2, 4, 5))
    for t in range(3):
        change = sum(turning[order[t][i] : order[t][i] + 1, :] * torque[i] for i in range(3))
        rows.append(motion[3 + t, 0] + change)
    table[4] = jnp.concatenate(rows + [jnp.zeros((2, n_clump), F32)], 0)
    place.lateral(
        lambda dl: around(lambda ds, d: table_copy(ds, d, 8 - (ds + 1) * 3 - d - 1).start(), dl)
    )
    place.lateral(
        lambda dl: around(lambda ds, d: table_copy(ds, d, (ds + 1) * 3 + d + 1).wait_recv(), dl)
    )
    place.lateral(
        lambda dl: around(lambda ds, d: sums_copy(ds, d, (ds + 1) * 3 + d + 1).wait_send(), dl)
    )
    place.lateral(
        lambda dl: around(lambda ds, d: table_copy(ds, d, 8 - (ds + 1) * 3 - d - 1).wait_send(), dl)
    )


def spread_kernel(
    table,
    hot_piece,
    hot_clump,
    centre_hbm,
    off_hbm,
    clump_hbm,
    sphere_hbm,
    centre,
    off,
    clump_out,
    sphere_out,
    pose,
    sem,
):
    loads = [
        pltpu.make_async_copy(centre_hbm, centre, sem.at[0]),
        pltpu.make_async_copy(off_hbm, off, sem.at[1]),
    ]
    for load in loads:
        load.start()
    tables = jnp.concatenate([rows3(table[c]) for c in range(9)], 1)
    by_piece = lax.dot_general(tables, hot_clump[...], ROWS, preferred_element_type=F32)
    by_piece = by_piece.astype(BF16)
    by_sphere = sum3(
        lax.dot_general(by_piece, hot_piece[...], ROWS, preferred_element_type=F32)
    )
    loads[0].wait()
    for t in range(6):
        row = table[4, t : t + 1, :]
        if t < 3:
            clump_out[t, 0] = centre[t, 0] + TIME_STEP * row
        clump_out[3 + t, 0] = row
    stores = [pltpu.make_async_copy(clump_out, clump_hbm, sem.at[2])]
    stores[0].start()
    for m in range(16):
        pose[m * 8 : m * 8 + 8, :] = by_sphere[:, m * 128 : m * 128 + 128]
    loads[1].wait()
    for j in range(2):
        vx, vy, vz, sx, sy, sz = (
            pose[pl.ds(j * 64 + t, 8, stride=8), :] for t in range(6)
        )
        bx, by, bz = (off[t, 0, j] for t in range(3))
        hx, hy, hz = (0.5 * TIME_STEP * s for s in (sx, sy, sz))
        scale = 2.0 / (1.0 + (hx * hx + hy * hy + hz * hz))
        cx, cy, cz = hy * bz - hz * by, hz * bx - hx * bz, hx * by - hy * bx
        tx = bx + scale * (cx + hy * cz - hz * cy)
        ty = by + scale * (cy + hz * cx - hx * cz)
        tz = bz + scale * (cz + hx * cy - hy * cx)
        sphere_out[0, 0, j], sphere_out[1, 0, j], sphere_out[2, 0, j] = tx, ty, tz
        sphere_out[3, 0, j] = vx + (sy * tz - sz * ty)
        sphere_out[4, 0, j] = vy + (sz * tx - sx * tz)
        sphere_out[5, 0, j] = vz + (sx * ty - sy * tx)
        stores.append(
            pltpu.make_async_copy(
                sphere_out.at[:, :, pl.ds(j, 1)], sphere_hbm.at[:, :, pl.ds(j, 1)], sem.at[3 + j]
            )
        )
        stores[-1].start()
    for store in stores:
        store.wait()


def contact_call(lat_cells, blade_phase, ext, inside, tables, off, angles, inertia, **extra):
    n_clump = angles.shape[-1]
    return pl.pallas_call(
        functools.partial(contact_kernel, lat_cells),
        out_shape=(
            jax.ShapeDtypeStruct((128, 128), F32),
            jax.ShapeDtypeStruct((8, n_clump), F32),
        ),
        in_specs=[SMEM] + [VMEM] * 3 + [HBM] * 3,
        out_specs=(VMEM, VMEM),
        scratch_shapes=[
            pltpu.VMEM(off.shape, F32),
            pltpu.VMEM(angles.shape, F32),
            pltpu.VMEM(inertia.shape, F32),
            pltpu.VMEM((144, 128), jnp.int32),
            pltpu.VMEM((16, 512), jnp.int32),
            pltpu.SMEM((16, 512), jnp.int32),
            pltpu.SMEM((2, 16), jnp.int32),
            pltpu.VMEM((9, 8, 256, KEYS), F32),
            pltpu.VMEM((9 * 1024 + 8 * 72 + 256, KEYS), F32),
            pltpu.SemaphoreType.DMA((4,)),
        ],
        compiler_params=pltpu.CompilerParams(vmem_limit_bytes=24 << 20),
        name="contact",
        **extra,
    )(blade_phase, ext, inside, tables, off, angles, inertia)


def on_device(
    n_shaft,
    n_lat,
    sphere_position,
    sphere_velocity,
    sphere_radius,
    sphere_offset,
    sphere_piece,
    piece_route,
    piece_clump,
    blade_phase,
    clump_centre,
    clump_motion,
    clump_angles,
    clump_inverse_mass,
    clump_inverse_inertia,
):
    n_piece, n_clump = piece_route.shape[-1], clump_angles.shape[-1]
    sphere_position, sphere_velocity, sphere_radius, sphere_piece, piece_route, piece_clump = (
        pltpu.with_memory_space_constraint(v, pltpu.HBM)
        for v in (
            sphere_position,
            sphere_velocity,
            sphere_radius,
            sphere_piece,
            piece_route,
            piece_clump,
        )
    )
    sphere_offset, clump_centre, clump_motion = (
        pltpu.with_memory_space_constraint(v, pltpu.HBM)
        for v in (sphere_offset, clump_centre, clump_motion)
    )
    clump_angles, clump_inverse_mass, clump_inverse_inertia = (
        pltpu.with_memory_space_constraint(v, pltpu.HBM)
        for v in (clump_angles, clump_inverse_mass, clump_inverse_inertia)
    )
    ext, hot_piece, hot_clump, inside, tables = pl.pallas_call(
        functools.partial(halo_kernel, n_shaft, n_lat),
        out_shape=(
            jax.ShapeDtypeStruct((3, 4, 8, 8, 128), F32),
            jax.ShapeDtypeStruct((n_piece, 2048), BF16),
            jax.ShapeDtypeStruct((9 * n_clump, n_piece), BF16),
            jax.ShapeDtypeStruct((128, 128), F32),
            jax.ShapeDtypeStruct((16, KEYS, TERMS * 128), BF16),
        ),
        in_specs=[HBM] * 6,
        out_specs=(VMEM,) * 5,
        scratch_shapes=[
            pltpu.VMEM(sphere_piece.shape, jnp.int32),
            pltpu.VMEM(piece_route.shape, jnp.int32),
            pltpu.VMEM(piece_clump.shape, jnp.int32),
            pltpu.SemaphoreType.DMA((3, 4, 3)),
            pltpu.SemaphoreType.DMA((3, 4, 3)),
            pltpu.SemaphoreType.DMA((2, 3)),
            pltpu.SemaphoreType.DMA((3,)),
        ],
        compiler_params=pltpu.CompilerParams(
            collective_id=0, has_side_effects=True, vmem_limit_bytes=16 << 20
        ),
        name="halo",
    )(
        sphere_position,
        sphere_velocity,
        sphere_radius,
        sphere_piece,
        piece_route,
        piece_clump,
    )
    force, turning = contact_call(
        2 * n_lat,
        blade_phase,
        ext.reshape(768, 128),
        inside,
        tables,
        sphere_offset,
        clump_angles,
        clump_inverse_inertia,
    )
    table = pl.pallas_call(
        functools.partial(exchange_kernel, n_shaft, n_lat),
        out_shape=jax.ShapeDtypeStruct((9, 8, n_clump), F32),
        in_specs=[VMEM] * 4 + [HBM] * 2,
        out_specs=VMEM,
        scratch_shapes=[
            pltpu.VMEM(clump_motion.shape, F32),
            pltpu.VMEM(clump_inverse_mass.shape, F32),
            pltpu.VMEM((9, 8, n_clump), F32),
            pltpu.VMEM((9, 8, n_clump), F32),
            pltpu.SemaphoreType.DMA((2, 9)),
            pltpu.SemaphoreType.DMA((2, 9)),
            pltpu.SemaphoreType.DMA((2,)),
        ],
        compiler_params=pltpu.CompilerParams(
            collective_id=1, has_side_effects=True, vmem_limit_bytes=16 << 20
        ),
        name="exchange",
    )(force, hot_piece, hot_clump, turning, clump_motion, clump_inverse_mass)
    return pl.pallas_call(
        spread_kernel,
        out_shape=(
            jax.ShapeDtypeStruct((9, 1, 1, n_clump), F32),
            jax.ShapeDtypeStruct((6, 1, 2, 8, 128), F32),
        ),
        in_specs=[VMEM] * 3 + [HBM] * 2,
        out_specs=(HBM, HBM),
        scratch_shapes=[
            pltpu.VMEM(clump_centre.shape, F32),
            pltpu.VMEM(sphere_offset.shape, F32),
            pltpu.VMEM((9, 1, 1, n_clump), F32),
            pltpu.VMEM((6, 1, 2, 8, 128), F32),
            pltpu.VMEM((128, 128), F32),
            pltpu.SemaphoreType.DMA((5,)),
        ],
        compiler_params=pltpu.CompilerParams(vmem_limit_bytes=16 << 20),
        name="spread",
    )(table, hot_piece, hot_clump, clump_centre, sphere_offset)


def solution(mesh):
    placed = (
        P(None, "shaft", "lat", None, None),
        P(None, "shaft", "lat", None, None),
        P("shaft", "lat", None, None),
        P(None, "shaft", "lat", None, None),
        P("shaft", "lat", None),
        P("shaft", "lat", None),
        P("shaft", "lat", None),
        P(),
        P(None, "shaft", "lat", None),
        P(None, "shaft", "lat", None),
        P(None, "shaft", "lat", None),
        P("shaft", "lat", None),
        P(None, "shaft", "lat", None),
    )
    return jax.shard_map(
        functools.partial(on_device, mesh.shape["shaft"], mesh.shape["lat"]),
        mesh=mesh,
        in_specs=placed,
        out_specs=(P(None, "shaft", "lat", None), P(None, "shaft", "lat", None, None)),
        check_vma=False,
    )
```

```python
import functools
import math

import jax
import jax.numpy as jnp
from jax import lax
from jax.experimental import pallas as pl
from jax.experimental.pallas import tpu as pltpu
from jax.sharding import PartitionSpec as P

PHASES = 64
CELL_SIDE = 5.0
BLADE_STIFFNESS = 20.0
BLADE_THICKNESS = 1.0
TIME_STEP = 0.5
GRAVITY = 0.5

REACH = 0.6001
CHUNK = 64
F32 = jnp.float32
BF16 = jnp.bfloat16
MESH = pl.DeviceIdType.MESH
LANES = (((1,), (1,)), ((), ()))
ROWS = (((1,), (0,)), ((), ()))
VMEM = pl.BlockSpec(memory_space=pltpu.VMEM)
SMEM = pl.BlockSpec(memory_space=pltpu.SMEM)
HBM = pl.BlockSpec(memory_space=pltpu.HBM)


def split3(x):
    high = x.astype(BF16)
    rest = x - high.astype(F32)
    middle = rest.astype(BF16)
    low = (rest - middle.astype(F32)).astype(BF16)
    return high, middle, low


def rows3(x):
    high = x.astype(BF16).astype(F32)
    rest = x - high
    middle = rest.astype(BF16).astype(F32)
    return jnp.concatenate([high, middle, rest - middle], 0)


def sum3(x):
    return x[0:8] + x[8:16] + x[16:24]


def one_hot(rows, row):
    length = row.shape[-1]
    ids = lax.broadcasted_iota(jnp.int32, (rows, length), 0)
    return jnp.where(ids == row, 1.0, 0.0).astype(BF16)


class Place:
    def __init__(self, n_shaft, n_lat):
        self.n_shaft, self.n_lat = n_shaft, n_lat
        self.s, self.l = lax.axis_index("shaft"), lax.axis_index("lat")

    def at(self, ds, dl):
        return {"shaft": lax.rem(self.s + ds + self.n_shaft, self.n_shaft), "lat": self.l + dl}

    def lateral(self, act):
        act(0)
        pl.when(self.l > 0)(lambda: act(-1))
        pl.when(self.l < self.n_lat - 1)(lambda: act(1))

    def greet(self):
        sem = pltpu.get_barrier_semaphore()

        def signal(dl):
            for ds in (-1, 0, 1):
                if (ds, dl) != (0, 0):
                    pl.semaphore_signal(
                        sem, inc=1, device_id=self.at(ds, dl), device_id_type=MESH
                    )

        self.lateral(signal)

    def meet(self):
        sem = pltpu.get_barrier_semaphore()
        edge = jnp.logical_or(self.l == 0, self.l == self.n_lat - 1)
        pl.semaphore_wait(sem, jnp.where(edge, 5, 8))


def halo_kernel(
    n_shaft,
    n_lat,
    pos,
    vel,
    rad,
    piece_hbm,
    route_hbm,
    clump_hbm,
    ext,
    hot_piece,
    hot_clump,
    route_rows,
    inside,
    tables,
    piece,
    route,
    clump,
    send_sem,
    recv_sem,
    own_sem,
    load_sem,
):
    place = Place(n_shaft, n_lat)

    def parts(j, si, lj):
        return (
            (pos.at[:, 0, j], ext.at[si, lj, 0:3]),
            (vel.at[:, 0, j], ext.at[si, lj, 3:6]),
            (rad.at[0, pl.ds(j, 1)], ext.at[si, lj, 6:7]),
        )

    def remote(j, ds, dl, si, lj):
        return [
            pltpu.make_async_remote_copy(
                src_ref=src,
                dst_ref=dst,
                send_sem=send_sem.at[si, lj, t],
                recv_sem=recv_sem.at[si, lj, t],
                device_id=place.at(ds, dl),
                device_id_type=MESH,
            )
            for t, (src, dst) in enumerate(parts(j, si, lj))
        ]

    def outgoing(dl):
        found = []
        for ds in (-1, 0, 1):
            for j in (0, 1):
                lj = j - 2 * dl + 1
                if 0 <= lj <= 3 and (ds, dl) != (0, 0):
                    found += remote(j, ds, dl, 1 - ds, lj)
        return found

    def incoming(dl):
        found = []
        for ds in (-1, 0, 1):
            for lj in {0: (1, 2), -1: (0,), 1: (3,)}[dl]:
                if (ds, dl) != (0, 0):
                    found += remote(0, ds, dl, 1 + ds, lj)
        return found

    own = [
        pltpu.make_async_copy(src, dst, own_sem.at[j, t])
        for j in (0, 1)
        for t, (src, dst) in enumerate(parts(j, 1, 1 + j))
    ]
    own += [
        pltpu.make_async_copy(src, dst, load_sem.at[t])
        for t, (src, dst) in enumerate(
            ((piece_hbm, piece), (route_hbm, route), (clump_hbm, clump))
        )
    ]
    for c in own:
        c.start()
    place.greet()
    place.meet()
    place.lateral(lambda dl: [c.start() for c in outgoing(dl)] and None)
    ext[:, :, 7] = jnp.zeros((3, 4, 8, 128), F32)

    @pl.when(place.l == 0)
    def _():
        ext[:, 0, 0:7] = jnp.zeros((3, 7, 8, 128), F32)

    @pl.when(place.l == n_lat - 1)
    def _():
        ext[:, 3, 0:7] = jnp.zeros((3, 7, 8, 128), F32)

    for c in own:
        c.wait()
    sub = lax.broadcasted_iota(jnp.int32, (8, 128), 0)
    every = one_hot(128, lax.broadcasted_iota(jnp.int32, (1, 128), 1))
    inside[...] = jnp.zeros((128, 128), F32)

    def cell(m, _):
        j, k = m // 8, m % 8
        mine = [ext[1, 1 + j, t, pl.ds(k, 1), :] for t in range(7)]
        mine[2] = mine[2] + (CELL_SIDE * k.astype(F32) - 20.0)
        own_table(mine, sub, tables.at[m])
        value = jnp.concatenate(mine + [mine[6]], 0)
        rows = lax.dot_general(every, keyed(value, sub), LANES, preferred_element_type=F32)
        zero = jnp.zeros((8, 128), F32)
        acc = (zero, zero, zero)
        for i in range(0, 128, CHUNK):
            acc = add_pairs(rows[i : i + CHUNK], tables.at[m], acc)
        for t in range(3):
            inside[pl.ds((j * 8 + t) * 8 + k, 1), :] = jnp.sum(acc[t], 0, keepdims=True)
        return 0

    lax.fori_loop(0, 16, cell, 0)
    for m in range(16):
        hot_piece[:, m * 128 : m * 128 + 128] = one_hot(
            hot_piece.shape[0], piece[0, :, m * 128 : m * 128 + 128]
        )
    hot_clump[...] = one_hot(hot_clump.shape[0], clump[0])
    route_rows[...] = jnp.broadcast_to(route[0], route_rows.shape)
    place.lateral(lambda dl: [c.wait_recv() for c in incoming(dl)] and None)
    place.lateral(lambda dl: [c.wait_send() for c in outgoing(dl)] and None)


USUAL = {0: (128, 64, 64, 64), 1: (64, 24, 40, 24), 2: (32, 16, 24, 16)}
KEYS = 32
TERMS = 9


def kind(c):
    return (c // 3 != 1) + (c % 3 != 1)


def keyed(value, sub):
    radius = value[6:7]
    value = jnp.where(sub == 7, radius * radius * 0.0625, value)
    high = value.astype(BF16).astype(F32)
    rest = value - high
    middle = rest.astype(BF16).astype(F32)
    more = jnp.where(
        sub < 3,
        1.0,
        jnp.where(sub < 5, high[6:7], jnp.where(sub == 5, middle[6:7], 0.0)),
    )
    return jnp.concatenate([high, middle, rest - middle, more], 0).astype(BF16)


def own_table(own, sub, table):
    zero = jnp.zeros((8, 128), F32)

    def split(row):
        return [p.astype(F32) for p in split3(jnp.broadcast_to(row, (8, 128)))]

    def constants(row):
        high, middle, low = split(row)
        return jnp.where(sub == 0, high, jnp.where(sub == 1, middle, jnp.where(sub == 2, low, 0.0)))

    def put(t, same, more):
        block = jnp.concatenate([same, same, same, more], 0)
        table[:, t * 128 : t * 128 + 128] = block.astype(BF16)

    for t in range(7):
        put(t, jnp.where(sub == t, 1.0 if t == 6 else -1.0, zero), constants(own[t]))
    high, middle, low = split(4.0 * own[6])
    same = jnp.where(sub == 6, high, 0.0)
    more = jnp.where(sub == 4, low, jnp.where((sub == 3) | (sub == 5), middle, 0.0))
    put(7, same, more)
    put(
        8,
        jnp.where(sub == 7, 1.0, same * 0.03125),
        more * 0.03125 + constants(own[6] * own[6] * 0.0625),
    )


def pair_sums(pair, acc):
    dx, dy, dz, du, dv, dw, radii, product, least = pair
    square = dx * dx + dy * dy + dz * dz
    clamped = jnp.maximum(square, least)
    inverse = lax.rsqrt(clamped)
    delta = jnp.maximum(radii - clamped * inverse, 0.0)
    normal_speed = (du * dx + dv * dy + dw * dz) * inverse
    speed = du * du + dv * dv + dw * dw
    unit = square * (inverse * inverse)
    sliding = speed + normal_speed * normal_speed * (unit - 2.0)
    load = product * delta
    root = load * lax.rsqrt(jnp.maximum(load * radii, 1e-30))
    root2 = root * root
    cap = 2.5 * delta
    shear = root2 * cap * lax.rsqrt(jnp.maximum(root2 * (sliding + cap * cap), 0.0) + 1e-06)
    push = root * (cap + cap - normal_speed - 0.25)
    along = (push + shear * normal_speed) * inverse
    return (
        acc[0] + (along * dx - shear * du),
        acc[1] + (along * dy - shear * dv),
        acc[2] + (along * dz - shear * dw),
    )


def add_pairs(rows, table, acc):
    pairs = lax.dot_general(rows.astype(BF16), table[...], ROWS, preferred_element_type=F32)
    for g in range(0, CHUNK, 8):
        acc = pair_sums([pairs[g : g + 8, t * 128 : t * 128 + 128] for t in range(TERMS)], acc)
    return acc


def contact_kernel(
    lat_cells,
    phase,
    ext,
    inside,
    tables,
    off_hbm,
    angles_hbm,
    inertia_hbm,
    force,
    turning,
    off,
    angles,
    inertia,
    dest,
    count_v,
    count_s,
    bounds,
    picked,
    packed,
    copy_sem,
):
    loads = [
        pltpu.make_async_copy(src, dst, copy_sem.at[1 + t])
        for t, (src, dst) in enumerate(
            ((angles_hbm, angles), (inertia_hbm, inertia), (off_hbm, off))
        )
    ]
    for load in loads:
        load.start()
    sub = lax.broadcasted_iota(jnp.int32, (8, 128), 0)

    before = jnp.where(
        lax.broadcasted_iota(jnp.int32, (128, 128), 0)
        < lax.broadcasted_iota(jnp.int32, (128, 128), 1),
        1.0,
        0.0,
    ).astype(BF16)
    ones = jnp.ones((128, 128), BF16)
    for j in range(2):
        masks = []
        for c in range(9):
            di, dj = c // 3 - 1, c % 3 - 1
            base = ((1 + di) * 4 + 1 + j + dj) * 64
            x, y, z = (ext[base + 8 * t : base + 8 * t + 8, :] for t in range(3))
            radius = ext[base + 48 : base + 56, :]
            keep = radius > 0.0
            near = radius + REACH
            away = [v if d > 0 else CELL_SIDE - v for v, d in ((x, di), (y, dj)) if d]
            if len(away) == 1:
                keep &= away[0] < near
            if len(away) == 2:
                keep &= away[0] * away[0] + away[1] * away[1] < near * near
            low, high = z < near, CELL_SIDE - z < near
            kept = jnp.where(keep, 1.0, 0.0)
            low_f = jnp.where(low, kept, 0.0)
            high_f = jnp.where(high, kept, 0.0)
            mid_f = jnp.zeros((8, 128), F32) if c == 4 else kept - low_f - high_f
            masks += [low_f, mid_f, high_f]
        mask = jnp.concatenate(masks, 0).astype(BF16)
        prefix = lax.dot_general(mask, before, ROWS, preferred_element_type=F32)
        total = lax.dot_general(mask, ones, ROWS, preferred_element_type=F32)
        counts = lax.dot_general(ones[0:8], mask, LANES, preferred_element_type=F32)
        count_v[0:8, j * 256 : j * 256 + 216] = counts.astype(jnp.int32)
        over = jnp.full((8, 128), -1.0, F32)
        for c in range(9):
            a = c * 24
            low_p, mid_p, high_p = (prefix[a + 8 * t : a + 8 * t + 8] for t in range(3))
            low_n, mid_n, high_n = (total[a + 8 * t : a + 8 * t + 8] for t in range(3))
            spot = (
                masks[3 * c] * low_p
                + masks[3 * c + 1] * (low_n + mid_p)
                + masks[3 * c + 2] * (low_n + mid_n + high_p)
            )
            any_of = masks[3 * c] + masks[3 * c + 1] + masks[3 * c + 2]
            spot = jnp.where(any_of > 0.0, spot, -1.0).astype(jnp.int32)
            dest[(j * 9 + c) * 8 : (j * 9 + c) * 8 + 8, :] = spot
            sizes = (low_n + mid_n + high_n, low_n, mid_n, high_n)
            for size, usual in zip(sizes, USUAL[kind(c)]):
                over = jnp.maximum(over, size - usual)
        over = jnp.broadcast_to(jnp.max(over, 0, keepdims=True), (8, 128))
        count_v[8:16, j * 128 : j * 128 + 128] = over.astype(jnp.int32)
    copy = pltpu.make_async_copy(count_v, count_s, copy_sem.at[0])
    copy.start()

    angle = jnp.full((8, 128), phase[0].astype(F32) * (2.0 * math.pi / PHASES), F32)
    cos_b, sin_b = jnp.cos(angle), jnp.sin(angle)
    height_cells = 8
    centre_y, centre_z = 0.5 * CELL_SIDE * lat_cells, 0.5 * CELL_SIDE * height_cells
    reach = 0.45 * CELL_SIDE * min(lat_cells, height_cells)
    shaft_id = lax.axis_index("shaft").astype(F32)
    lat_id = (lax.axis_index("lat") * 2).astype(F32)
    up_id = sub.astype(F32)
    blade = []
    for j in range(2):
        base = (5 + j) * 64
        x, y, z = (ext[base + 8 * t : base + 8 * t + 8, :] for t in range(3))
        radius = ext[base + 48 : base + 56, :]
        x = CELL_SIDE * shaft_id + x
        y = CELL_SIDE * (lat_id + j) + y - centre_y
        z = CELL_SIDE * up_id + z - centre_z
        across = y * cos_b + z * sin_b
        radial = z * cos_b - y * sin_b
        depth = jnp.maximum(jnp.minimum(radius - across, radius + BLADE_THICKNESS + across), 0.0)
        window = jnp.maximum(radial * (reach - radial), 0.0) * (4.0 / (reach * reach))
        gate = jnp.maximum(jnp.cos(x * (2.0 * math.pi / (2.0 * CELL_SIDE))), 0.0)
        size = BLADE_STIFFNESS * depth * window * gate
        blade.append(size)

    loads[0].wait()
    loads[1].wait()
    n_clump = turning.shape[-1]
    cos_z, cos_y, cos_x = (jnp.cos(angles[t, 0]) for t in range(3))
    sin_z, sin_y, sin_x = (jnp.sin(angles[t, 0]) for t in range(3))
    rotation = [
        [
            cos_z * cos_y,
            cos_z * sin_y * sin_x - sin_z * cos_x,
            cos_z * sin_y * cos_x + sin_z * sin_x,
        ],
        [
            sin_z * cos_y,
            sin_z * sin_y * sin_x + cos_z * cos_x,
            sin_z * sin_y * cos_x - cos_z * sin_x,
        ],
        [-sin_y, cos_y * sin_x, cos_y * cos_x],
    ]
    for t, (a, b) in enumerate(((0, 0), (0, 1), (0, 2), (1, 1), (1, 2), (2, 2))):
        turning[t : t + 1, :] = TIME_STEP * sum(
            rotation[a][i] * inertia[i, 0] * rotation[b][i] for i in range(3)
        )
    turning[6:8, :] = jnp.zeros((2, n_clump), F32)
    copy.wait()

    lane = lax.broadcasted_iota(jnp.int32, (64, KEYS), 1)
    inert = jnp.where((lane >= 24) & (lane < 27), 1.0, 0.0)
    for j in range(2):

        def count(c, t, k):
            return count_s[0, j * 256 + (c * 3 + t) * 8 + k]

        def pick(c, k, rows, into):
            di, dj = c // 3 - 1, c % 3 - 1
            base = ((1 + di) * 4 + 1 + j + dj) * 64
            rise = CELL_SIDE * k.astype(F32) - 20.0
            shift = jnp.where(
                sub == 0,
                CELL_SIDE * di,
                jnp.where(sub == 1, CELL_SIDE * dj, jnp.where(sub == 2, rise, 0.0)),
            )
            value = ext[pl.ds(base + k, 8, stride=8), :] + shift
            spot = dest[pl.ds((j * 9 + c) * 8 + k, 1), :]
            into[k, 0:rows, :] = lax.dot_general(
                one_hot(rows, spot), keyed(value, sub), LANES, preferred_element_type=F32
            )

        sides = [c for c in range(9) if c != 4]

        def pick_two(i, _):
            for k in (2 * i, 2 * i + 1):
                for c in range(9):
                    pick(c, k, USUAL[kind(c)][0], picked.at[c])
            return 0

        lax.fori_loop(0, 4, pick_two, 0)

        def gather_level(k, offset, sizes):
            for t in range(3):
                start_of_part = offset
                if t == 2:
                    bounds[0, k] = offset
                for c in sides:
                    start = 0 if t == 0 else count(c, 0, k)
                    if t == 2:
                        start = start + count(c, 1, k)
                    length = sizes[kind(c)][1 + t]
                    packed[pl.ds(offset, length), :] = picked[c, k, pl.ds(start, length), :]
                    offset = offset + count(c, t, k)
                if t == 0:
                    bounds[1, k] = offset
                if t == 1:
                    packed[pl.ds(offset, 64), :] = inert
                    offset = jnp.maximum(offset, start_of_part + 64)
                    below, above = (k + 7) % 8, (k + 1) % 8
                    length = sizes[0][1]
                    start = count(4, 0, below)
                    packed[pl.ds(offset, length), :] = picked[4, below, pl.ds(start, length), :]
                    offset = offset + jnp.where(k > 0, count(4, 2, below), 0)
                    packed[pl.ds(offset, length), :] = picked[4, above, pl.ds(0, length), :]
                    offset = offset + jnp.where(k < 7, count(4, 0, above), 0)
                    packed[pl.ds(offset, 8), :] = inert[0:8]
                    offset = (offset + 7) // 8 * 8
            return offset

        def gather_usual():
            offset = 0
            for k in range(8):
                offset = gather_level(k, offset, USUAL)
            return offset

        def gather_any():
            def level(k, offset):
                for c in sides:
                    pick(c, k, 128, picked.at[c])
                return gather_level(k, offset, {t: (128,) * 4 for t in range(3)})

            return lax.fori_loop(0, 8, level, jnp.int32(0))

        end = lax.cond(count_s[8, j * 128] > 0, gather_any, gather_usual)
        packed[pl.ds(end, 64), :] = inert
        bounds[1, 8] = end

        def cell(k, _):
            first = jnp.where(k == 0, 0, bounds[0, jnp.maximum(k - 1, 0)])
            last = bounds[1, k + 1]
            table = tables.at[j * 8 + k]

            def chunk(i, acc):
                at = pl.multiple_of(first + i * CHUNK, 8)
                return add_pairs(packed[pl.ds(at, CHUNK), :], table, acc)

            zero = jnp.zeros((8, 128), F32)
            sums = lax.fori_loop(0, (last - first + CHUNK - 1) // CHUNK, chunk, (zero, zero, zero))
            for t in range(3):
                force[pl.ds((j * 8 + t) * 8 + k, 1), :] = jnp.sum(sums[t], 0, keepdims=True)
            return 0

        lax.fori_loop(0, 8, cell, 0)

    loads[2].wait()
    for j in range(2):
        fx, fy, fz = (
            force[(j * 8 + t) * 8 : (j * 8 + t) * 8 + 8, :]
            + inside[(j * 8 + t) * 8 : (j * 8 + t) * 8 + 8, :]
            for t in range(3)
        )
        fy, fz = fy + blade[j] * cos_b, fz + blade[j] * sin_b
        ox, oy, oz = (off[t, 0, j] for t in range(3))
        six = [fx, fy, fz, oy * fz - oz * fy, oz * fx - ox * fz, ox * fy - oy * fx]
        for t in range(8):
            force[(j * 8 + t) * 8 : (j * 8 + t) * 8 + 8, :] = (
                six[t] if t < 6 else jnp.zeros((8, 128), F32)
            )


def exchange_kernel(
    n_shaft,
    n_lat,
    force,
    hot_piece,
    hot_clump,
    route_rows,
    turning,
    motion_hbm,
    inverse_mass_hbm,
    table,
    motion,
    inverse_mass,
    part,
    got,
    send_sem,
    recv_sem,
    load_sem,
):
    place = Place(n_shaft, n_lat)
    n_clump = turning.shape[-1]
    place.greet()
    loads = [
        pltpu.make_async_copy(motion_hbm, motion, load_sem.at[0]),
        pltpu.make_async_copy(inverse_mass_hbm, inverse_mass, load_sem.at[1]),
    ]
    for load in loads:
        load.start()

    def sums_copy(ds, dl, slot):
        c = (ds + 1) * 3 + dl + 1
        return pltpu.make_async_remote_copy(
            src_ref=part.at[c],
            dst_ref=got.at[slot],
            send_sem=send_sem.at[0, slot],
            recv_sem=recv_sem.at[0, slot],
            device_id=place.at(ds, dl),
            device_id_type=MESH,
        )

    def table_copy(ds, dl, slot):
        return pltpu.make_async_remote_copy(
            src_ref=table.at[4],
            dst_ref=table.at[slot],
            send_sem=send_sem.at[1, slot],
            recv_sem=recv_sem.at[1, slot],
            device_id=place.at(ds, dl),
            device_id_type=MESH,
        )

    def around(act, dl):
        for ds in (-1, 0, 1):
            if (ds, dl) != (0, 0):
                act(ds, dl)

    terms = [
        rows3(force[pl.ds(j * 64 + k, 8, stride=8), :]).astype(BF16) for j in range(2) for k in range(8)
    ]
    sums = lax.dot_general(
        jnp.concatenate(terms, 1), hot_piece[...], LANES, preferred_element_type=F32
    )
    sums = rows3(sum3(sums))
    route = jnp.concatenate([route_rows[...]] * 3, 0)
    routed = jnp.concatenate([jnp.where(route == c, sums, 0.0) for c in range(9)], 0)
    sums = lax.dot_general(
        routed.astype(BF16), hot_clump[...], LANES, preferred_element_type=F32
    )
    for c in range(9):
        part[c] = sum3(sums[24 * c : 24 * c + 24])

    def clear(edge, column):
        @pl.when(place.l == edge)
        def _():
            for row in range(3):
                table[row * 3 + column] = jnp.zeros((8, n_clump), F32)
                got[row * 3 + 2 - column] = jnp.zeros((8, n_clump), F32)

    clear(0, 0)
    clear(n_lat - 1, 2)
    place.meet()
    place.lateral(
        lambda dl: around(lambda ds, d: sums_copy(ds, d, (ds + 1) * 3 + d + 1).start(), dl)
    )
    for load in loads:
        load.wait()
    place.lateral(
        lambda dl: around(lambda ds, d: sums_copy(ds, d, 8 - (ds + 1) * 3 - d - 1).wait_recv(), dl)
    )
    sums = part[4]
    for c in range(9):
        if c != 4:
            sums = sums + got[c]
    rows = []
    for t in range(3):
        pull = -GRAVITY if t == 2 else 0.0
        rows.append(motion[t, 0] + TIME_STEP * (inverse_mass[0] * sums[t : t + 1] + pull))
    torque = [sums[3 + t : 4 + t] for t in range(3)]
    order = ((0, 1, 2), (1, 3, 4), (2, 4, 5))
    for t in range(3):
        change = sum(turning[order[t][i] : order[t][i] + 1, :] * torque[i] for i in range(3))
        rows.append(motion[3 + t, 0] + change)
    table[4] = jnp.concatenate(rows + [jnp.zeros((2, n_clump), F32)], 0)
    place.lateral(
        lambda dl: around(lambda ds, d: table_copy(ds, d, 8 - (ds + 1) * 3 - d - 1).start(), dl)
    )
    place.lateral(
        lambda dl: around(lambda ds, d: table_copy(ds, d, (ds + 1) * 3 + d + 1).wait_recv(), dl)
    )
    place.lateral(
        lambda dl: around(lambda ds, d: sums_copy(ds, d, (ds + 1) * 3 + d + 1).wait_send(), dl)
    )
    place.lateral(
        lambda dl: around(lambda ds, d: table_copy(ds, d, 8 - (ds + 1) * 3 - d - 1).wait_send(), dl)
    )


def spread_kernel(
    table,
    hot_piece,
    hot_clump,
    route_rows,
    centre_hbm,
    off_hbm,
    clump_hbm,
    sphere_hbm,
    centre,
    off,
    clump_out,
    sphere_out,
    pose,
    sem,
):
    loads = [
        pltpu.make_async_copy(centre_hbm, centre, sem.at[0]),
        pltpu.make_async_copy(off_hbm, off, sem.at[1]),
    ]
    for load in loads:
        load.start()
    tables = jnp.concatenate([rows3(table[c]) for c in range(9)], 0).astype(BF16)
    found = lax.dot_general(tables, hot_clump[...], ROWS, preferred_element_type=F32)
    route = jnp.concatenate([route_rows[...]] * 3, 0)
    by_piece = found[0:24]
    for c in range(1, 9):
        by_piece = jnp.where(route == c, found[24 * c : 24 * c + 24], by_piece)
    by_sphere = sum3(
        lax.dot_general(by_piece.astype(BF16), hot_piece[...], ROWS, preferred_element_type=F32)
    )
    loads[0].wait()
    for t in range(6):
        row = table[4, t : t + 1, :]
        if t < 3:
            clump_out[t, 0] = centre[t, 0] + TIME_STEP * row
        clump_out[3 + t, 0] = row
    stores = [pltpu.make_async_copy(clump_out, clump_hbm, sem.at[2])]
    stores[0].start()
    for m in range(16):
        pose[m * 8 : m * 8 + 8, :] = by_sphere[:, m * 128 : m * 128 + 128]
    loads[1].wait()
    for j in range(2):
        vx, vy, vz, sx, sy, sz = (
            pose[pl.ds(j * 64 + t, 8, stride=8), :] for t in range(6)
        )
        bx, by, bz = (off[t, 0, j] for t in range(3))
        hx, hy, hz = (0.5 * TIME_STEP * s for s in (sx, sy, sz))
        scale = 2.0 / (1.0 + (hx * hx + hy * hy + hz * hz))
        cx, cy, cz = hy * bz - hz * by, hz * bx - hx * bz, hx * by - hy * bx
        tx = bx + scale * (cx + hy * cz - hz * cy)
        ty = by + scale * (cy + hz * cx - hx * cz)
        tz = bz + scale * (cz + hx * cy - hy * cx)
        sphere_out[0, 0, j], sphere_out[1, 0, j], sphere_out[2, 0, j] = tx, ty, tz
        sphere_out[3, 0, j] = vx + (sy * tz - sz * ty)
        sphere_out[4, 0, j] = vy + (sz * tx - sx * tz)
        sphere_out[5, 0, j] = vz + (sx * ty - sy * tx)
        stores.append(
            pltpu.make_async_copy(
                sphere_out.at[:, :, pl.ds(j, 1)], sphere_hbm.at[:, :, pl.ds(j, 1)], sem.at[3 + j]
            )
        )
        stores[-1].start()
    for store in stores:
        store.wait()


def contact_call(lat_cells, blade_phase, ext, inside, tables, off, angles, inertia, **extra):
    n_clump = angles.shape[-1]
    return pl.pallas_call(
        functools.partial(contact_kernel, lat_cells),
        out_shape=(
            jax.ShapeDtypeStruct((128, 128), F32),
            jax.ShapeDtypeStruct((8, n_clump), F32),
        ),
        in_specs=[SMEM] + [VMEM] * 3 + [HBM] * 3,
        out_specs=(VMEM, VMEM),
        scratch_shapes=[
            pltpu.VMEM(off.shape, F32),
            pltpu.VMEM(angles.shape, F32),
            pltpu.VMEM(inertia.shape, F32),
            pltpu.VMEM((144, 128), jnp.int32),
            pltpu.VMEM((16, 512), jnp.int32),
            pltpu.SMEM((16, 512), jnp.int32),
            pltpu.SMEM((2, 16), jnp.int32),
            pltpu.VMEM((9, 8, 256, KEYS), F32),
            pltpu.VMEM((9 * 1024 + 8 * 72 + 256, KEYS), F32),
            pltpu.SemaphoreType.DMA((4,)),
        ],
        compiler_params=pltpu.CompilerParams(vmem_limit_bytes=24 << 20),
        name="contact",
        **extra,
    )(blade_phase, ext, inside, tables, off, angles, inertia)


def on_device(
    n_shaft,
    n_lat,
    sphere_position,
    sphere_velocity,
    sphere_radius,
    sphere_offset,
    sphere_piece,
    piece_route,
    piece_clump,
    blade_phase,
    clump_centre,
    clump_motion,
    clump_angles,
    clump_inverse_mass,
    clump_inverse_inertia,
):
    n_piece, n_clump = piece_route.shape[-1], clump_angles.shape[-1]
    sphere_position, sphere_velocity, sphere_radius, sphere_piece, piece_route, piece_clump = (
        pltpu.with_memory_space_constraint(v, pltpu.HBM)
        for v in (
            sphere_position,
            sphere_velocity,
            sphere_radius,
            sphere_piece,
            piece_route,
            piece_clump,
        )
    )
    sphere_offset, clump_centre, clump_motion = (
        pltpu.with_memory_space_constraint(v, pltpu.HBM)
        for v in (sphere_offset, clump_centre, clump_motion)
    )
    clump_angles, clump_inverse_mass, clump_inverse_inertia = (
        pltpu.with_memory_space_constraint(v, pltpu.HBM)
        for v in (clump_angles, clump_inverse_mass, clump_inverse_inertia)
    )
    ext, hot_piece, hot_clump, route_rows, inside, tables = pl.pallas_call(
        functools.partial(halo_kernel, n_shaft, n_lat),
        out_shape=(
            jax.ShapeDtypeStruct((3, 4, 8, 8, 128), F32),
            jax.ShapeDtypeStruct((n_piece, 2048), BF16),
            jax.ShapeDtypeStruct((n_clump, n_piece), BF16),
            jax.ShapeDtypeStruct((8, n_piece), jnp.int32),
            jax.ShapeDtypeStruct((128, 128), F32),
            jax.ShapeDtypeStruct((16, KEYS, TERMS * 128), BF16),
        ),
        in_specs=[HBM] * 6,
        out_specs=(VMEM,) * 6,
        scratch_shapes=[
            pltpu.VMEM(sphere_piece.shape, jnp.int32),
            pltpu.VMEM(piece_route.shape, jnp.int32),
            pltpu.VMEM(piece_clump.shape, jnp.int32),
            pltpu.SemaphoreType.DMA((3, 4, 3)),
            pltpu.SemaphoreType.DMA((3, 4, 3)),
            pltpu.SemaphoreType.DMA((2, 3)),
            pltpu.SemaphoreType.DMA((3,)),
        ],
        compiler_params=pltpu.CompilerParams(
            collective_id=0, has_side_effects=True, vmem_limit_bytes=16 << 20
        ),
        name="halo",
    )(
        sphere_position,
        sphere_velocity,
        sphere_radius,
        sphere_piece,
        piece_route,
        piece_clump,
    )
    force, turning = contact_call(
        2 * n_lat,
        blade_phase,
        ext.reshape(768, 128),
        inside,
        tables,
        sphere_offset,
        clump_angles,
        clump_inverse_inertia,
    )
    table = pl.pallas_call(
        functools.partial(exchange_kernel, n_shaft, n_lat),
        out_shape=jax.ShapeDtypeStruct((9, 8, n_clump), F32),
        in_specs=[VMEM] * 5 + [HBM] * 2,
        out_specs=VMEM,
        scratch_shapes=[
            pltpu.VMEM(clump_motion.shape, F32),
            pltpu.VMEM(clump_inverse_mass.shape, F32),
            pltpu.VMEM((9, 8, n_clump), F32),
            pltpu.VMEM((9, 8, n_clump), F32),
            pltpu.SemaphoreType.DMA((2, 9)),
            pltpu.SemaphoreType.DMA((2, 9)),
            pltpu.SemaphoreType.DMA((2,)),
        ],
        compiler_params=pltpu.CompilerParams(
            collective_id=1, has_side_effects=True, vmem_limit_bytes=16 << 20
        ),
        name="exchange",
    )(force, hot_piece, hot_clump, route_rows, turning, clump_motion, clump_inverse_mass)
    return pl.pallas_call(
        spread_kernel,
        out_shape=(
            jax.ShapeDtypeStruct((9, 1, 1, n_clump), F32),
            jax.ShapeDtypeStruct((6, 1, 2, 8, 128), F32),
        ),
        in_specs=[VMEM] * 4 + [HBM] * 2,
        out_specs=(HBM, HBM),
        scratch_shapes=[
            pltpu.VMEM(clump_centre.shape, F32),
            pltpu.VMEM(sphere_offset.shape, F32),
            pltpu.VMEM((9, 1, 1, n_clump), F32),
            pltpu.VMEM((6, 1, 2, 8, 128), F32),
            pltpu.VMEM((128, 128), F32),
            pltpu.SemaphoreType.DMA((5,)),
        ],
        compiler_params=pltpu.CompilerParams(vmem_limit_bytes=16 << 20),
        name="spread",
    )(table, hot_piece, hot_clump, route_rows, clump_centre, sphere_offset)


def solution(mesh):
    placed = (
        P(None, "shaft", "lat", None, None),
        P(None, "shaft", "lat", None, None),
        P("shaft", "lat", None, None),
        P(None, "shaft", "lat", None, None),
        P("shaft", "lat", None),
        P("shaft", "lat", None),
        P("shaft", "lat", None),
        P(),
        P(None, "shaft", "lat", None),
        P(None, "shaft", "lat", None),
        P(None, "shaft", "lat", None),
        P("shaft", "lat", None),
        P(None, "shaft", "lat", None),
    )
    return jax.shard_map(
        functools.partial(on_device, mesh.shape["shaft"], mesh.shape["lat"]),
        mesh=mesh,
        in_specs=placed,
        out_specs=(P(None, "shaft", "lat", None), P(None, "shaft", "lat", None, None)),
        check_vma=False,
    )
```

```python
import functools
import math

import jax
import jax.numpy as jnp
from jax import lax
from jax.experimental import pallas as pl
from jax.experimental.pallas import tpu as pltpu
from jax.sharding import PartitionSpec as P

PHASES = 64
CELL_SIDE = 5.0
BLADE_STIFFNESS = 20.0
BLADE_THICKNESS = 1.0
TIME_STEP = 0.5
GRAVITY = 0.5

REACH = 0.6001
CHUNK = 64
F32 = jnp.float32
BF16 = jnp.bfloat16
MESH = pl.DeviceIdType.MESH
LANES = (((1,), (1,)), ((), ()))
ROWS = (((1,), (0,)), ((), ()))
VMEM = pl.BlockSpec(memory_space=pltpu.VMEM)
SMEM = pl.BlockSpec(memory_space=pltpu.SMEM)
HBM = pl.BlockSpec(memory_space=pltpu.HBM)


def split3(x):
    high = x.astype(BF16)
    rest = x - high.astype(F32)
    middle = rest.astype(BF16)
    low = (rest - middle.astype(F32)).astype(BF16)
    return high, middle, low


def rows3(x):
    high = x.astype(BF16).astype(F32)
    rest = x - high
    middle = rest.astype(BF16).astype(F32)
    return jnp.concatenate([high, middle, rest - middle], 0)


def sum3(x):
    return x[0:8] + x[8:16] + x[16:24]


def one_hot(rows, row):
    length = row.shape[-1]
    ids = lax.broadcasted_iota(jnp.int32, (rows, length), 0)
    return jnp.where(ids == row, 1.0, 0.0).astype(BF16)


class Place:
    def __init__(self, n_shaft, n_lat):
        self.n_shaft, self.n_lat = n_shaft, n_lat
        self.s, self.l = lax.axis_index("shaft"), lax.axis_index("lat")

    def at(self, ds, dl):
        return {"shaft": lax.rem(self.s + ds + self.n_shaft, self.n_shaft), "lat": self.l + dl}

    def lateral(self, act):
        act(0)
        pl.when(self.l > 0)(lambda: act(-1))
        pl.when(self.l < self.n_lat - 1)(lambda: act(1))

    def greet(self):
        sem = pltpu.get_barrier_semaphore()

        def signal(dl):
            for ds in (-1, 0, 1):
                if (ds, dl) != (0, 0):
                    pl.semaphore_signal(
                        sem, inc=1, device_id=self.at(ds, dl), device_id_type=MESH
                    )

        self.lateral(signal)

    def meet(self):
        sem = pltpu.get_barrier_semaphore()
        edge = jnp.logical_or(self.l == 0, self.l == self.n_lat - 1)
        pl.semaphore_wait(sem, jnp.where(edge, 5, 8))


def halo_kernel(
    n_shaft,
    n_lat,
    pos,
    vel,
    rad,
    piece_hbm,
    route_hbm,
    clump_hbm,
    ext,
    hot_piece,
    hot_clump,
    route_rows,
    inside,
    tables,
    piece,
    route,
    clump,
    send_sem,
    recv_sem,
    own_sem,
    load_sem,
):
    place = Place(n_shaft, n_lat)

    def parts(j, si, lj):
        return (
            (pos.at[:, 0, j], ext.at[si, lj, 0:3]),
            (vel.at[:, 0, j], ext.at[si, lj, 3:6]),
            (rad.at[0, pl.ds(j, 1)], ext.at[si, lj, 6:7]),
        )

    def remote(j, ds, dl, si, lj):
        return [
            pltpu.make_async_remote_copy(
                src_ref=src,
                dst_ref=dst,
                send_sem=send_sem.at[si, lj, t],
                recv_sem=recv_sem.at[si, lj, t],
                device_id=place.at(ds, dl),
                device_id_type=MESH,
            )
            for t, (src, dst) in enumerate(parts(j, si, lj))
        ]

    def outgoing(dl):
        found = []
        for ds in (-1, 0, 1):
            for j in (0, 1):
                lj = j - 2 * dl + 1
                if 0 <= lj <= 3 and (ds, dl) != (0, 0):
                    found += remote(j, ds, dl, 1 - ds, lj)
        return found

    def incoming(dl):
        found = []
        for ds in (-1, 0, 1):
            for lj in {0: (1, 2), -1: (0,), 1: (3,)}[dl]:
                if (ds, dl) != (0, 0):
                    found += remote(0, ds, dl, 1 + ds, lj)
        return found

    own = [
        pltpu.make_async_copy(src, dst, own_sem.at[j, t])
        for j in (0, 1)
        for t, (src, dst) in enumerate(parts(j, 1, 1 + j))
    ]
    own += [
        pltpu.make_async_copy(src, dst, load_sem.at[t])
        for t, (src, dst) in enumerate(
            ((piece_hbm, piece), (route_hbm, route), (clump_hbm, clump))
        )
    ]
    for c in own:
        c.start()
    place.greet()
    place.meet()
    place.lateral(lambda dl: [c.start() for c in outgoing(dl)] and None)
    ext[:, :, 7] = jnp.zeros((3, 4, 8, 128), F32)

    @pl.when(place.l == 0)
    def _():
        ext[:, 0, 0:7] = jnp.zeros((3, 7, 8, 128), F32)

    @pl.when(place.l == n_lat - 1)
    def _():
        ext[:, 3, 0:7] = jnp.zeros((3, 7, 8, 128), F32)

    for c in own:
        c.wait()
    sub = lax.broadcasted_iota(jnp.int32, (8, 128), 0)
    every = one_hot(128, lax.broadcasted_iota(jnp.int32, (1, 128), 1))
    inside[...] = jnp.zeros((128, 128), F32)

    def cell(m):
        j, k = m // 8, m % 8
        mine = [ext[1, 1 + j, t, pl.ds(k, 1), :] for t in range(7)]
        mine[2] = mine[2] + (CELL_SIDE * k.astype(F32) - 20.0)
        own_table(mine, sub, tables.at[m])
        value = jnp.concatenate(mine + [mine[6]], 0)
        rows = lax.dot_general(every, keyed(value, sub), LANES, preferred_element_type=F32)
        zero = jnp.zeros((8, 128), F32)
        acc = (zero, zero, zero)
        for i in range(0, 128, CHUNK):
            acc = add_pairs(rows[i : i + CHUNK], tables.at[m], acc)
        for t in range(3):
            inside[pl.ds((j * 8 + t) * 8 + k, 1), :] = jnp.sum(acc[t], 0, keepdims=True)

    def cells(i, _):
        cell(2 * i)
        cell(2 * i + 1)
        return 0

    lax.fori_loop(0, 8, cells, 0)
    for m in range(16):
        hot_piece[:, m * 128 : m * 128 + 128] = one_hot(
            hot_piece.shape[0], piece[0, :, m * 128 : m * 128 + 128]
        )
    hot_clump[...] = one_hot(hot_clump.shape[0], clump[0])
    route_rows[...] = jnp.broadcast_to(route[0], route_rows.shape)
    place.lateral(lambda dl: [c.wait_recv() for c in incoming(dl)] and None)
    place.lateral(lambda dl: [c.wait_send() for c in outgoing(dl)] and None)


USUAL = {0: (128, 64, 64, 64), 1: (64, 24, 40, 24), 2: (32, 16, 24, 16)}
KEYS = 32
TERMS = 9


def kind(c):
    return (c // 3 != 1) + (c % 3 != 1)


def keyed(value, sub):
    radius = value[6:7]
    value = jnp.where(sub == 7, radius * radius * 0.0625, value)
    high = value.astype(BF16).astype(F32)
    rest = value - high
    middle = rest.astype(BF16).astype(F32)
    more = jnp.where(
        sub < 3,
        1.0,
        jnp.where(sub < 5, high[6:7], jnp.where(sub == 5, middle[6:7], 0.0)),
    )
    return jnp.concatenate([high, middle, rest - middle, more], 0).astype(BF16)


def own_table(own, sub, table):
    zero = jnp.zeros((8, 128), F32)

    def split(row):
        return [p.astype(F32) for p in split3(jnp.broadcast_to(row, (8, 128)))]

    def constants(row):
        high, middle, low = split(row)
        return jnp.where(sub == 0, high, jnp.where(sub == 1, middle, jnp.where(sub == 2, low, 0.0)))

    def put(t, same, more):
        block = jnp.concatenate([same, same, same, more], 0)
        table[:, t * 128 : t * 128 + 128] = block.astype(BF16)

    for t in range(7):
        put(t, jnp.where(sub == t, 1.0 if t == 6 else -1.0, zero), constants(own[t]))
    high, middle, low = split(4.0 * own[6])
    same = jnp.where(sub == 6, high, 0.0)
    more = jnp.where(sub == 4, low, jnp.where((sub == 3) | (sub == 5), middle, 0.0))
    put(7, same, more)
    put(
        8,
        jnp.where(sub == 7, 1.0, same * 0.03125),
        more * 0.03125 + constants(own[6] * own[6] * 0.0625),
    )


def pair_sums(pair, acc):
    dx, dy, dz, du, dv, dw, radii, product, least = pair
    square = dx * dx + dy * dy + dz * dz
    clamped = jnp.maximum(square, least)
    inverse = lax.rsqrt(clamped)
    delta = jnp.maximum(radii - clamped * inverse, 0.0)
    normal_speed = (du * dx + dv * dy + dw * dz) * inverse
    speed = du * du + dv * dv + dw * dw
    unit = square * (inverse * inverse)
    sliding = speed + normal_speed * normal_speed * (unit - 2.0)
    load = product * delta
    root = load * lax.rsqrt(jnp.maximum(load * radii, 1e-30))
    root2 = root * root
    cap = 2.5 * delta
    shear = root2 * cap * lax.rsqrt(jnp.maximum(root2 * (sliding + cap * cap), 0.0) + 1e-06)
    push = root * (cap + cap - normal_speed - 0.25)
    along = (push + shear * normal_speed) * inverse
    return (
        acc[0] + (along * dx - shear * du),
        acc[1] + (along * dy - shear * dv),
        acc[2] + (along * dz - shear * dw),
    )


def add_pairs(rows, table, acc):
    pairs = lax.dot_general(rows.astype(BF16), table[...], ROWS, preferred_element_type=F32)
    for g in range(0, CHUNK, 8):
        acc = pair_sums([pairs[g : g + 8, t * 128 : t * 128 + 128] for t in range(TERMS)], acc)
    return acc


def contact_kernel(
    lat_cells,
    phase,
    ext,
    inside,
    tables,
    off_hbm,
    angles_hbm,
    inertia_hbm,
    force,
    turning,
    off,
    angles,
    inertia,
    dest,
    count_v,
    count_s,
    bounds,
    picked,
    packed,
    copy_sem,
):
    loads = [
        pltpu.make_async_copy(src, dst, copy_sem.at[1 + t])
        for t, (src, dst) in enumerate(
            ((angles_hbm, angles), (inertia_hbm, inertia), (off_hbm, off))
        )
    ]
    for load in loads:
        load.start()
    sub = lax.broadcasted_iota(jnp.int32, (8, 128), 0)

    before = jnp.where(
        lax.broadcasted_iota(jnp.int32, (128, 128), 0)
        < lax.broadcasted_iota(jnp.int32, (128, 128), 1),
        1.0,
        0.0,
    ).astype(BF16)
    ones = jnp.ones((128, 128), BF16)
    for j in range(2):
        masks = []
        for c in range(9):
            di, dj = c // 3 - 1, c % 3 - 1
            base = ((1 + di) * 4 + 1 + j + dj) * 64
            x, y, z = (ext[base + 8 * t : base + 8 * t + 8, :] for t in range(3))
            radius = ext[base + 48 : base + 56, :]
            keep = radius > 0.0
            near = radius + REACH
            away = [v if d > 0 else CELL_SIDE - v for v, d in ((x, di), (y, dj)) if d]
            if len(away) == 1:
                keep &= away[0] < near
            if len(away) == 2:
                keep &= away[0] * away[0] + away[1] * away[1] < near * near
            low, high = z < near, CELL_SIDE - z < near
            kept = jnp.where(keep, 1.0, 0.0)
            low_f = jnp.where(low, kept, 0.0)
            high_f = jnp.where(high, kept, 0.0)
            mid_f = jnp.zeros((8, 128), F32) if c == 4 else kept - low_f - high_f
            masks += [low_f, mid_f, high_f]
        mask = jnp.concatenate(masks, 0).astype(BF16)
        prefix = lax.dot_general(mask, before, ROWS, preferred_element_type=F32)
        total = lax.dot_general(mask, ones, ROWS, preferred_element_type=F32)
        counts = lax.dot_general(ones[0:8], mask, LANES, preferred_element_type=F32)
        count_v[0:8, j * 256 : j * 256 + 216] = counts.astype(jnp.int32)
        over = jnp.full((8, 128), -1.0, F32)
        for c in range(9):
            a = c * 24
            low_p, mid_p, high_p = (prefix[a + 8 * t : a + 8 * t + 8] for t in range(3))
            low_n, mid_n, high_n = (total[a + 8 * t : a + 8 * t + 8] for t in range(3))
            spot = (
                masks[3 * c] * low_p
                + masks[3 * c + 1] * (low_n + mid_p)
                + masks[3 * c + 2] * (low_n + mid_n + high_p)
            )
            any_of = masks[3 * c] + masks[3 * c + 1] + masks[3 * c + 2]
            spot = jnp.where(any_of > 0.0, spot, -1.0).astype(jnp.int32)
            dest[(j * 9 + c) * 8 : (j * 9 + c) * 8 + 8, :] = spot
            sizes = (low_n + mid_n + high_n, low_n, mid_n, high_n)
            for size, usual in zip(sizes, USUAL[kind(c)]):
                over = jnp.maximum(over, size - usual)
        over = jnp.broadcast_to(jnp.max(over, 0, keepdims=True), (8, 128))
        count_v[8:16, j * 128 : j * 128 + 128] = over.astype(jnp.int32)
    copy = pltpu.make_async_copy(count_v, count_s, copy_sem.at[0])
    copy.start()

    angle = jnp.full((8, 128), phase[0].astype(F32) * (2.0 * math.pi / PHASES), F32)
    cos_b, sin_b = jnp.cos(angle), jnp.sin(angle)
    height_cells = 8
    centre_y, centre_z = 0.5 * CELL_SIDE * lat_cells, 0.5 * CELL_SIDE * height_cells
    reach = 0.45 * CELL_SIDE * min(lat_cells, height_cells)
    shaft_id = lax.axis_index("shaft").astype(F32)
    lat_id = (lax.axis_index("lat") * 2).astype(F32)
    up_id = sub.astype(F32)
    blade = []
    for j in range(2):
        base = (5 + j) * 64
        x, y, z = (ext[base + 8 * t : base + 8 * t + 8, :] for t in range(3))
        radius = ext[base + 48 : base + 56, :]
        x = CELL_SIDE * shaft_id + x
        y = CELL_SIDE * (lat_id + j) + y - centre_y
        z = CELL_SIDE * up_id + z - centre_z
        across = y * cos_b + z * sin_b
        radial = z * cos_b - y * sin_b
        depth = jnp.maximum(jnp.minimum(radius - across, radius + BLADE_THICKNESS + across), 0.0)
        window = jnp.maximum(radial * (reach - radial), 0.0) * (4.0 / (reach * reach))
        gate = jnp.maximum(jnp.cos(x * (2.0 * math.pi / (2.0 * CELL_SIDE))), 0.0)
        size = BLADE_STIFFNESS * depth * window * gate
        blade.append(size)

    loads[0].wait()
    loads[1].wait()
    n_clump = turning.shape[-1]
    cos_z, cos_y, cos_x = (jnp.cos(angles[t, 0]) for t in range(3))
    sin_z, sin_y, sin_x = (jnp.sin(angles[t, 0]) for t in range(3))
    rotation = [
        [
            cos_z * cos_y,
            cos_z * sin_y * sin_x - sin_z * cos_x,
            cos_z * sin_y * cos_x + sin_z * sin_x,
        ],
        [
            sin_z * cos_y,
            sin_z * sin_y * sin_x + cos_z * cos_x,
            sin_z * sin_y * cos_x - cos_z * sin_x,
        ],
        [-sin_y, cos_y * sin_x, cos_y * cos_x],
    ]
    for t, (a, b) in enumerate(((0, 0), (0, 1), (0, 2), (1, 1), (1, 2), (2, 2))):
        turning[t : t + 1, :] = TIME_STEP * sum(
            rotation[a][i] * inertia[i, 0] * rotation[b][i] for i in range(3)
        )
    turning[6:8, :] = jnp.zeros((2, n_clump), F32)
    copy.wait()

    lane = lax.broadcasted_iota(jnp.int32, (64, 128), 1)
    inert = jnp.where((lane >= 24) & (lane < 27), 1.0, 0.0)
    for j in range(2):

        def count(c, t, k):
            return count_s[0, j * 256 + (c * 3 + t) * 8 + k]

        def pick(c, k, rows, into):
            di, dj = c // 3 - 1, c % 3 - 1
            base = ((1 + di) * 4 + 1 + j + dj) * 64
            rise = CELL_SIDE * k.astype(F32) - 20.0
            shift = jnp.where(
                sub == 0,
                CELL_SIDE * di,
                jnp.where(sub == 1, CELL_SIDE * dj, jnp.where(sub == 2, rise, 0.0)),
            )
            value = ext[pl.ds(base + k, 8, stride=8), :] + shift
            spot = dest[pl.ds((j * 9 + c) * 8 + k, 1), :]
            keys = jnp.concatenate([keyed(value, sub), jnp.zeros((128 - KEYS, 128), BF16)], 0)
            into[k, 0:rows, :] = lax.dot_general(
                one_hot(rows, spot), keys, LANES, preferred_element_type=F32
            )

        sides = [c for c in range(9) if c != 4]

        def pick_some(i, _):
            for k in (4 * i, 4 * i + 1, 4 * i + 2, 4 * i + 3):
                for c in range(9):
                    pick(c, k, USUAL[kind(c)][0], picked.at[c])
            return 0

        lax.fori_loop(0, 2, pick_some, 0)

        def gather_level(k, offset, sizes):
            for t in range(3):
                start_of_part = offset
                if t == 2:
                    bounds[0, k] = offset
                for c in sides:
                    start = 0 if t == 0 else count(c, 0, k)
                    if t == 2:
                        start = start + count(c, 1, k)
                    length = sizes[kind(c)][1 + t]
                    packed[pl.ds(offset, length), :] = picked[c, k, pl.ds(start, length), :]
                    offset = offset + count(c, t, k)
                if t == 0:
                    bounds[1, k] = offset
                if t == 1:
                    packed[pl.ds(offset, 64), :] = inert
                    offset = jnp.maximum(offset, start_of_part + 64)
                    below, above = (k + 7) % 8, (k + 1) % 8
                    length = sizes[0][1]
                    start = count(4, 0, below)
                    packed[pl.ds(offset, length), :] = picked[4, below, pl.ds(start, length), :]
                    offset = offset + jnp.where(k > 0, count(4, 2, below), 0)
                    packed[pl.ds(offset, length), :] = picked[4, above, pl.ds(0, length), :]
                    offset = offset + jnp.where(k < 7, count(4, 0, above), 0)
                    packed[pl.ds(offset, 8), :] = inert[0:8]
                    offset = (offset + 7) // 8 * 8
            return offset

        def gather_usual():
            offset = 0
            for k in range(8):
                offset = gather_level(k, offset, USUAL)
            return offset

        def gather_any():
            def level(k, offset):
                for c in sides:
                    pick(c, k, 128, picked.at[c])
                return gather_level(k, offset, {t: (128,) * 4 for t in range(3)})

            return lax.fori_loop(0, 8, level, jnp.int32(0))

        end = lax.cond(count_s[8, j * 128] > 0, gather_any, gather_usual)
        packed[pl.ds(end, 64), :] = inert
        bounds[1, 8] = end

        def cell(k, _):
            first = jnp.where(k == 0, 0, bounds[0, jnp.maximum(k - 1, 0)])
            last = bounds[1, k + 1]
            table = tables.at[j * 8 + k]

            def chunk(i, acc):
                at = pl.multiple_of(first + i * CHUNK, 8)
                return add_pairs(packed[pl.ds(at, CHUNK), 0:KEYS], table, acc)

            zero = jnp.zeros((8, 128), F32)
            sums = lax.fori_loop(0, (last - first + CHUNK - 1) // CHUNK, chunk, (zero, zero, zero))
            for t in range(3):
                force[pl.ds((j * 8 + t) * 8 + k, 1), :] = jnp.sum(sums[t], 0, keepdims=True)
            return 0

        lax.fori_loop(0, 8, cell, 0)

    loads[2].wait()
    for j in range(2):
        fx, fy, fz = (
            force[(j * 8 + t) * 8 : (j * 8 + t) * 8 + 8, :]
            + inside[(j * 8 + t) * 8 : (j * 8 + t) * 8 + 8, :]
            for t in range(3)
        )
        fy, fz = fy + blade[j] * cos_b, fz + blade[j] * sin_b
        ox, oy, oz = (off[t, 0, j] for t in range(3))
        six = [fx, fy, fz, oy * fz - oz * fy, oz * fx - ox * fz, ox * fy - oy * fx]
        for t in range(8):
            force[(j * 8 + t) * 8 : (j * 8 + t) * 8 + 8, :] = (
                six[t] if t < 6 else jnp.zeros((8, 128), F32)
            )


def exchange_kernel(
    n_shaft,
    n_lat,
    force,
    hot_piece,
    hot_clump,
    route_rows,
    turning,
    motion_hbm,
    inverse_mass_hbm,
    table,
    motion,
    inverse_mass,
    part,
    got,
    send_sem,
    recv_sem,
    load_sem,
):
    place = Place(n_shaft, n_lat)
    n_clump = turning.shape[-1]
    place.greet()
    loads = [
        pltpu.make_async_copy(motion_hbm, motion, load_sem.at[0]),
        pltpu.make_async_copy(inverse_mass_hbm, inverse_mass, load_sem.at[1]),
    ]
    for load in loads:
        load.start()

    def sums_copy(ds, dl, slot):
        c = (ds + 1) * 3 + dl + 1
        return pltpu.make_async_remote_copy(
            src_ref=part.at[c],
            dst_ref=got.at[slot],
            send_sem=send_sem.at[0, slot],
            recv_sem=recv_sem.at[0, slot],
            device_id=place.at(ds, dl),
            device_id_type=MESH,
        )

    def table_copy(ds, dl, slot):
        return pltpu.make_async_remote_copy(
            src_ref=table.at[4],
            dst_ref=table.at[slot],
            send_sem=send_sem.at[1, slot],
            recv_sem=recv_sem.at[1, slot],
            device_id=place.at(ds, dl),
            device_id_type=MESH,
        )

    def around(act, dl):
        for ds in (-1, 0, 1):
            if (ds, dl) != (0, 0):
                act(ds, dl)

    terms = [
        rows3(force[pl.ds(j * 64 + k, 8, stride=8), :]).astype(BF16) for j in range(2) for k in range(8)
    ]
    sums = lax.dot_general(
        jnp.concatenate(terms, 1), hot_piece[...], LANES, preferred_element_type=F32
    )
    sums = rows3(sum3(sums))
    route = jnp.concatenate([route_rows[...]] * 3, 0)
    routed = jnp.concatenate([jnp.where(route == c, sums, 0.0) for c in range(9)], 0)
    sums = lax.dot_general(
        routed.astype(BF16), hot_clump[...], LANES, preferred_element_type=F32
    )
    for c in range(9):
        part[c] = sum3(sums[24 * c : 24 * c + 24])

    def clear(edge, column):
        @pl.when(place.l == edge)
        def _():
            for row in range(3):
                table[row * 3 + column] = jnp.zeros((8, n_clump), F32)
                got[row * 3 + 2 - column] = jnp.zeros((8, n_clump), F32)

    clear(0, 0)
    clear(n_lat - 1, 2)
    place.meet()
    place.lateral(
        lambda dl: around(lambda ds, d: sums_copy(ds, d, (ds + 1) * 3 + d + 1).start(), dl)
    )
    for load in loads:
        load.wait()
    place.lateral(
        lambda dl: around(lambda ds, d: sums_copy(ds, d, 8 - (ds + 1) * 3 - d - 1).wait_recv(), dl)
    )
    sums = part[4]
    for c in range(9):
        if c != 4:
            sums = sums + got[c]
    rows = []
    for t in range(3):
        pull = -GRAVITY if t == 2 else 0.0
        rows.append(motion[t, 0] + TIME_STEP * (inverse_mass[0] * sums[t : t + 1] + pull))
    torque = [sums[3 + t : 4 + t] for t in range(3)]
    order = ((0, 1, 2), (1, 3, 4), (2, 4, 5))
    for t in range(3):
        change = sum(turning[order[t][i] : order[t][i] + 1, :] * torque[i] for i in range(3))
        rows.append(motion[3 + t, 0] + change)
    table[4] = jnp.concatenate(rows + [jnp.zeros((2, n_clump), F32)], 0)
    place.lateral(
        lambda dl: around(lambda ds, d: table_copy(ds, d, 8 - (ds + 1) * 3 - d - 1).start(), dl)
    )
    place.lateral(
        lambda dl: around(lambda ds, d: table_copy(ds, d, (ds + 1) * 3 + d + 1).wait_recv(), dl)
    )
    place.lateral(
        lambda dl: around(lambda ds, d: sums_copy(ds, d, (ds + 1) * 3 + d + 1).wait_send(), dl)
    )
    place.lateral(
        lambda dl: around(lambda ds, d: table_copy(ds, d, 8 - (ds + 1) * 3 - d - 1).wait_send(), dl)
    )


def spread_kernel(
    table,
    hot_piece,
    hot_clump,
    route_rows,
    centre_hbm,
    off_hbm,
    clump_hbm,
    sphere_hbm,
    centre,
    off,
    clump_out,
    sphere_out,
    pose,
    sem,
):
    loads = [
        pltpu.make_async_copy(centre_hbm, centre, sem.at[0]),
        pltpu.make_async_copy(off_hbm, off, sem.at[1]),
    ]
    for load in loads:
        load.start()
    tables = jnp.concatenate([rows3(table[c]) for c in range(9)], 0).astype(BF16)
    found = lax.dot_general(tables, hot_clump[...], ROWS, preferred_element_type=F32)
    route = jnp.concatenate([route_rows[...]] * 3, 0)
    by_piece = found[0:24]
    for c in range(1, 9):
        by_piece = jnp.where(route == c, found[24 * c : 24 * c + 24], by_piece)
    by_sphere = sum3(
        lax.dot_general(by_piece.astype(BF16), hot_piece[...], ROWS, preferred_element_type=F32)
    )
    loads[0].wait()
    for t in range(6):
        row = table[4, t : t + 1, :]
        if t < 3:
            clump_out[t, 0] = centre[t, 0] + TIME_STEP * row
        clump_out[3 + t, 0] = row
    stores = [pltpu.make_async_copy(clump_out, clump_hbm, sem.at[2])]
    stores[0].start()
    for m in range(16):
        pose[m * 8 : m * 8 + 8, :] = by_sphere[:, m * 128 : m * 128 + 128]
    loads[1].wait()
    for j in range(2):
        vx, vy, vz, sx, sy, sz = (
            pose[pl.ds(j * 64 + t, 8, stride=8), :] for t in range(6)
        )
        bx, by, bz = (off[t, 0, j] for t in range(3))
        hx, hy, hz = (0.5 * TIME_STEP * s for s in (sx, sy, sz))
        scale = 2.0 / (1.0 + (hx * hx + hy * hy + hz * hz))
        cx, cy, cz = hy * bz - hz * by, hz * bx - hx * bz, hx * by - hy * bx
        tx = bx + scale * (cx + hy * cz - hz * cy)
        ty = by + scale * (cy + hz * cx - hx * cz)
        tz = bz + scale * (cz + hx * cy - hy * cx)
        sphere_out[0, 0, j], sphere_out[1, 0, j], sphere_out[2, 0, j] = tx, ty, tz
        sphere_out[3, 0, j] = vx + (sy * tz - sz * ty)
        sphere_out[4, 0, j] = vy + (sz * tx - sx * tz)
        sphere_out[5, 0, j] = vz + (sx * ty - sy * tx)
        stores.append(
            pltpu.make_async_copy(
                sphere_out.at[:, :, pl.ds(j, 1)], sphere_hbm.at[:, :, pl.ds(j, 1)], sem.at[3 + j]
            )
        )
        stores[-1].start()
    for store in stores:
        store.wait()


def contact_call(lat_cells, blade_phase, ext, inside, tables, off, angles, inertia, **extra):
    n_clump = angles.shape[-1]
    return pl.pallas_call(
        functools.partial(contact_kernel, lat_cells),
        out_shape=(
            jax.ShapeDtypeStruct((128, 128), F32),
            jax.ShapeDtypeStruct((8, n_clump), F32),
        ),
        in_specs=[SMEM] + [VMEM] * 3 + [HBM] * 3,
        out_specs=(VMEM, VMEM),
        scratch_shapes=[
            pltpu.VMEM(off.shape, F32),
            pltpu.VMEM(angles.shape, F32),
            pltpu.VMEM(inertia.shape, F32),
            pltpu.VMEM((144, 128), jnp.int32),
            pltpu.VMEM((16, 512), jnp.int32),
            pltpu.SMEM((16, 512), jnp.int32),
            pltpu.SMEM((2, 16), jnp.int32),
            pltpu.VMEM((9, 8, 256, 128), F32),
            pltpu.VMEM((9 * 1024 + 8 * 72 + 256, 128), F32),
            pltpu.SemaphoreType.DMA((4,)),
        ],
        compiler_params=pltpu.CompilerParams(vmem_limit_bytes=24 << 20),
        name="contact",
        **extra,
    )(blade_phase, ext, inside, tables, off, angles, inertia)


def on_device(
    n_shaft,
    n_lat,
    sphere_position,
    sphere_velocity,
    sphere_radius,
    sphere_offset,
    sphere_piece,
    piece_route,
    piece_clump,
    blade_phase,
    clump_centre,
    clump_motion,
    clump_angles,
    clump_inverse_mass,
    clump_inverse_inertia,
):
    n_piece, n_clump = piece_route.shape[-1], clump_angles.shape[-1]
    sphere_position, sphere_velocity, sphere_radius, sphere_piece, piece_route, piece_clump = (
        pltpu.with_memory_space_constraint(v, pltpu.HBM)
        for v in (
            sphere_position,
            sphere_velocity,
            sphere_radius,
            sphere_piece,
            piece_route,
            piece_clump,
        )
    )
    sphere_offset, clump_centre, clump_motion = (
        pltpu.with_memory_space_constraint(v, pltpu.HBM)
        for v in (sphere_offset, clump_centre, clump_motion)
    )
    clump_angles, clump_inverse_mass, clump_inverse_inertia = (
        pltpu.with_memory_space_constraint(v, pltpu.HBM)
        for v in (clump_angles, clump_inverse_mass, clump_inverse_inertia)
    )
    ext, hot_piece, hot_clump, route_rows, inside, tables = pl.pallas_call(
        functools.partial(halo_kernel, n_shaft, n_lat),
        out_shape=(
            jax.ShapeDtypeStruct((3, 4, 8, 8, 128), F32),
            jax.ShapeDtypeStruct((n_piece, 2048), BF16),
            jax.ShapeDtypeStruct((n_clump, n_piece), BF16),
            jax.ShapeDtypeStruct((8, n_piece), jnp.int32),
            jax.ShapeDtypeStruct((128, 128), F32),
            jax.ShapeDtypeStruct((16, KEYS, TERMS * 128), BF16),
        ),
        in_specs=[HBM] * 6,
        out_specs=(VMEM,) * 6,
        scratch_shapes=[
            pltpu.VMEM(sphere_piece.shape, jnp.int32),
            pltpu.VMEM(piece_route.shape, jnp.int32),
            pltpu.VMEM(piece_clump.shape, jnp.int32),
            pltpu.SemaphoreType.DMA((3, 4, 3)),
            pltpu.SemaphoreType.DMA((3, 4, 3)),
            pltpu.SemaphoreType.DMA((2, 3)),
            pltpu.SemaphoreType.DMA((3,)),
        ],
        compiler_params=pltpu.CompilerParams(
            collective_id=0, has_side_effects=True, vmem_limit_bytes=16 << 20
        ),
        name="halo",
    )(
        sphere_position,
        sphere_velocity,
        sphere_radius,
        sphere_piece,
        piece_route,
        piece_clump,
    )
    force, turning = contact_call(
        2 * n_lat,
        blade_phase,
        ext.reshape(768, 128),
        inside,
        tables,
        sphere_offset,
        clump_angles,
        clump_inverse_inertia,
    )
    table = pl.pallas_call(
        functools.partial(exchange_kernel, n_shaft, n_lat),
        out_shape=jax.ShapeDtypeStruct((9, 8, n_clump), F32),
        in_specs=[VMEM] * 5 + [HBM] * 2,
        out_specs=VMEM,
        scratch_shapes=[
            pltpu.VMEM(clump_motion.shape, F32),
            pltpu.VMEM(clump_inverse_mass.shape, F32),
            pltpu.VMEM((9, 8, n_clump), F32),
            pltpu.VMEM((9, 8, n_clump), F32),
            pltpu.SemaphoreType.DMA((2, 9)),
            pltpu.SemaphoreType.DMA((2, 9)),
            pltpu.SemaphoreType.DMA((2,)),
        ],
        compiler_params=pltpu.CompilerParams(
            collective_id=1, has_side_effects=True, vmem_limit_bytes=16 << 20
        ),
        name="exchange",
    )(force, hot_piece, hot_clump, route_rows, turning, clump_motion, clump_inverse_mass)
    return pl.pallas_call(
        spread_kernel,
        out_shape=(
            jax.ShapeDtypeStruct((9, 1, 1, n_clump), F32),
            jax.ShapeDtypeStruct((6, 1, 2, 8, 128), F32),
        ),
        in_specs=[VMEM] * 4 + [HBM] * 2,
        out_specs=(HBM, HBM),
        scratch_shapes=[
            pltpu.VMEM(clump_centre.shape, F32),
            pltpu.VMEM(sphere_offset.shape, F32),
            pltpu.VMEM((9, 1, 1, n_clump), F32),
            pltpu.VMEM((6, 1, 2, 8, 128), F32),
            pltpu.VMEM((128, 128), F32),
            pltpu.SemaphoreType.DMA((5,)),
        ],
        compiler_params=pltpu.CompilerParams(vmem_limit_bytes=16 << 20),
        name="spread",
    )(table, hot_piece, hot_clump, route_rows, clump_centre, sphere_offset)


def solution(mesh):
    placed = (
        P(None, "shaft", "lat", None, None),
        P(None, "shaft", "lat", None, None),
        P("shaft", "lat", None, None),
        P(None, "shaft", "lat", None, None),
        P("shaft", "lat", None),
        P("shaft", "lat", None),
        P("shaft", "lat", None),
        P(),
        P(None, "shaft", "lat", None),
        P(None, "shaft", "lat", None),
        P(None, "shaft", "lat", None),
        P("shaft", "lat", None),
        P(None, "shaft", "lat", None),
    )
    return jax.shard_map(
        functools.partial(on_device, mesh.shape["shaft"], mesh.shape["lat"]),
        mesh=mesh,
        in_specs=placed,
        out_specs=(P(None, "shaft", "lat", None), P(None, "shaft", "lat", None, None)),
        check_vma=False,
    )
```

```python
import functools
import math

import jax
import jax.numpy as jnp
from jax import lax
from jax.experimental import pallas as pl
from jax.experimental.pallas import tpu as pltpu
from jax.sharding import PartitionSpec as P

PHASES = 64
CELL_SIDE = 5.0
BLADE_STIFFNESS = 20.0
BLADE_THICKNESS = 1.0
TIME_STEP = 0.5
GRAVITY = 0.5

REACH = 0.6001
CHUNK = 64
F32 = jnp.float32
BF16 = jnp.bfloat16
MESH = pl.DeviceIdType.MESH
LANES = (((1,), (1,)), ((), ()))
ROWS = (((1,), (0,)), ((), ()))
VMEM = pl.BlockSpec(memory_space=pltpu.VMEM)
SMEM = pl.BlockSpec(memory_space=pltpu.SMEM)
HBM = pl.BlockSpec(memory_space=pltpu.HBM)


def split3(x):
    high = x.astype(BF16)
    rest = x - high.astype(F32)
    middle = rest.astype(BF16)
    low = (rest - middle.astype(F32)).astype(BF16)
    return high, middle, low


def rows3(x):
    high = x.astype(BF16).astype(F32)
    rest = x - high
    middle = rest.astype(BF16).astype(F32)
    return jnp.concatenate([high, middle, rest - middle], 0)


def sum3(x):
    return x[0:8] + x[8:16] + x[16:24]


def one_hot(rows, row):
    length = row.shape[-1]
    ids = lax.broadcasted_iota(jnp.int32, (rows, length), 0)
    return jnp.where(ids == row, 1.0, 0.0).astype(BF16)


class Place:
    def __init__(self, n_shaft, n_lat):
        self.n_shaft, self.n_lat = n_shaft, n_lat
        self.s, self.l = lax.axis_index("shaft"), lax.axis_index("lat")

    def at(self, ds, dl):
        return {"shaft": lax.rem(self.s + ds + self.n_shaft, self.n_shaft), "lat": self.l + dl}

    def lateral(self, act):
        act(0)
        pl.when(self.l > 0)(lambda: act(-1))
        pl.when(self.l < self.n_lat - 1)(lambda: act(1))

    def greet(self):
        sem = pltpu.get_barrier_semaphore()

        def signal(dl):
            for ds in (-1, 0, 1):
                if (ds, dl) != (0, 0):
                    pl.semaphore_signal(
                        sem, inc=1, device_id=self.at(ds, dl), device_id_type=MESH
                    )

        self.lateral(signal)

    def meet(self):
        sem = pltpu.get_barrier_semaphore()
        edge = jnp.logical_or(self.l == 0, self.l == self.n_lat - 1)
        pl.semaphore_wait(sem, jnp.where(edge, 5, 8))


def halo_kernel(
    n_shaft,
    n_lat,
    pos,
    vel,
    rad,
    piece_hbm,
    route_hbm,
    clump_hbm,
    ext,
    hot_piece,
    hot_clump,
    route_rows,
    inside,
    tables,
    piece,
    route,
    clump,
    send_sem,
    recv_sem,
    own_sem,
    load_sem,
):
    place = Place(n_shaft, n_lat)

    def parts(j, si, lj):
        return (
            (pos.at[:, 0, j], ext.at[si, lj, 0:3]),
            (vel.at[:, 0, j], ext.at[si, lj, 3:6]),
            (rad.at[0, pl.ds(j, 1)], ext.at[si, lj, 6:7]),
        )

    def remote(j, ds, dl, si, lj):
        return [
            pltpu.make_async_remote_copy(
                src_ref=src,
                dst_ref=dst,
                send_sem=send_sem.at[si, lj, t],
                recv_sem=recv_sem.at[si, lj, t],
                device_id=place.at(ds, dl),
                device_id_type=MESH,
            )
            for t, (src, dst) in enumerate(parts(j, si, lj))
        ]

    def outgoing(dl):
        found = []
        for ds in (-1, 0, 1):
            for j in (0, 1):
                lj = j - 2 * dl + 1
                if 0 <= lj <= 3 and (ds, dl) != (0, 0):
                    found += remote(j, ds, dl, 1 - ds, lj)
        return found

    def incoming(dl):
        found = []
        for ds in (-1, 0, 1):
            for lj in {0: (1, 2), -1: (0,), 1: (3,)}[dl]:
                if (ds, dl) != (0, 0):
                    found += remote(0, ds, dl, 1 + ds, lj)
        return found

    own = [
        pltpu.make_async_copy(src, dst, own_sem.at[j, t])
        for j in (0, 1)
        for t, (src, dst) in enumerate(parts(j, 1, 1 + j))
    ]
    own += [
        pltpu.make_async_copy(src, dst, load_sem.at[t])
        for t, (src, dst) in enumerate(
            ((piece_hbm, piece), (route_hbm, route), (clump_hbm, clump))
        )
    ]
    for c in own:
        c.start()
    place.greet()
    place.meet()
    place.lateral(lambda dl: [c.start() for c in outgoing(dl)] and None)
    ext[:, :, 7] = jnp.zeros((3, 4, 8, 128), F32)

    @pl.when(place.l == 0)
    def _():
        ext[:, 0, 0:7] = jnp.zeros((3, 7, 8, 128), F32)

    @pl.when(place.l == n_lat - 1)
    def _():
        ext[:, 3, 0:7] = jnp.zeros((3, 7, 8, 128), F32)

    for c in own:
        c.wait()
    sub = lax.broadcasted_iota(jnp.int32, (8, 128), 0)
    every = one_hot(128, lax.broadcasted_iota(jnp.int32, (1, 128), 1))
    inside[...] = jnp.zeros((128, 128), F32)

    def cell(m):
        j, k = m // 8, m % 8
        mine = [ext[1, 1 + j, t, pl.ds(k, 1), :] for t in range(7)]
        mine[2] = mine[2] + (CELL_SIDE * k.astype(F32) - 20.0)
        own_table(mine, sub, tables.at[m])
        value = jnp.concatenate(mine + [mine[6]], 0)
        rows = lax.dot_general(every, keyed(value, sub), LANES, preferred_element_type=F32)
        zero = jnp.zeros((8, 128), F32)
        acc = (zero, zero, zero)
        for i in range(0, 128, CHUNK):
            acc = add_pairs(rows[i : i + CHUNK], tables.at[m], acc)
        for t in range(3):
            inside[pl.ds((j * 8 + t) * 8 + k, 1), :] = jnp.sum(acc[t], 0, keepdims=True)

    def cells(i, _):
        cell(2 * i)
        cell(2 * i + 1)
        return 0

    lax.fori_loop(0, 8, cells, 0)
    for m in range(16):
        hot_piece[:, m * 128 : m * 128 + 128] = one_hot(
            hot_piece.shape[0], piece[0, :, m * 128 : m * 128 + 128]
        )
    hot_clump[...] = one_hot(hot_clump.shape[0], clump[0])
    route_rows[...] = jnp.broadcast_to(route[0], route_rows.shape)
    place.lateral(lambda dl: [c.wait_recv() for c in incoming(dl)] and None)
    place.lateral(lambda dl: [c.wait_send() for c in outgoing(dl)] and None)


USUAL = {0: (128, 64, 64, 64), 1: (64, 24, 40, 24), 2: (32, 16, 24, 16)}
KEYS = 32
TERMS = 9


def kind(c):
    return (c // 3 != 1) + (c % 3 != 1)


def keyed(value, sub):
    radius = value[6:7]
    value = jnp.where(sub == 7, radius * radius * 0.0625, value)
    high = value.astype(BF16).astype(F32)
    rest = value - high
    middle = rest.astype(BF16).astype(F32)
    more = jnp.where(
        sub < 3,
        1.0,
        jnp.where(sub < 5, high[6:7], jnp.where(sub == 5, middle[6:7], 0.0)),
    )
    return jnp.concatenate([high, middle, rest - middle, more], 0).astype(BF16)


def own_table(own, sub, table):
    zero = jnp.zeros((8, 128), F32)

    def split(row):
        return [p.astype(F32) for p in split3(jnp.broadcast_to(row, (8, 128)))]

    def constants(row):
        high, middle, low = split(row)
        return jnp.where(sub == 0, high, jnp.where(sub == 1, middle, jnp.where(sub == 2, low, 0.0)))

    def put(t, same, more):
        block = jnp.concatenate([same, same, same, more], 0)
        table[:, t * 128 : t * 128 + 128] = block.astype(BF16)

    for t in range(7):
        put(t, jnp.where(sub == t, 1.0 if t == 6 else -1.0, zero), constants(own[t]))
    high, middle, low = split(4.0 * own[6])
    same = jnp.where(sub == 6, high, 0.0)
    more = jnp.where(sub == 4, low, jnp.where((sub == 3) | (sub == 5), middle, 0.0))
    put(7, same, more)
    put(
        8,
        jnp.where(sub == 7, 1.0, same * 0.03125),
        more * 0.03125 + constants(own[6] * own[6] * 0.0625),
    )


def pair_sums(pair, acc):
    dx, dy, dz, du, dv, dw, radii, product, least = pair
    square = dx * dx + dy * dy + dz * dz
    clamped = jnp.maximum(square, least)
    inverse = lax.rsqrt(clamped)
    delta = jnp.maximum(radii - clamped * inverse, 0.0)
    normal_speed = (du * dx + dv * dy + dw * dz) * inverse
    speed = du * du + dv * dv + dw * dw
    unit = square * (inverse * inverse)
    sliding = speed + normal_speed * normal_speed * (unit - 2.0)
    load = product * delta
    root = load * lax.rsqrt(jnp.maximum(load * radii, 1e-30))
    root2 = root * root
    cap = 2.5 * delta
    shear = root2 * cap * lax.rsqrt(jnp.maximum(root2 * (sliding + cap * cap), 0.0) + 1e-06)
    push = root * (cap + cap - normal_speed - 0.25)
    along = (push + shear * normal_speed) * inverse
    return (
        acc[0] + (along * dx - shear * du),
        acc[1] + (along * dy - shear * dv),
        acc[2] + (along * dz - shear * dw),
    )


def add_pairs(rows, table, acc):
    pairs = lax.dot_general(rows.astype(BF16), table[...], ROWS, preferred_element_type=F32)
    for g in range(0, rows.shape[0], 8):
        acc = pair_sums([pairs[g : g + 8, t * 128 : t * 128 + 128] for t in range(TERMS)], acc)
    return acc


def contact_kernel(
    lat_cells,
    phase,
    ext,
    inside,
    tables,
    off_hbm,
    angles_hbm,
    inertia_hbm,
    force,
    turning,
    off,
    angles,
    inertia,
    dest,
    count_v,
    count_s,
    bounds,
    picked,
    packed,
    copy_sem,
):
    loads = [
        pltpu.make_async_copy(src, dst, copy_sem.at[1 + t])
        for t, (src, dst) in enumerate(
            ((angles_hbm, angles), (inertia_hbm, inertia), (off_hbm, off))
        )
    ]
    for load in loads:
        load.start()
    sub = lax.broadcasted_iota(jnp.int32, (8, 128), 0)

    before = jnp.where(
        lax.broadcasted_iota(jnp.int32, (128, 128), 0)
        < lax.broadcasted_iota(jnp.int32, (128, 128), 1),
        1.0,
        0.0,
    ).astype(BF16)
    ones = jnp.ones((128, 128), BF16)
    for j in range(2):
        masks = []
        for c in range(9):
            di, dj = c // 3 - 1, c % 3 - 1
            base = ((1 + di) * 4 + 1 + j + dj) * 64
            x, y, z = (ext[base + 8 * t : base + 8 * t + 8, :] for t in range(3))
            radius = ext[base + 48 : base + 56, :]
            keep = radius > 0.0
            near = radius + REACH
            away = [v if d > 0 else CELL_SIDE - v for v, d in ((x, di), (y, dj)) if d]
            if len(away) == 1:
                keep &= away[0] < near
            if len(away) == 2:
                keep &= away[0] * away[0] + away[1] * away[1] < near * near
            low, high = z < near, CELL_SIDE - z < near
            kept = jnp.where(keep, 1.0, 0.0)
            low_f = jnp.where(low, kept, 0.0)
            high_f = jnp.where(high, kept, 0.0)
            mid_f = jnp.zeros((8, 128), F32) if c == 4 else kept - low_f - high_f
            masks += [low_f, mid_f, high_f]
        mask = jnp.concatenate(masks, 0).astype(BF16)
        prefix = lax.dot_general(mask, before, ROWS, preferred_element_type=F32)
        total = lax.dot_general(mask, ones, ROWS, preferred_element_type=F32)
        counts = lax.dot_general(ones[0:8], mask, LANES, preferred_element_type=F32)
        count_v[0:8, j * 256 : j * 256 + 216] = counts.astype(jnp.int32)
        over = jnp.full((8, 128), -1.0, F32)
        for c in range(9):
            a = c * 24
            low_p, mid_p, high_p = (prefix[a + 8 * t : a + 8 * t + 8] for t in range(3))
            low_n, mid_n, high_n = (total[a + 8 * t : a + 8 * t + 8] for t in range(3))
            spot = (
                masks[3 * c] * low_p
                + masks[3 * c + 1] * (low_n + mid_p)
                + masks[3 * c + 2] * (low_n + mid_n + high_p)
            )
            any_of = masks[3 * c] + masks[3 * c + 1] + masks[3 * c + 2]
            spot = jnp.where(any_of > 0.0, spot, -1.0).astype(jnp.int32)
            dest[(j * 9 + c) * 8 : (j * 9 + c) * 8 + 8, :] = spot
            sizes = (low_n + mid_n + high_n, low_n, mid_n, high_n)
            for size, usual in zip(sizes, USUAL[kind(c)]):
                over = jnp.maximum(over, size - usual)
        over = jnp.broadcast_to(jnp.max(over, 0, keepdims=True), (8, 128))
        count_v[8:16, j * 128 : j * 128 + 128] = over.astype(jnp.int32)
    copy = pltpu.make_async_copy(count_v, count_s, copy_sem.at[0])
    copy.start()

    angle = jnp.full((8, 128), phase[0].astype(F32) * (2.0 * math.pi / PHASES), F32)
    cos_b, sin_b = jnp.cos(angle), jnp.sin(angle)
    height_cells = 8
    centre_y, centre_z = 0.5 * CELL_SIDE * lat_cells, 0.5 * CELL_SIDE * height_cells
    reach = 0.45 * CELL_SIDE * min(lat_cells, height_cells)
    shaft_id = lax.axis_index("shaft").astype(F32)
    lat_id = (lax.axis_index("lat") * 2).astype(F32)
    up_id = sub.astype(F32)
    blade = []
    for j in range(2):
        base = (5 + j) * 64
        x, y, z = (ext[base + 8 * t : base + 8 * t + 8, :] for t in range(3))
        radius = ext[base + 48 : base + 56, :]
        x = CELL_SIDE * shaft_id + x
        y = CELL_SIDE * (lat_id + j) + y - centre_y
        z = CELL_SIDE * up_id + z - centre_z
        across = y * cos_b + z * sin_b
        radial = z * cos_b - y * sin_b
        depth = jnp.maximum(jnp.minimum(radius - across, radius + BLADE_THICKNESS + across), 0.0)
        window = jnp.maximum(radial * (reach - radial), 0.0) * (4.0 / (reach * reach))
        gate = jnp.maximum(jnp.cos(x * (2.0 * math.pi / (2.0 * CELL_SIDE))), 0.0)
        size = BLADE_STIFFNESS * depth * window * gate
        blade.append(size)

    loads[0].wait()
    loads[1].wait()
    n_clump = turning.shape[-1]
    cos_z, cos_y, cos_x = (jnp.cos(angles[t, 0]) for t in range(3))
    sin_z, sin_y, sin_x = (jnp.sin(angles[t, 0]) for t in range(3))
    rotation = [
        [
            cos_z * cos_y,
            cos_z * sin_y * sin_x - sin_z * cos_x,
            cos_z * sin_y * cos_x + sin_z * sin_x,
        ],
        [
            sin_z * cos_y,
            sin_z * sin_y * sin_x + cos_z * cos_x,
            sin_z * sin_y * cos_x - cos_z * sin_x,
        ],
        [-sin_y, cos_y * sin_x, cos_y * cos_x],
    ]
    for t, (a, b) in enumerate(((0, 0), (0, 1), (0, 2), (1, 1), (1, 2), (2, 2))):
        turning[t : t + 1, :] = TIME_STEP * sum(
            rotation[a][i] * inertia[i, 0] * rotation[b][i] for i in range(3)
        )
    turning[6:8, :] = jnp.zeros((2, n_clump), F32)
    lane = lax.broadcasted_iota(jnp.int32, (32, 128), 1)
    inert = jnp.where((lane >= 24) & (lane < 27), 1.0, 0.0)
    for j in range(2):

        def count(c, t, k):
            return count_s[0, j * 256 + (c * 3 + t) * 8 + k]

        def pick(c, k, rows, into):
            di, dj = c // 3 - 1, c % 3 - 1
            base = ((1 + di) * 4 + 1 + j + dj) * 64
            rise = CELL_SIDE * k.astype(F32) - 20.0
            shift = jnp.where(
                sub == 0,
                CELL_SIDE * di,
                jnp.where(sub == 1, CELL_SIDE * dj, jnp.where(sub == 2, rise, 0.0)),
            )
            value = ext[pl.ds(base + k, 8, stride=8), :] + shift
            spot = dest[pl.ds((j * 9 + c) * 8 + k, 1), :]
            keys = jnp.concatenate([keyed(value, sub), jnp.zeros((128 - KEYS, 128), BF16)], 0)
            into[k, 0:rows, :] = lax.dot_general(
                one_hot(rows, spot), keys, LANES, preferred_element_type=F32
            )

        sides = [c for c in range(9) if c != 4]

        def pick_some(i, _):
            for k in (4 * i, 4 * i + 1, 4 * i + 2, 4 * i + 3):
                for c in range(9):
                    pick(c, k, USUAL[kind(c)][0], picked.at[c])
            return 0

        lax.fori_loop(0, 2, pick_some, 0)
        if j == 0:
            copy.wait()

        def gather_level(k, offset, sizes):
            for t in range(3):
                start_of_part = offset
                if t == 2:
                    bounds[0, k] = offset
                for c in sides:
                    start = 0 if t == 0 else count(c, 0, k)
                    if t == 2:
                        start = start + count(c, 1, k)
                    length = sizes[kind(c)][1 + t]
                    packed[pl.ds(offset, length), :] = picked[c, k, pl.ds(start, length), :]
                    offset = offset + count(c, t, k)
                if t == 0:
                    bounds[1, k] = offset
                if t == 1:
                    packed[pl.ds(offset, 32), :] = inert
                    offset = jnp.maximum(offset, start_of_part + 32)
                    below, above = (k + 7) % 8, (k + 1) % 8
                    length = sizes[0][1]
                    start = count(4, 0, below)
                    packed[pl.ds(offset, length), :] = picked[4, below, pl.ds(start, length), :]
                    offset = offset + jnp.where(k > 0, count(4, 2, below), 0)
                    packed[pl.ds(offset, length), :] = picked[4, above, pl.ds(0, length), :]
                    offset = offset + jnp.where(k < 7, count(4, 0, above), 0)
                    packed[pl.ds(offset, 8), :] = inert[0:8]
                    offset = (offset + 7) // 8 * 8
            return offset

        def gather_usual():
            offset = 0
            for k in range(8):
                offset = gather_level(k, offset, USUAL)
            return offset

        def gather_any():
            def level(k, offset):
                for c in sides:
                    pick(c, k, 128, picked.at[c])
                return gather_level(k, offset, {t: (128,) * 4 for t in range(3)})

            return lax.fori_loop(0, 8, level, jnp.int32(0))

        end = lax.cond(count_s[8, j * 128] > 0, gather_any, gather_usual)
        packed[pl.ds(end, 32), :] = inert
        bounds[1, 8] = end

        def cell(k, _):
            first = jnp.where(k == 0, 0, bounds[0, jnp.maximum(k - 1, 0)])
            last = bounds[1, k + 1]
            table = tables.at[j * 8 + k]

            parts = (last - first + 31) // 32
            sums = (jnp.zeros((8, 128), F32),) * 3
            for size, times in ((128, parts // 4), (64, parts % 4 // 2), (32, parts % 2 // 1)):

                def chunk(i, acc, size=size):
                    at = pl.multiple_of(first + i * size, 8)
                    return add_pairs(packed[pl.ds(at, size), 0:KEYS], table, acc)

                sums = lax.fori_loop(0, times, chunk, sums)
                first = first + times * size
            for t in range(3):
                force[pl.ds((j * 8 + t) * 8 + k, 1), :] = jnp.sum(sums[t], 0, keepdims=True)
            return 0

        lax.fori_loop(0, 8, cell, 0)

    loads[2].wait()
    for j in range(2):
        fx, fy, fz = (
            force[(j * 8 + t) * 8 : (j * 8 + t) * 8 + 8, :]
            + inside[(j * 8 + t) * 8 : (j * 8 + t) * 8 + 8, :]
            for t in range(3)
        )
        fy, fz = fy + blade[j] * cos_b, fz + blade[j] * sin_b
        ox, oy, oz = (off[t, 0, j] for t in range(3))
        six = [fx, fy, fz, oy * fz - oz * fy, oz * fx - ox * fz, ox * fy - oy * fx]
        for t in range(8):
            force[(j * 8 + t) * 8 : (j * 8 + t) * 8 + 8, :] = (
                six[t] if t < 6 else jnp.zeros((8, 128), F32)
            )


def exchange_kernel(
    n_shaft,
    n_lat,
    force,
    hot_piece,
    hot_clump,
    route_rows,
    turning,
    motion_hbm,
    inverse_mass_hbm,
    table,
    motion,
    inverse_mass,
    part,
    got,
    send_sem,
    recv_sem,
    load_sem,
):
    place = Place(n_shaft, n_lat)
    n_clump = turning.shape[-1]
    place.greet()
    loads = [
        pltpu.make_async_copy(motion_hbm, motion, load_sem.at[0]),
        pltpu.make_async_copy(inverse_mass_hbm, inverse_mass, load_sem.at[1]),
    ]
    for load in loads:
        load.start()

    def sums_copy(ds, dl, slot):
        c = (ds + 1) * 3 + dl + 1
        return pltpu.make_async_remote_copy(
            src_ref=part.at[c],
            dst_ref=got.at[slot],
            send_sem=send_sem.at[0, slot],
            recv_sem=recv_sem.at[0, slot],
            device_id=place.at(ds, dl),
            device_id_type=MESH,
        )

    def table_copy(ds, dl, slot):
        return pltpu.make_async_remote_copy(
            src_ref=table.at[4],
            dst_ref=table.at[slot],
            send_sem=send_sem.at[1, slot],
            recv_sem=recv_sem.at[1, slot],
            device_id=place.at(ds, dl),
            device_id_type=MESH,
        )

    def around(act, dl):
        for ds in (-1, 0, 1):
            if (ds, dl) != (0, 0):
                act(ds, dl)

    terms = [
        rows3(force[pl.ds(j * 64 + k, 8, stride=8), :]).astype(BF16) for j in range(2) for k in range(8)
    ]
    sums = lax.dot_general(
        jnp.concatenate(terms, 1), hot_piece[...], LANES, preferred_element_type=F32
    )
    sums = rows3(sum3(sums))
    route = jnp.concatenate([route_rows[...]] * 3, 0)
    routed = jnp.concatenate([jnp.where(route == c, sums, 0.0) for c in range(9)], 0)
    sums = lax.dot_general(
        routed.astype(BF16), hot_clump[...], LANES, preferred_element_type=F32
    )
    for c in range(9):
        part[c] = sum3(sums[24 * c : 24 * c + 24])

    def clear(edge, column):
        @pl.when(place.l == edge)
        def _():
            for row in range(3):
                table[row * 3 + column] = jnp.zeros((8, n_clump), F32)
                got[row * 3 + 2 - column] = jnp.zeros((8, n_clump), F32)

    clear(0, 0)
    clear(n_lat - 1, 2)
    place.meet()
    place.lateral(
        lambda dl: around(lambda ds, d: sums_copy(ds, d, (ds + 1) * 3 + d + 1).start(), dl)
    )
    for load in loads:
        load.wait()
    place.lateral(
        lambda dl: around(lambda ds, d: sums_copy(ds, d, 8 - (ds + 1) * 3 - d - 1).wait_recv(), dl)
    )
    sums = part[4]
    for c in range(9):
        if c != 4:
            sums = sums + got[c]
    rows = []
    for t in range(3):
        pull = -GRAVITY if t == 2 else 0.0
        rows.append(motion[t, 0] + TIME_STEP * (inverse_mass[0] * sums[t : t + 1] + pull))
    torque = [sums[3 + t : 4 + t] for t in range(3)]
    order = ((0, 1, 2), (1, 3, 4), (2, 4, 5))
    for t in range(3):
        change = sum(turning[order[t][i] : order[t][i] + 1, :] * torque[i] for i in range(3))
        rows.append(motion[3 + t, 0] + change)
    table[4] = jnp.concatenate(rows + [jnp.zeros((2, n_clump), F32)], 0)
    place.lateral(
        lambda dl: around(lambda ds, d: table_copy(ds, d, 8 - (ds + 1) * 3 - d - 1).start(), dl)
    )
    place.lateral(
        lambda dl: around(lambda ds, d: table_copy(ds, d, (ds + 1) * 3 + d + 1).wait_recv(), dl)
    )
    place.lateral(
        lambda dl: around(lambda ds, d: sums_copy(ds, d, (ds + 1) * 3 + d + 1).wait_send(), dl)
    )
    place.lateral(
        lambda dl: around(lambda ds, d: table_copy(ds, d, 8 - (ds + 1) * 3 - d - 1).wait_send(), dl)
    )


def spread_kernel(
    table,
    hot_piece,
    hot_clump,
    route_rows,
    centre_hbm,
    off_hbm,
    clump_hbm,
    sphere_hbm,
    centre,
    off,
    clump_out,
    sphere_out,
    pose,
    sem,
):
    loads = [
        pltpu.make_async_copy(centre_hbm, centre, sem.at[0]),
        pltpu.make_async_copy(off_hbm, off, sem.at[1]),
    ]
    for load in loads:
        load.start()
    tables = jnp.concatenate([rows3(table[c]) for c in range(9)], 0).astype(BF16)
    found = lax.dot_general(tables, hot_clump[...], ROWS, preferred_element_type=F32)
    route = jnp.concatenate([route_rows[...]] * 3, 0)
    by_piece = found[0:24]
    for c in range(1, 9):
        by_piece = jnp.where(route == c, found[24 * c : 24 * c + 24], by_piece)
    by_sphere = sum3(
        lax.dot_general(by_piece.astype(BF16), hot_piece[...], ROWS, preferred_element_type=F32)
    )
    loads[0].wait()
    for t in range(6):
        row = table[4, t : t + 1, :]
        if t < 3:
            clump_out[t, 0] = centre[t, 0] + TIME_STEP * row
        clump_out[3 + t, 0] = row
    stores = [pltpu.make_async_copy(clump_out, clump_hbm, sem.at[2])]
    stores[0].start()
    for m in range(16):
        pose[m * 8 : m * 8 + 8, :] = by_sphere[:, m * 128 : m * 128 + 128]
    loads[1].wait()
    for j in range(2):
        vx, vy, vz, sx, sy, sz = (
            pose[pl.ds(j * 64 + t, 8, stride=8), :] for t in range(6)
        )
        bx, by, bz = (off[t, 0, j] for t in range(3))
        hx, hy, hz = (0.5 * TIME_STEP * s for s in (sx, sy, sz))
        scale = 2.0 / (1.0 + (hx * hx + hy * hy + hz * hz))
        cx, cy, cz = hy * bz - hz * by, hz * bx - hx * bz, hx * by - hy * bx
        tx = bx + scale * (cx + hy * cz - hz * cy)
        ty = by + scale * (cy + hz * cx - hx * cz)
        tz = bz + scale * (cz + hx * cy - hy * cx)
        sphere_out[0, 0, j], sphere_out[1, 0, j], sphere_out[2, 0, j] = tx, ty, tz
        sphere_out[3, 0, j] = vx + (sy * tz - sz * ty)
        sphere_out[4, 0, j] = vy + (sz * tx - sx * tz)
        sphere_out[5, 0, j] = vz + (sx * ty - sy * tx)
        stores.append(
            pltpu.make_async_copy(
                sphere_out.at[:, :, pl.ds(j, 1)], sphere_hbm.at[:, :, pl.ds(j, 1)], sem.at[3 + j]
            )
        )
        stores[-1].start()
    for store in stores:
        store.wait()


def contact_call(lat_cells, blade_phase, ext, inside, tables, off, angles, inertia, **extra):
    n_clump = angles.shape[-1]
    return pl.pallas_call(
        functools.partial(contact_kernel, lat_cells),
        out_shape=(
            jax.ShapeDtypeStruct((128, 128), F32),
            jax.ShapeDtypeStruct((8, n_clump), F32),
        ),
        in_specs=[SMEM] + [VMEM] * 3 + [HBM] * 3,
        out_specs=(VMEM, VMEM),
        scratch_shapes=[
            pltpu.VMEM(off.shape, F32),
            pltpu.VMEM(angles.shape, F32),
            pltpu.VMEM(inertia.shape, F32),
            pltpu.VMEM((144, 128), jnp.int32),
            pltpu.VMEM((16, 512), jnp.int32),
            pltpu.SMEM((16, 512), jnp.int32),
            pltpu.SMEM((2, 16), jnp.int32),
            pltpu.VMEM((9, 8, 256, 128), F32),
            pltpu.VMEM((9 * 1024 + 8 * 72 + 256, 128), F32),
            pltpu.SemaphoreType.DMA((4,)),
        ],
        compiler_params=pltpu.CompilerParams(vmem_limit_bytes=24 << 20),
        name="contact",
        **extra,
    )(blade_phase, ext, inside, tables, off, angles, inertia)


def on_device(
    n_shaft,
    n_lat,
    sphere_position,
    sphere_velocity,
    sphere_radius,
    sphere_offset,
    sphere_piece,
    piece_route,
    piece_clump,
    blade_phase,
    clump_centre,
    clump_motion,
    clump_angles,
    clump_inverse_mass,
    clump_inverse_inertia,
):
    n_piece, n_clump = piece_route.shape[-1], clump_angles.shape[-1]
    sphere_position, sphere_velocity, sphere_radius, sphere_piece, piece_route, piece_clump = (
        pltpu.with_memory_space_constraint(v, pltpu.HBM)
        for v in (
            sphere_position,
            sphere_velocity,
            sphere_radius,
            sphere_piece,
            piece_route,
            piece_clump,
        )
    )
    sphere_offset, clump_centre, clump_motion = (
        pltpu.with_memory_space_constraint(v, pltpu.HBM)
        for v in (sphere_offset, clump_centre, clump_motion)
    )
    clump_angles, clump_inverse_mass, clump_inverse_inertia = (
        pltpu.with_memory_space_constraint(v, pltpu.HBM)
        for v in (clump_angles, clump_inverse_mass, clump_inverse_inertia)
    )
    ext, hot_piece, hot_clump, route_rows, inside, tables = pl.pallas_call(
        functools.partial(halo_kernel, n_shaft, n_lat),
        out_shape=(
            jax.ShapeDtypeStruct((3, 4, 8, 8, 128), F32),
            jax.ShapeDtypeStruct((n_piece, 2048), BF16),
            jax.ShapeDtypeStruct((n_clump, n_piece), BF16),
            jax.ShapeDtypeStruct((8, n_piece), jnp.int32),
            jax.ShapeDtypeStruct((128, 128), F32),
            jax.ShapeDtypeStruct((16, KEYS, TERMS * 128), BF16),
        ),
        in_specs=[HBM] * 6,
        out_specs=(VMEM,) * 6,
        scratch_shapes=[
            pltpu.VMEM(sphere_piece.shape, jnp.int32),
            pltpu.VMEM(piece_route.shape, jnp.int32),
            pltpu.VMEM(piece_clump.shape, jnp.int32),
            pltpu.SemaphoreType.DMA((3, 4, 3)),
            pltpu.SemaphoreType.DMA((3, 4, 3)),
            pltpu.SemaphoreType.DMA((2, 3)),
            pltpu.SemaphoreType.DMA((3,)),
        ],
        compiler_params=pltpu.CompilerParams(
            collective_id=0, has_side_effects=True, vmem_limit_bytes=16 << 20
        ),
        name="halo",
    )(
        sphere_position,
        sphere_velocity,
        sphere_radius,
        sphere_piece,
        piece_route,
        piece_clump,
    )
    force, turning = contact_call(
        2 * n_lat,
        blade_phase,
        ext.reshape(768, 128),
        inside,
        tables,
        sphere_offset,
        clump_angles,
        clump_inverse_inertia,
    )
    table = pl.pallas_call(
        functools.partial(exchange_kernel, n_shaft, n_lat),
        out_shape=jax.ShapeDtypeStruct((9, 8, n_clump), F32),
        in_specs=[VMEM] * 5 + [HBM] * 2,
        out_specs=VMEM,
        scratch_shapes=[
            pltpu.VMEM(clump_motion.shape, F32),
            pltpu.VMEM(clump_inverse_mass.shape, F32),
            pltpu.VMEM((9, 8, n_clump), F32),
            pltpu.VMEM((9, 8, n_clump), F32),
            pltpu.SemaphoreType.DMA((2, 9)),
            pltpu.SemaphoreType.DMA((2, 9)),
            pltpu.SemaphoreType.DMA((2,)),
        ],
        compiler_params=pltpu.CompilerParams(
            collective_id=1, has_side_effects=True, vmem_limit_bytes=16 << 20
        ),
        name="exchange",
    )(force, hot_piece, hot_clump, route_rows, turning, clump_motion, clump_inverse_mass)
    return pl.pallas_call(
        spread_kernel,
        out_shape=(
            jax.ShapeDtypeStruct((9, 1, 1, n_clump), F32),
            jax.ShapeDtypeStruct((6, 1, 2, 8, 128), F32),
        ),
        in_specs=[VMEM] * 4 + [HBM] * 2,
        out_specs=(HBM, HBM),
        scratch_shapes=[
            pltpu.VMEM(clump_centre.shape, F32),
            pltpu.VMEM(sphere_offset.shape, F32),
            pltpu.VMEM((9, 1, 1, n_clump), F32),
            pltpu.VMEM((6, 1, 2, 8, 128), F32),
            pltpu.VMEM((128, 128), F32),
            pltpu.SemaphoreType.DMA((5,)),
        ],
        compiler_params=pltpu.CompilerParams(vmem_limit_bytes=16 << 20),
        name="spread",
    )(table, hot_piece, hot_clump, route_rows, clump_centre, sphere_offset)


def solution(mesh):
    placed = (
        P(None, "shaft", "lat", None, None),
        P(None, "shaft", "lat", None, None),
        P("shaft", "lat", None, None),
        P(None, "shaft", "lat", None, None),
        P("shaft", "lat", None),
        P("shaft", "lat", None),
        P("shaft", "lat", None),
        P(),
        P(None, "shaft", "lat", None),
        P(None, "shaft", "lat", None),
        P(None, "shaft", "lat", None),
        P("shaft", "lat", None),
        P(None, "shaft", "lat", None),
    )
    return jax.shard_map(
        functools.partial(on_device, mesh.shape["shaft"], mesh.shape["lat"]),
        mesh=mesh,
        in_specs=placed,
        out_specs=(P(None, "shaft", "lat", None), P(None, "shaft", "lat", None, None)),
        check_vma=False,
    )
```

```python
import functools
import math

import jax
import jax.numpy as jnp
from jax import lax
from jax.experimental import pallas as pl
from jax.experimental.pallas import tpu as pltpu
from jax.sharding import PartitionSpec as P

PHASES = 64
CELL_SIDE = 5.0
BLADE_STIFFNESS = 20.0
BLADE_THICKNESS = 1.0
TIME_STEP = 0.5
GRAVITY = 0.5

REACH = 0.6001
CHUNK = 64
F32 = jnp.float32
BF16 = jnp.bfloat16
MESH = pl.DeviceIdType.MESH
LANES = (((1,), (1,)), ((), ()))
ROWS = (((1,), (0,)), ((), ()))
VMEM = pl.BlockSpec(memory_space=pltpu.VMEM)
SMEM = pl.BlockSpec(memory_space=pltpu.SMEM)
HBM = pl.BlockSpec(memory_space=pltpu.HBM)


def split3(x):
    high = x.astype(BF16)
    rest = x - high.astype(F32)
    middle = rest.astype(BF16)
    low = (rest - middle.astype(F32)).astype(BF16)
    return high, middle, low


def rows3(x):
    high = x.astype(BF16).astype(F32)
    rest = x - high
    middle = rest.astype(BF16).astype(F32)
    return jnp.concatenate([high, middle, rest - middle], 0)


def sum3(x):
    return x[0:8] + x[8:16] + x[16:24]


def one_hot(rows, row):
    length = row.shape[-1]
    ids = lax.broadcasted_iota(jnp.int16, (rows, length), 0)
    return jnp.where(ids == row.astype(jnp.int16), jnp.ones((), BF16), jnp.zeros((), BF16))


class Place:
    def __init__(self, n_shaft, n_lat):
        self.n_shaft, self.n_lat = n_shaft, n_lat
        self.s, self.l = lax.axis_index("shaft"), lax.axis_index("lat")

    def at(self, ds, dl):
        return {"shaft": lax.rem(self.s + ds + self.n_shaft, self.n_shaft), "lat": self.l + dl}

    def lateral(self, act):
        act(0)
        pl.when(self.l > 0)(lambda: act(-1))
        pl.when(self.l < self.n_lat - 1)(lambda: act(1))

    def greet(self):
        sem = pltpu.get_barrier_semaphore()

        def signal(dl):
            for ds in (-1, 0, 1):
                if (ds, dl) != (0, 0):
                    pl.semaphore_signal(
                        sem, inc=1, device_id=self.at(ds, dl), device_id_type=MESH
                    )

        self.lateral(signal)

    def meet(self):
        sem = pltpu.get_barrier_semaphore()
        edge = jnp.logical_or(self.l == 0, self.l == self.n_lat - 1)
        pl.semaphore_wait(sem, jnp.where(edge, 5, 8))


def halo_kernel(
    n_shaft,
    n_lat,
    pos,
    vel,
    rad,
    piece_hbm,
    route_hbm,
    clump_hbm,
    ext,
    hot_piece,
    hot_clump,
    route_rows,
    inside,
    tables,
    piece,
    route,
    clump,
    send_sem,
    recv_sem,
    own_sem,
    load_sem,
):
    place = Place(n_shaft, n_lat)

    def parts(j, si, lj):
        return (
            (pos.at[:, 0, j], ext.at[si, lj, 0:3]),
            (vel.at[:, 0, j], ext.at[si, lj, 3:6]),
            (rad.at[0, pl.ds(j, 1)], ext.at[si, lj, 6:7]),
        )

    def remote(j, ds, dl, si, lj):
        return [
            pltpu.make_async_remote_copy(
                src_ref=src,
                dst_ref=dst,
                send_sem=send_sem.at[si, lj, t],
                recv_sem=recv_sem.at[si, lj, t],
                device_id=place.at(ds, dl),
                device_id_type=MESH,
            )
            for t, (src, dst) in enumerate(parts(j, si, lj))
        ]

    def outgoing(dl):
        found = []
        for ds in (-1, 0, 1):
            for j in (0, 1):
                lj = j - 2 * dl + 1
                if 0 <= lj <= 3 and (ds, dl) != (0, 0):
                    found += remote(j, ds, dl, 1 - ds, lj)
        return found

    def incoming(dl):
        found = []
        for ds in (-1, 0, 1):
            for lj in {0: (1, 2), -1: (0,), 1: (3,)}[dl]:
                if (ds, dl) != (0, 0):
                    found += remote(0, ds, dl, 1 + ds, lj)
        return found

    own = [
        pltpu.make_async_copy(src, dst, own_sem.at[j, t])
        for j in (0, 1)
        for t, (src, dst) in enumerate(parts(j, 1, 1 + j))
    ]
    own += [
        pltpu.make_async_copy(src, dst, load_sem.at[t])
        for t, (src, dst) in enumerate(
            ((piece_hbm, piece), (route_hbm, route), (clump_hbm, clump))
        )
    ]
    for c in own:
        c.start()
    place.greet()
    place.meet()
    place.lateral(lambda dl: [c.start() for c in outgoing(dl)] and None)
    ext[:, :, 7] = jnp.zeros((3, 4, 8, 128), F32)

    @pl.when(place.l == 0)
    def _():
        ext[:, 0, 0:7] = jnp.zeros((3, 7, 8, 128), F32)

    @pl.when(place.l == n_lat - 1)
    def _():
        ext[:, 3, 0:7] = jnp.zeros((3, 7, 8, 128), F32)

    for c in own:
        c.wait()
    sub = lax.broadcasted_iota(jnp.int32, (8, 128), 0)
    every = one_hot(128, lax.broadcasted_iota(jnp.int32, (1, 128), 1))
    inside[...] = jnp.zeros((128, 128), F32)

    def cell(m):
        j, k = m // 8, m % 8
        mine = [ext[1, 1 + j, t, pl.ds(k, 1), :] for t in range(7)]
        mine[2] = mine[2] + (CELL_SIDE * k.astype(F32) - 20.0)
        own_table(mine, sub, tables.at[m])
        value = jnp.concatenate(mine + [mine[6]], 0)
        rows = lax.dot_general(every, keyed(value, sub), LANES, preferred_element_type=F32)
        zero = jnp.zeros((8, 128), F32)
        acc = (zero, zero, zero)
        for i in range(0, 128, CHUNK):
            acc = add_pairs(rows[i : i + CHUNK], tables.at[m], acc)
        for t in range(3):
            inside[pl.ds((j * 8 + t) * 8 + k, 1), :] = jnp.sum(acc[t], 0, keepdims=True)

    def cells(i, _):
        for t in range(4):
            cell(4 * i + t)
        return 0

    lax.fori_loop(0, 4, cells, 0)
    for m in range(16):
        hot_piece[:, m * 128 : m * 128 + 128] = one_hot(
            hot_piece.shape[0], piece[0, :, m * 128 : m * 128 + 128]
        )
    hot_clump[...] = one_hot(hot_clump.shape[0], clump[0])
    route_rows[...] = jnp.broadcast_to(route[0], route_rows.shape)
    place.lateral(lambda dl: [c.wait_recv() for c in incoming(dl)] and None)
    place.lateral(lambda dl: [c.wait_send() for c in outgoing(dl)] and None)


USUAL = {0: (128, 64, 64, 64), 1: (64, 24, 40, 24), 2: (32, 16, 24, 16)}
KEYS = 32
TERMS = 9


def kind(c):
    return (c // 3 != 1) + (c % 3 != 1)


def keyed(value, sub):
    radius = value[6:7]
    value = jnp.where(sub == 7, radius * radius * 0.0625, value)
    high = value.astype(BF16).astype(F32)
    rest = value - high
    middle = rest.astype(BF16).astype(F32)
    more = jnp.where(
        sub < 3,
        1.0,
        jnp.where(sub < 5, high[6:7], jnp.where(sub == 5, middle[6:7], 0.0)),
    )
    return jnp.concatenate([high, middle, rest - middle, more], 0).astype(BF16)


def own_table(own, sub, table):
    zero = jnp.zeros((8, 128), F32)

    def split(row):
        return [p.astype(F32) for p in split3(jnp.broadcast_to(row, (8, 128)))]

    def constants(row):
        high, middle, low = split(row)
        return jnp.where(sub == 0, high, jnp.where(sub == 1, middle, jnp.where(sub == 2, low, 0.0)))

    def put(t, same, more):
        block = jnp.concatenate([same, same, same, more], 0)
        table[:, t * 128 : t * 128 + 128] = block.astype(BF16)

    for t in range(7):
        put(t, jnp.where(sub == t, 1.0 if t == 6 else -1.0, zero), constants(own[t]))
    high, middle, low = split(4.0 * own[6])
    same = jnp.where(sub == 6, high, 0.0)
    more = jnp.where(sub == 4, low, jnp.where((sub == 3) | (sub == 5), middle, 0.0))
    put(7, same, more)
    put(
        8,
        jnp.where(sub == 7, 1.0, same * 0.03125),
        more * 0.03125 + constants(own[6] * own[6] * 0.0625),
    )


def pair_sums(pair, acc):
    dx, dy, dz, du, dv, dw, radii, product, least = pair
    square = dx * dx + dy * dy + dz * dz
    clamped = jnp.maximum(square, least)
    inverse = lax.rsqrt(clamped)
    delta = jnp.maximum(radii - clamped * inverse, 0.0)
    normal_speed = (du * dx + dv * dy + dw * dz) * inverse
    speed = du * du + dv * dv + dw * dw
    unit = square * (inverse * inverse)
    sliding = speed + normal_speed * normal_speed * (unit - 2.0)
    load = product * delta
    root = load * lax.rsqrt(jnp.maximum(load * radii, 1e-30))
    root2 = root * root
    cap = 2.5 * delta
    shear = root2 * cap * lax.rsqrt(jnp.maximum(root2 * (sliding + cap * cap), 0.0) + 1e-06)
    push = root * (cap + cap - normal_speed - 0.25)
    along = (push + shear * normal_speed) * inverse
    return (
        acc[0] + (along * dx - shear * du),
        acc[1] + (along * dy - shear * dv),
        acc[2] + (along * dz - shear * dw),
    )


def add_pairs(rows, table, acc):
    pairs = lax.dot_general(rows.astype(BF16), table[...], ROWS, preferred_element_type=F32)
    for g in range(0, rows.shape[0], 8):
        acc = pair_sums([pairs[g : g + 8, t * 128 : t * 128 + 128] for t in range(TERMS)], acc)
    return acc


def contact_kernel(
    lat_cells,
    phase,
    ext,
    inside,
    tables,
    off_hbm,
    angles_hbm,
    inertia_hbm,
    force,
    turning,
    off,
    angles,
    inertia,
    dest,
    count_v,
    count_s,
    bounds,
    picked,
    packed,
    copy_sem,
):
    loads = [
        pltpu.make_async_copy(src, dst, copy_sem.at[1 + t])
        for t, (src, dst) in enumerate(
            ((angles_hbm, angles), (inertia_hbm, inertia), (off_hbm, off))
        )
    ]
    for load in loads:
        load.start()
    sub = lax.broadcasted_iota(jnp.int32, (8, 128), 0)

    before = jnp.where(
        lax.broadcasted_iota(jnp.int32, (128, 128), 0)
        < lax.broadcasted_iota(jnp.int32, (128, 128), 1),
        1.0,
        0.0,
    ).astype(BF16)
    ones = jnp.ones((128, 128), BF16)
    for j in range(2):
        masks = []
        for c in range(9):
            di, dj = c // 3 - 1, c % 3 - 1
            base = ((1 + di) * 4 + 1 + j + dj) * 64
            x, y, z = (ext[base + 8 * t : base + 8 * t + 8, :] for t in range(3))
            radius = ext[base + 48 : base + 56, :]
            keep = radius > 0.0
            near = radius + REACH
            away = [v if d > 0 else CELL_SIDE - v for v, d in ((x, di), (y, dj)) if d]
            if len(away) == 1:
                keep &= away[0] < near
            if len(away) == 2:
                keep &= away[0] * away[0] + away[1] * away[1] < near * near
            low, high = z < near, CELL_SIDE - z < near
            kept = jnp.where(keep, 1.0, 0.0)
            low_f = jnp.where(low, kept, 0.0)
            high_f = jnp.where(high, kept, 0.0)
            mid_f = jnp.zeros((8, 128), F32) if c == 4 else kept - low_f - high_f
            masks += [low_f, mid_f, high_f]
        mask = jnp.concatenate(masks, 0).astype(BF16)
        prefix = lax.dot_general(mask, before, ROWS, preferred_element_type=F32)
        total = lax.dot_general(mask, ones, ROWS, preferred_element_type=F32)
        counts = lax.dot_general(ones[0:8], mask, LANES, preferred_element_type=F32)
        count_v[0:8, j * 256 : j * 256 + 216] = counts.astype(jnp.int32)
        over = jnp.full((8, 128), -1.0, F32)
        for c in range(9):
            a = c * 24
            low_p, mid_p, high_p = (prefix[a + 8 * t : a + 8 * t + 8] for t in range(3))
            low_n, mid_n, high_n = (total[a + 8 * t : a + 8 * t + 8] for t in range(3))
            spot = (
                masks[3 * c] * low_p
                + masks[3 * c + 1] * (low_n + mid_p)
                + masks[3 * c + 2] * (low_n + mid_n + high_p)
            )
            any_of = masks[3 * c] + masks[3 * c + 1] + masks[3 * c + 2]
            spot = jnp.where(any_of > 0.0, spot, -1.0).astype(jnp.int32)
            dest[(j * 9 + c) * 8 : (j * 9 + c) * 8 + 8, :] = spot
            sizes = (low_n + mid_n + high_n, low_n, mid_n, high_n)
            for size, usual in zip(sizes, USUAL[kind(c)]):
                over = jnp.maximum(over, size - usual)
        over = jnp.broadcast_to(jnp.max(over, 0, keepdims=True), (8, 128))
        count_v[8:16, j * 128 : j * 128 + 128] = over.astype(jnp.int32)
    copy = pltpu.make_async_copy(count_v, count_s, copy_sem.at[0])
    copy.start()

    angle = jnp.full((8, 128), phase[0].astype(F32) * (2.0 * math.pi / PHASES), F32)
    cos_b, sin_b = jnp.cos(angle), jnp.sin(angle)
    height_cells = 8
    centre_y, centre_z = 0.5 * CELL_SIDE * lat_cells, 0.5 * CELL_SIDE * height_cells
    reach = 0.45 * CELL_SIDE * min(lat_cells, height_cells)
    shaft_id = lax.axis_index("shaft").astype(F32)
    lat_id = (lax.axis_index("lat") * 2).astype(F32)
    up_id = sub.astype(F32)
    blade = []
    for j in range(2):
        base = (5 + j) * 64
        x, y, z = (ext[base + 8 * t : base + 8 * t + 8, :] for t in range(3))
        radius = ext[base + 48 : base + 56, :]
        x = CELL_SIDE * shaft_id + x
        y = CELL_SIDE * (lat_id + j) + y - centre_y
        z = CELL_SIDE * up_id + z - centre_z
        across = y * cos_b + z * sin_b
        radial = z * cos_b - y * sin_b
        depth = jnp.maximum(jnp.minimum(radius - across, radius + BLADE_THICKNESS + across), 0.0)
        window = jnp.maximum(radial * (reach - radial), 0.0) * (4.0 / (reach * reach))
        gate = jnp.maximum(jnp.cos(x * (2.0 * math.pi / (2.0 * CELL_SIDE))), 0.0)
        size = BLADE_STIFFNESS * depth * window * gate
        blade.append(size)

    loads[0].wait()
    loads[1].wait()
    n_clump = turning.shape[-1]
    cos_z, cos_y, cos_x = (jnp.cos(angles[t, 0]) for t in range(3))
    sin_z, sin_y, sin_x = (jnp.sin(angles[t, 0]) for t in range(3))
    rotation = [
        [
            cos_z * cos_y,
            cos_z * sin_y * sin_x - sin_z * cos_x,
            cos_z * sin_y * cos_x + sin_z * sin_x,
        ],
        [
            sin_z * cos_y,
            sin_z * sin_y * sin_x + cos_z * cos_x,
            sin_z * sin_y * cos_x - cos_z * sin_x,
        ],
        [-sin_y, cos_y * sin_x, cos_y * cos_x],
    ]
    for t, (a, b) in enumerate(((0, 0), (0, 1), (0, 2), (1, 1), (1, 2), (2, 2))):
        turning[t : t + 1, :] = TIME_STEP * sum(
            rotation[a][i] * inertia[i, 0] * rotation[b][i] for i in range(3)
        )
    turning[6:8, :] = jnp.zeros((2, n_clump), F32)
    lane = lax.broadcasted_iota(jnp.int32, (32, 128), 1)
    inert = jnp.where((lane >= 24) & (lane < 27), 1.0, 0.0)
    for j in range(2):

        def count(c, t, k):
            return count_s[0, j * 256 + (c * 3 + t) * 8 + k]

        def pick(c, k, rows, into):
            di, dj = c // 3 - 1, c % 3 - 1
            base = ((1 + di) * 4 + 1 + j + dj) * 64
            rise = CELL_SIDE * k.astype(F32) - 20.0
            shift = jnp.where(
                sub == 0,
                CELL_SIDE * di,
                jnp.where(sub == 1, CELL_SIDE * dj, jnp.where(sub == 2, rise, 0.0)),
            )
            value = ext[pl.ds(base + k, 8, stride=8), :] + shift
            spot = dest[pl.ds((j * 9 + c) * 8 + k, 1), :]
            keys = jnp.concatenate([keyed(value, sub), jnp.zeros((128 - KEYS, 128), BF16)], 0)
            into[k, 0:rows, :] = lax.dot_general(
                one_hot(rows, spot), keys, LANES, preferred_element_type=F32
            )

        sides = [c for c in range(9) if c != 4]

        def pick_some(i, _):
            for k in (4 * i, 4 * i + 1, 4 * i + 2, 4 * i + 3):
                for c in range(9):
                    pick(c, k, USUAL[kind(c)][0], picked.at[c])
            return 0

        lax.fori_loop(0, 2, pick_some, 0)
        if j == 0:
            copy.wait()

        def gather_level(k, offset, sizes):
            for t in range(3):
                start_of_part = offset
                if t == 2:
                    bounds[0, k] = offset
                for c in sides:
                    start = 0 if t == 0 else count(c, 0, k)
                    if t == 2:
                        start = start + count(c, 1, k)
                    length = sizes[kind(c)][1 + t]
                    packed[pl.ds(offset, length), :] = picked[c, k, pl.ds(start, length), :]
                    offset = offset + count(c, t, k)
                if t == 0:
                    bounds[1, k] = offset
                if t == 1:
                    packed[pl.ds(offset, 32), :] = inert
                    offset = jnp.maximum(offset, start_of_part + 32)
                    below, above = (k + 7) % 8, (k + 1) % 8
                    length = sizes[0][1]
                    start = count(4, 0, below)
                    packed[pl.ds(offset, length), :] = picked[4, below, pl.ds(start, length), :]
                    offset = offset + jnp.where(k > 0, count(4, 2, below), 0)
                    packed[pl.ds(offset, length), :] = picked[4, above, pl.ds(0, length), :]
                    offset = offset + jnp.where(k < 7, count(4, 0, above), 0)
                    packed[pl.ds(offset, 8), :] = inert[0:8]
                    offset = (offset + 7) // 8 * 8
            return offset

        def gather_usual():
            offset = 0
            for k in range(8):
                offset = gather_level(k, offset, USUAL)
            return offset

        def gather_any():
            def level(k, offset):
                for c in sides:
                    pick(c, k, 128, picked.at[c])
                return gather_level(k, offset, {t: (128,) * 4 for t in range(3)})

            return lax.fori_loop(0, 8, level, jnp.int32(0))

        end = lax.cond(count_s[8, j * 128] > 0, gather_any, gather_usual)
        packed[pl.ds(end, 32), :] = inert
        bounds[1, 8] = end

        def cell(k, _):
            first = jnp.where(k == 0, 0, bounds[0, jnp.maximum(k - 1, 0)])
            last = bounds[1, k + 1]
            table = tables.at[j * 8 + k]

            parts = (last - first + 31) // 32
            sums = (jnp.zeros((8, 128), F32),) * 3
            for size, times in ((128, parts // 4), (64, parts % 4 // 2), (32, parts % 2 // 1)):

                def chunk(i, acc, size=size):
                    at = pl.multiple_of(first + i * size, 8)
                    return add_pairs(packed[pl.ds(at, size), 0:KEYS], table, acc)

                sums = lax.fori_loop(0, times, chunk, sums)
                first = first + times * size
            for t in range(3):
                force[pl.ds((j * 8 + t) * 8 + k, 1), :] = jnp.sum(sums[t], 0, keepdims=True)
            return 0

        lax.fori_loop(0, 8, cell, 0)

    loads[2].wait()
    for j in range(2):
        fx, fy, fz = (
            force[(j * 8 + t) * 8 : (j * 8 + t) * 8 + 8, :]
            + inside[(j * 8 + t) * 8 : (j * 8 + t) * 8 + 8, :]
            for t in range(3)
        )
        fy, fz = fy + blade[j] * cos_b, fz + blade[j] * sin_b
        ox, oy, oz = (off[t, 0, j] for t in range(3))
        six = [fx, fy, fz, oy * fz - oz * fy, oz * fx - ox * fz, ox * fy - oy * fx]
        for t in range(8):
            force[(j * 8 + t) * 8 : (j * 8 + t) * 8 + 8, :] = (
                six[t] if t < 6 else jnp.zeros((8, 128), F32)
            )


def exchange_kernel(
    n_shaft,
    n_lat,
    force,
    hot_piece,
    hot_clump,
    route_rows,
    turning,
    motion_hbm,
    inverse_mass_hbm,
    table,
    motion,
    inverse_mass,
    part,
    got,
    send_sem,
    recv_sem,
    load_sem,
):
    place = Place(n_shaft, n_lat)
    n_clump = turning.shape[-1]
    place.greet()
    loads = [
        pltpu.make_async_copy(motion_hbm, motion, load_sem.at[0]),
        pltpu.make_async_copy(inverse_mass_hbm, inverse_mass, load_sem.at[1]),
    ]
    for load in loads:
        load.start()

    def sums_copy(ds, dl, slot):
        c = (ds + 1) * 3 + dl + 1
        return pltpu.make_async_remote_copy(
            src_ref=part.at[c],
            dst_ref=got.at[slot],
            send_sem=send_sem.at[0, slot],
            recv_sem=recv_sem.at[0, slot],
            device_id=place.at(ds, dl),
            device_id_type=MESH,
        )

    def table_copy(ds, dl, slot):
        return pltpu.make_async_remote_copy(
            src_ref=table.at[4],
            dst_ref=table.at[slot],
            send_sem=send_sem.at[1, slot],
            recv_sem=recv_sem.at[1, slot],
            device_id=place.at(ds, dl),
            device_id_type=MESH,
        )

    def around(act, dl):
        for ds in (-1, 0, 1):
            if (ds, dl) != (0, 0):
                act(ds, dl)

    terms = [
        rows3(force[pl.ds(j * 64 + k, 8, stride=8), :]).astype(BF16) for j in range(2) for k in range(8)
    ]
    sums = lax.dot_general(
        jnp.concatenate(terms, 1), hot_piece[...], LANES, preferred_element_type=F32
    )
    sums = rows3(sum3(sums))
    route = jnp.concatenate([route_rows[...]] * 3, 0)
    routed = jnp.concatenate([jnp.where(route == c, sums, 0.0) for c in range(9)], 0)
    sums = lax.dot_general(
        routed.astype(BF16), hot_clump[...], LANES, preferred_element_type=F32
    )
    for c in range(9):
        part[c] = sum3(sums[24 * c : 24 * c + 24])

    def clear(edge, column):
        @pl.when(place.l == edge)
        def _():
            for row in range(3):
                table[row * 3 + column] = jnp.zeros((8, n_clump), F32)
                got[row * 3 + 2 - column] = jnp.zeros((8, n_clump), F32)

    clear(0, 0)
    clear(n_lat - 1, 2)
    place.meet()
    place.lateral(
        lambda dl: around(lambda ds, d: sums_copy(ds, d, (ds + 1) * 3 + d + 1).start(), dl)
    )
    for load in loads:
        load.wait()
    place.lateral(
        lambda dl: around(lambda ds, d: sums_copy(ds, d, 8 - (ds + 1) * 3 - d - 1).wait_recv(), dl)
    )
    sums = part[4]
    for c in range(9):
        if c != 4:
            sums = sums + got[c]
    rows = []
    for t in range(3):
        pull = -GRAVITY if t == 2 else 0.0
        rows.append(motion[t, 0] + TIME_STEP * (inverse_mass[0] * sums[t : t + 1] + pull))
    torque = [sums[3 + t : 4 + t] for t in range(3)]
    order = ((0, 1, 2), (1, 3, 4), (2, 4, 5))
    for t in range(3):
        change = sum(turning[order[t][i] : order[t][i] + 1, :] * torque[i] for i in range(3))
        rows.append(motion[3 + t, 0] + change)
    table[4] = jnp.concatenate(rows + [jnp.zeros((2, n_clump), F32)], 0)
    place.lateral(
        lambda dl: around(lambda ds, d: table_copy(ds, d, 8 - (ds + 1) * 3 - d - 1).start(), dl)
    )
    place.lateral(
        lambda dl: around(lambda ds, d: table_copy(ds, d, (ds + 1) * 3 + d + 1).wait_recv(), dl)
    )
    place.lateral(
        lambda dl: around(lambda ds, d: sums_copy(ds, d, (ds + 1) * 3 + d + 1).wait_send(), dl)
    )
    place.lateral(
        lambda dl: around(lambda ds, d: table_copy(ds, d, 8 - (ds + 1) * 3 - d - 1).wait_send(), dl)
    )


def spread_kernel(
    table,
    hot_piece,
    hot_clump,
    route_rows,
    centre_hbm,
    off_hbm,
    clump_hbm,
    sphere_hbm,
    centre,
    off,
    clump_out,
    sphere_out,
    pose,
    sem,
):
    loads = [
        pltpu.make_async_copy(centre_hbm, centre, sem.at[0]),
        pltpu.make_async_copy(off_hbm, off, sem.at[1]),
    ]
    for load in loads:
        load.start()
    tables = jnp.concatenate([rows3(table[c]) for c in range(9)], 0).astype(BF16)
    found = lax.dot_general(tables, hot_clump[...], ROWS, preferred_element_type=F32)
    route = jnp.concatenate([route_rows[...]] * 3, 0)
    by_piece = found[0:24]
    for c in range(1, 9):
        by_piece = jnp.where(route == c, found[24 * c : 24 * c + 24], by_piece)
    by_sphere = sum3(
        lax.dot_general(by_piece.astype(BF16), hot_piece[...], ROWS, preferred_element_type=F32)
    )
    loads[0].wait()
    for t in range(6):
        row = table[4, t : t + 1, :]
        if t < 3:
            clump_out[t, 0] = centre[t, 0] + TIME_STEP * row
        clump_out[3 + t, 0] = row
    stores = [pltpu.make_async_copy(clump_out, clump_hbm, sem.at[2])]
    stores[0].start()
    for m in range(16):
        pose[m * 8 : m * 8 + 8, :] = by_sphere[:, m * 128 : m * 128 + 128]
    loads[1].wait()
    for j in range(2):
        vx, vy, vz, sx, sy, sz = (
            pose[pl.ds(j * 64 + t, 8, stride=8), :] for t in range(6)
        )
        bx, by, bz = (off[t, 0, j] for t in range(3))
        hx, hy, hz = (0.5 * TIME_STEP * s for s in (sx, sy, sz))
        scale = 2.0 / (1.0 + (hx * hx + hy * hy + hz * hz))
        cx, cy, cz = hy * bz - hz * by, hz * bx - hx * bz, hx * by - hy * bx
        tx = bx + scale * (cx + hy * cz - hz * cy)
        ty = by + scale * (cy + hz * cx - hx * cz)
        tz = bz + scale * (cz + hx * cy - hy * cx)
        sphere_out[0, 0, j], sphere_out[1, 0, j], sphere_out[2, 0, j] = tx, ty, tz
        sphere_out[3, 0, j] = vx + (sy * tz - sz * ty)
        sphere_out[4, 0, j] = vy + (sz * tx - sx * tz)
        sphere_out[5, 0, j] = vz + (sx * ty - sy * tx)
        stores.append(
            pltpu.make_async_copy(
                sphere_out.at[:, :, pl.ds(j, 1)], sphere_hbm.at[:, :, pl.ds(j, 1)], sem.at[3 + j]
            )
        )
        stores[-1].start()
    for store in stores:
        store.wait()


def contact_call(lat_cells, blade_phase, ext, inside, tables, off, angles, inertia, **extra):
    n_clump = angles.shape[-1]
    return pl.pallas_call(
        functools.partial(contact_kernel, lat_cells),
        out_shape=(
            jax.ShapeDtypeStruct((128, 128), F32),
            jax.ShapeDtypeStruct((8, n_clump), F32),
        ),
        in_specs=[SMEM] + [VMEM] * 3 + [HBM] * 3,
        out_specs=(VMEM, VMEM),
        scratch_shapes=[
            pltpu.VMEM(off.shape, F32),
            pltpu.VMEM(angles.shape, F32),
            pltpu.VMEM(inertia.shape, F32),
            pltpu.VMEM((144, 128), jnp.int32),
            pltpu.VMEM((16, 512), jnp.int32),
            pltpu.SMEM((16, 512), jnp.int32),
            pltpu.SMEM((2, 16), jnp.int32),
            pltpu.VMEM((9, 8, 256, 128), F32),
            pltpu.VMEM((9 * 1024 + 8 * 72 + 256, 128), F32),
            pltpu.SemaphoreType.DMA((4,)),
        ],
        compiler_params=pltpu.CompilerParams(vmem_limit_bytes=24 << 20),
        name="contact",
        **extra,
    )(blade_phase, ext, inside, tables, off, angles, inertia)


def on_device(
    n_shaft,
    n_lat,
    sphere_position,
    sphere_velocity,
    sphere_radius,
    sphere_offset,
    sphere_piece,
    piece_route,
    piece_clump,
    blade_phase,
    clump_centre,
    clump_motion,
    clump_angles,
    clump_inverse_mass,
    clump_inverse_inertia,
):
    n_piece, n_clump = piece_route.shape[-1], clump_angles.shape[-1]
    sphere_position, sphere_velocity, sphere_radius, sphere_piece, piece_route, piece_clump = (
        pltpu.with_memory_space_constraint(v, pltpu.HBM)
        for v in (
            sphere_position,
            sphere_velocity,
            sphere_radius,
            sphere_piece,
            piece_route,
            piece_clump,
        )
    )
    sphere_offset, clump_centre, clump_motion = (
        pltpu.with_memory_space_constraint(v, pltpu.HBM)
        for v in (sphere_offset, clump_centre, clump_motion)
    )
    clump_angles, clump_inverse_mass, clump_inverse_inertia = (
        pltpu.with_memory_space_constraint(v, pltpu.HBM)
        for v in (clump_angles, clump_inverse_mass, clump_inverse_inertia)
    )
    ext, hot_piece, hot_clump, route_rows, inside, tables = pl.pallas_call(
        functools.partial(halo_kernel, n_shaft, n_lat),
        out_shape=(
            jax.ShapeDtypeStruct((3, 4, 8, 8, 128), F32),
            jax.ShapeDtypeStruct((n_piece, 2048), BF16),
            jax.ShapeDtypeStruct((n_clump, n_piece), BF16),
            jax.ShapeDtypeStruct((8, n_piece), jnp.int32),
            jax.ShapeDtypeStruct((128, 128), F32),
            jax.ShapeDtypeStruct((16, KEYS, TERMS * 128), BF16),
        ),
        in_specs=[HBM] * 6,
        out_specs=(VMEM,) * 6,
        scratch_shapes=[
            pltpu.VMEM(sphere_piece.shape, jnp.int32),
            pltpu.VMEM(piece_route.shape, jnp.int32),
            pltpu.VMEM(piece_clump.shape, jnp.int32),
            pltpu.SemaphoreType.DMA((3, 4, 3)),
            pltpu.SemaphoreType.DMA((3, 4, 3)),
            pltpu.SemaphoreType.DMA((2, 3)),
            pltpu.SemaphoreType.DMA((3,)),
        ],
        compiler_params=pltpu.CompilerParams(
            collective_id=0, has_side_effects=True, vmem_limit_bytes=16 << 20
        ),
        name="halo",
    )(
        sphere_position,
        sphere_velocity,
        sphere_radius,
        sphere_piece,
        piece_route,
        piece_clump,
    )
    force, turning = contact_call(
        2 * n_lat,
        blade_phase,
        ext.reshape(768, 128),
        inside,
        tables,
        sphere_offset,
        clump_angles,
        clump_inverse_inertia,
    )
    table = pl.pallas_call(
        functools.partial(exchange_kernel, n_shaft, n_lat),
        out_shape=jax.ShapeDtypeStruct((9, 8, n_clump), F32),
        in_specs=[VMEM] * 5 + [HBM] * 2,
        out_specs=VMEM,
        scratch_shapes=[
            pltpu.VMEM(clump_motion.shape, F32),
            pltpu.VMEM(clump_inverse_mass.shape, F32),
            pltpu.VMEM((9, 8, n_clump), F32),
            pltpu.VMEM((9, 8, n_clump), F32),
            pltpu.SemaphoreType.DMA((2, 9)),
            pltpu.SemaphoreType.DMA((2, 9)),
            pltpu.SemaphoreType.DMA((2,)),
        ],
        compiler_params=pltpu.CompilerParams(
            collective_id=1, has_side_effects=True, vmem_limit_bytes=16 << 20
        ),
        name="exchange",
    )(force, hot_piece, hot_clump, route_rows, turning, clump_motion, clump_inverse_mass)
    return pl.pallas_call(
        spread_kernel,
        out_shape=(
            jax.ShapeDtypeStruct((9, 1, 1, n_clump), F32),
            jax.ShapeDtypeStruct((6, 1, 2, 8, 128), F32),
        ),
        in_specs=[VMEM] * 4 + [HBM] * 2,
        out_specs=(HBM, HBM),
        scratch_shapes=[
            pltpu.VMEM(clump_centre.shape, F32),
            pltpu.VMEM(sphere_offset.shape, F32),
            pltpu.VMEM((9, 1, 1, n_clump), F32),
            pltpu.VMEM((6, 1, 2, 8, 128), F32),
            pltpu.VMEM((128, 128), F32),
            pltpu.SemaphoreType.DMA((5,)),
        ],
        compiler_params=pltpu.CompilerParams(vmem_limit_bytes=16 << 20),
        name="spread",
    )(table, hot_piece, hot_clump, route_rows, clump_centre, sphere_offset)


def solution(mesh):
    placed = (
        P(None, "shaft", "lat", None, None),
        P(None, "shaft", "lat", None, None),
        P("shaft", "lat", None, None),
        P(None, "shaft", "lat", None, None),
        P("shaft", "lat", None),
        P("shaft", "lat", None),
        P("shaft", "lat", None),
        P(),
        P(None, "shaft", "lat", None),
        P(None, "shaft", "lat", None),
        P(None, "shaft", "lat", None),
        P("shaft", "lat", None),
        P(None, "shaft", "lat", None),
    )
    return jax.shard_map(
        functools.partial(on_device, mesh.shape["shaft"], mesh.shape["lat"]),
        mesh=mesh,
        in_specs=placed,
        out_specs=(P(None, "shaft", "lat", None), P(None, "shaft", "lat", None, None)),
        check_vma=False,
    )
```

```python
import functools
import math

import jax
import jax.numpy as jnp
from jax import lax
from jax.experimental import pallas as pl
from jax.experimental.pallas import tpu as pltpu
from jax.sharding import PartitionSpec as P

PHASES = 64
CELL_SIDE = 5.0
BLADE_STIFFNESS = 20.0
BLADE_THICKNESS = 1.0
TIME_STEP = 0.5
GRAVITY = 0.5

REACH = 0.6001
CHUNK = 64
F32 = jnp.float32
BF16 = jnp.bfloat16
MESH = pl.DeviceIdType.MESH
LANES = (((1,), (1,)), ((), ()))
ROWS = (((1,), (0,)), ((), ()))
VMEM = pl.BlockSpec(memory_space=pltpu.VMEM)
SMEM = pl.BlockSpec(memory_space=pltpu.SMEM)
HBM = pl.BlockSpec(memory_space=pltpu.HBM)


def split3(x):
    high = x.astype(BF16)
    rest = x - high.astype(F32)
    middle = rest.astype(BF16)
    low = (rest - middle.astype(F32)).astype(BF16)
    return high, middle, low


def rows3(x):
    high = x.astype(BF16).astype(F32)
    rest = x - high
    middle = rest.astype(BF16).astype(F32)
    return jnp.concatenate([high, middle, rest - middle], 0)


def sum3(x):
    return x[0:8] + x[8:16] + x[16:24]


def one_hot(rows, row):
    length = row.shape[-1]
    ids = lax.broadcasted_iota(jnp.int16, (rows, length), 0)
    return jnp.where(ids == row.astype(jnp.int16), jnp.ones((), BF16), jnp.zeros((), BF16))


class Place:
    def __init__(self, n_shaft, n_lat):
        self.n_shaft, self.n_lat = n_shaft, n_lat
        self.s, self.l = lax.axis_index("shaft"), lax.axis_index("lat")

    def at(self, ds, dl):
        return {"shaft": lax.rem(self.s + ds + self.n_shaft, self.n_shaft), "lat": self.l + dl}

    def lateral(self, act):
        pl.when(self.l > 0)(lambda: act(-1))
        pl.when(self.l < self.n_lat - 1)(lambda: act(1))
        act(0)

    def greet(self):
        sem = pltpu.get_barrier_semaphore()

        def signal(dl):
            for ds in (-1, 0, 1):
                if (ds, dl) != (0, 0):
                    pl.semaphore_signal(
                        sem, inc=1, device_id=self.at(ds, dl), device_id_type=MESH
                    )

        self.lateral(signal)

    def meet(self):
        sem = pltpu.get_barrier_semaphore()
        edge = jnp.logical_or(self.l == 0, self.l == self.n_lat - 1)
        pl.semaphore_wait(sem, jnp.where(edge, 5, 8))


def halo_kernel(
    n_shaft,
    n_lat,
    pos,
    vel,
    rad,
    piece_hbm,
    route_hbm,
    clump_hbm,
    ext,
    hot_piece,
    hot_clump,
    route_rows,
    inside,
    tables,
    piece,
    route,
    clump,
    send_sem,
    recv_sem,
    own_sem,
    load_sem,
):
    place = Place(n_shaft, n_lat)

    def parts(j, si, lj):
        return (
            (pos.at[:, 0, j], ext.at[si, lj, 0:3]),
            (vel.at[:, 0, j], ext.at[si, lj, 3:6]),
            (rad.at[0, pl.ds(j, 1)], ext.at[si, lj, 6:7]),
        )

    def remote(j, ds, dl, si, lj):
        return [
            pltpu.make_async_remote_copy(
                src_ref=src,
                dst_ref=dst,
                send_sem=send_sem.at[si, lj, t],
                recv_sem=recv_sem.at[si, lj, t],
                device_id=place.at(ds, dl),
                device_id_type=MESH,
            )
            for t, (src, dst) in enumerate(parts(j, si, lj))
        ]

    def outgoing(dl):
        found = []
        for ds in (-1, 0, 1):
            for j in (0, 1):
                lj = j - 2 * dl + 1
                if 0 <= lj <= 3 and (ds, dl) != (0, 0):
                    found += remote(j, ds, dl, 1 - ds, lj)
        return found

    def incoming(dl):
        found = []
        for ds in (-1, 0, 1):
            for lj in {0: (1, 2), -1: (0,), 1: (3,)}[dl]:
                if (ds, dl) != (0, 0):
                    found += remote(0, ds, dl, 1 + ds, lj)
        return found

    own = [
        pltpu.make_async_copy(src, dst, own_sem.at[j, t])
        for j in (0, 1)
        for t, (src, dst) in enumerate(parts(j, 1, 1 + j))
    ]
    own += [
        pltpu.make_async_copy(src, dst, load_sem.at[t])
        for t, (src, dst) in enumerate(
            ((piece_hbm, piece), (route_hbm, route), (clump_hbm, clump))
        )
    ]
    for c in own:
        c.start()
    place.greet()
    place.meet()
    place.lateral(lambda dl: [c.start() for c in outgoing(dl)] and None)
    ext[:, :, 7] = jnp.zeros((3, 4, 8, 128), F32)

    @pl.when(place.l == 0)
    def _():
        ext[:, 0, 0:7] = jnp.zeros((3, 7, 8, 128), F32)

    @pl.when(place.l == n_lat - 1)
    def _():
        ext[:, 3, 0:7] = jnp.zeros((3, 7, 8, 128), F32)

    for c in own:
        c.wait()
    sub = lax.broadcasted_iota(jnp.int32, (8, 128), 0)
    every = one_hot(128, lax.broadcasted_iota(jnp.int32, (1, 128), 1))
    inside[...] = jnp.zeros((128, 128), F32)

    def cell(m):
        j, k = m // 8, m % 8
        mine = [ext[1, 1 + j, t, pl.ds(k, 1), :] for t in range(7)]
        mine[2] = mine[2] + (CELL_SIDE * k.astype(F32) - 20.0)
        own_table(mine, sub, tables.at[m])
        value = jnp.concatenate(mine + [mine[6]], 0)
        rows = lax.dot_general(every, keyed(value, sub), LANES, preferred_element_type=F32)
        zero = jnp.zeros((8, 128), F32)
        acc = (zero, zero, zero)
        for i in range(0, 128, CHUNK):
            acc = add_pairs(rows[i : i + CHUNK], tables.at[m], acc)
        for t in range(3):
            inside[pl.ds((j * 8 + t) * 8 + k, 1), :] = jnp.sum(acc[t], 0, keepdims=True)

    def cells(i, _):
        for t in range(4):
            cell(4 * i + t)
        return 0

    lax.fori_loop(0, 4, cells, 0)
    for m in range(16):
        hot_piece[:, m * 128 : m * 128 + 128] = one_hot(
            hot_piece.shape[0], piece[0, :, m * 128 : m * 128 + 128]
        )
    hot_clump[...] = one_hot(hot_clump.shape[0], clump[0])
    route_rows[...] = jnp.broadcast_to(route[0], route_rows.shape)
    place.lateral(lambda dl: [c.wait_recv() for c in incoming(dl)] and None)
    place.lateral(lambda dl: [c.wait_send() for c in outgoing(dl)] and None)


USUAL = {0: (128, 64, 64, 64), 1: (64, 24, 40, 24), 2: (32, 16, 24, 16)}
KEYS = 32
TERMS = 9


def kind(c):
    return (c // 3 != 1) + (c % 3 != 1)


def keyed(value, sub):
    radius = value[6:7]
    value = jnp.where(sub == 7, radius * radius * 0.0625, value)
    high = value.astype(BF16).astype(F32)
    rest = value - high
    middle = rest.astype(BF16).astype(F32)
    more = jnp.where(
        sub < 3,
        1.0,
        jnp.where(sub < 5, high[6:7], jnp.where(sub == 5, middle[6:7], 0.0)),
    )
    return jnp.concatenate([high, middle, rest - middle, more], 0).astype(BF16)


def own_table(own, sub, table):
    zero = jnp.zeros((8, 128), F32)

    def split(row):
        return [p.astype(F32) for p in split3(jnp.broadcast_to(row, (8, 128)))]

    def constants(row):
        high, middle, low = split(row)
        return jnp.where(sub == 0, high, jnp.where(sub == 1, middle, jnp.where(sub == 2, low, 0.0)))

    def put(t, same, more):
        block = jnp.concatenate([same, same, same, more], 0)
        table[:, t * 128 : t * 128 + 128] = block.astype(BF16)

    for t in range(7):
        put(t, jnp.where(sub == t, 1.0 if t == 6 else -1.0, zero), constants(own[t]))
    high, middle, low = split(4.0 * own[6])
    same = jnp.where(sub == 6, high, 0.0)
    more = jnp.where(sub == 4, low, jnp.where((sub == 3) | (sub == 5), middle, 0.0))
    put(7, same, more)
    put(
        8,
        jnp.where(sub == 7, 1.0, same * 0.03125),
        more * 0.03125 + constants(own[6] * own[6] * 0.0625),
    )


def pair_sums(pair, acc):
    dx, dy, dz, du, dv, dw, radii, product, least = pair
    square = dx * dx + dy * dy + dz * dz
    clamped = jnp.maximum(square, least)
    inverse = lax.rsqrt(clamped)
    delta = jnp.maximum(radii - clamped * inverse, 0.0)
    normal_speed = (du * dx + dv * dy + dw * dz) * inverse
    speed = du * du + dv * dv + dw * dw
    unit = square * (inverse * inverse)
    sliding = speed + normal_speed * normal_speed * (unit - 2.0)
    load = product * delta
    root = load * lax.rsqrt(jnp.maximum(load * radii, 1e-30))
    root2 = root * root
    cap = 2.5 * delta
    shear = root2 * cap * lax.rsqrt(jnp.maximum(root2 * (sliding + cap * cap), 0.0) + 1e-06)
    push = root * (cap + cap - normal_speed - 0.25)
    along = (push + shear * normal_speed) * inverse
    return (
        acc[0] + (along * dx - shear * du),
        acc[1] + (along * dy - shear * dv),
        acc[2] + (along * dz - shear * dw),
    )


def add_pairs(rows, table, acc):
    pairs = lax.dot_general(rows.astype(BF16), table[...], ROWS, preferred_element_type=F32)
    for g in range(0, rows.shape[0], 8):
        acc = pair_sums([pairs[g : g + 8, t * 128 : t * 128 + 128] for t in range(TERMS)], acc)
    return acc


def contact_kernel(
    lat_cells,
    phase,
    ext,
    inside,
    tables,
    off_hbm,
    angles_hbm,
    inertia_hbm,
    force,
    turning,
    off,
    angles,
    inertia,
    dest,
    count_v,
    count_s,
    bounds,
    picked,
    packed,
    copy_sem,
):
    loads = [
        pltpu.make_async_copy(src, dst, copy_sem.at[1 + t])
        for t, (src, dst) in enumerate(
            ((angles_hbm, angles), (inertia_hbm, inertia), (off_hbm, off))
        )
    ]
    for load in loads:
        load.start()
    sub = lax.broadcasted_iota(jnp.int32, (8, 128), 0)

    before = jnp.where(
        lax.broadcasted_iota(jnp.int32, (128, 128), 0)
        < lax.broadcasted_iota(jnp.int32, (128, 128), 1),
        1.0,
        0.0,
    ).astype(BF16)
    ones = jnp.ones((128, 128), BF16)
    for j in range(2):
        masks = []
        for c in range(9):
            di, dj = c // 3 - 1, c % 3 - 1
            base = ((1 + di) * 4 + 1 + j + dj) * 64
            x, y, z = (ext[base + 8 * t : base + 8 * t + 8, :] for t in range(3))
            radius = ext[base + 48 : base + 56, :]
            keep = radius > 0.0
            near = radius + REACH
            away = [v if d > 0 else CELL_SIDE - v for v, d in ((x, di), (y, dj)) if d]
            up, square = CELL_SIDE - z, near * near
            low, high = z < near, up < near
            if away:
                flat = sum(v * v for v in away)
                keep &= flat < square
                low, high = flat + z * z < square, flat + up * up < square
            kept = jnp.where(keep, 1.0, 0.0)
            low_f = jnp.where(low, kept, 0.0)
            high_f = jnp.where(high, kept, 0.0)
            mid_f = jnp.zeros((8, 128), F32) if c == 4 else kept - low_f - high_f
            masks += [low_f, mid_f, high_f]
        mask = jnp.concatenate(masks, 0).astype(BF16)
        prefix = lax.dot_general(mask, before, ROWS, preferred_element_type=F32)
        total = lax.dot_general(mask, ones, ROWS, preferred_element_type=F32)
        counts = lax.dot_general(ones[0:8], mask, LANES, preferred_element_type=F32)
        count_v[0:8, j * 256 : j * 256 + 216] = counts.astype(jnp.int32)
        over = jnp.full((8, 128), -1.0, F32)
        for c in range(9):
            a = c * 24
            low_p, mid_p, high_p = (prefix[a + 8 * t : a + 8 * t + 8] for t in range(3))
            low_n, mid_n, high_n = (total[a + 8 * t : a + 8 * t + 8] for t in range(3))
            spot = (
                masks[3 * c] * low_p
                + masks[3 * c + 1] * (low_n + mid_p)
                + masks[3 * c + 2] * (low_n + mid_n + high_p)
            )
            any_of = masks[3 * c] + masks[3 * c + 1] + masks[3 * c + 2]
            spot = jnp.where(any_of > 0.0, spot, -1.0).astype(jnp.int32)
            dest[(j * 9 + c) * 8 : (j * 9 + c) * 8 + 8, :] = spot
            sizes = (low_n + mid_n + high_n, low_n, mid_n, high_n)
            for size, usual in zip(sizes, USUAL[kind(c)]):
                over = jnp.maximum(over, size - usual)
        over = jnp.broadcast_to(jnp.max(over, 0, keepdims=True), (8, 128))
        count_v[8:16, j * 128 : j * 128 + 128] = over.astype(jnp.int32)
    copy = pltpu.make_async_copy(count_v, count_s, copy_sem.at[0])
    copy.start()

    angle = jnp.full((8, 128), phase[0].astype(F32) * (2.0 * math.pi / PHASES), F32)
    cos_b, sin_b = jnp.cos(angle), jnp.sin(angle)
    height_cells = 8
    centre_y, centre_z = 0.5 * CELL_SIDE * lat_cells, 0.5 * CELL_SIDE * height_cells
    reach = 0.45 * CELL_SIDE * min(lat_cells, height_cells)
    shaft_id = lax.axis_index("shaft").astype(F32)
    lat_id = (lax.axis_index("lat") * 2).astype(F32)
    up_id = sub.astype(F32)
    blade = []
    for j in range(2):
        base = (5 + j) * 64
        x, y, z = (ext[base + 8 * t : base + 8 * t + 8, :] for t in range(3))
        radius = ext[base + 48 : base + 56, :]
        x = CELL_SIDE * shaft_id + x
        y = CELL_SIDE * (lat_id + j) + y - centre_y
        z = CELL_SIDE * up_id + z - centre_z
        across = y * cos_b + z * sin_b
        radial = z * cos_b - y * sin_b
        depth = jnp.maximum(jnp.minimum(radius - across, radius + BLADE_THICKNESS + across), 0.0)
        window = jnp.maximum(radial * (reach - radial), 0.0) * (4.0 / (reach * reach))
        gate = jnp.maximum(jnp.cos(x * (2.0 * math.pi / (2.0 * CELL_SIDE))), 0.0)
        size = BLADE_STIFFNESS * depth * window * gate
        blade.append(size)

    loads[0].wait()
    loads[1].wait()
    n_clump = turning.shape[-1]
    cos_z, cos_y, cos_x = (jnp.cos(angles[t, 0]) for t in range(3))
    sin_z, sin_y, sin_x = (jnp.sin(angles[t, 0]) for t in range(3))
    rotation = [
        [
            cos_z * cos_y,
            cos_z * sin_y * sin_x - sin_z * cos_x,
            cos_z * sin_y * cos_x + sin_z * sin_x,
        ],
        [
            sin_z * cos_y,
            sin_z * sin_y * sin_x + cos_z * cos_x,
            sin_z * sin_y * cos_x - cos_z * sin_x,
        ],
        [-sin_y, cos_y * sin_x, cos_y * cos_x],
    ]
    for t, (a, b) in enumerate(((0, 0), (0, 1), (0, 2), (1, 1), (1, 2), (2, 2))):
        turning[t : t + 1, :] = TIME_STEP * sum(
            rotation[a][i] * inertia[i, 0] * rotation[b][i] for i in range(3)
        )
    turning[6:8, :] = jnp.zeros((2, n_clump), F32)
    lane = lax.broadcasted_iota(jnp.int32, (32, 128), 1)
    inert = jnp.where((lane >= 24) & (lane < 27), 1.0, 0.0)
    for j in range(2):

        def count(c, t, k):
            return count_s[0, j * 256 + (c * 3 + t) * 8 + k]

        def pick(c, k, rows, into):
            di, dj = c // 3 - 1, c % 3 - 1
            base = ((1 + di) * 4 + 1 + j + dj) * 64
            rise = CELL_SIDE * k.astype(F32) - 20.0
            shift = jnp.where(
                sub == 0,
                CELL_SIDE * di,
                jnp.where(sub == 1, CELL_SIDE * dj, jnp.where(sub == 2, rise, 0.0)),
            )
            value = ext[pl.ds(base + k, 8, stride=8), :] + shift
            spot = dest[pl.ds((j * 9 + c) * 8 + k, 1), :]
            keys = jnp.concatenate([keyed(value, sub), jnp.zeros((128 - KEYS, 128), BF16)], 0)
            into[k, 0:rows, :] = lax.dot_general(
                one_hot(rows, spot), keys, LANES, preferred_element_type=F32
            )

        sides = [c for c in range(9) if c != 4]

        def pick_some(i, _):
            for k in (4 * i, 4 * i + 1, 4 * i + 2, 4 * i + 3):
                for c in range(9):
                    pick(c, k, USUAL[kind(c)][0], picked.at[c])
            return 0

        lax.fori_loop(0, 2, pick_some, 0)
        if j == 0:
            copy.wait()

        def gather_level(k, offset, sizes):
            for t in range(3):
                start_of_part = offset
                if t == 2:
                    bounds[0, k] = offset
                for c in sides:
                    start = 0 if t == 0 else count(c, 0, k)
                    if t == 2:
                        start = start + count(c, 1, k)
                    length = sizes[kind(c)][1 + t]
                    packed[pl.ds(offset, length), :] = picked[c, k, pl.ds(start, length), :]
                    offset = offset + count(c, t, k)
                if t == 0:
                    bounds[1, k] = offset
                if t == 1:
                    packed[pl.ds(offset, 32), :] = inert
                    offset = jnp.maximum(offset, start_of_part + 32)
                    below, above = (k + 7) % 8, (k + 1) % 8
                    length = sizes[0][1]
                    start = count(4, 0, below)
                    packed[pl.ds(offset, length), :] = picked[4, below, pl.ds(start, length), :]
                    offset = offset + jnp.where(k > 0, count(4, 2, below), 0)
                    packed[pl.ds(offset, length), :] = picked[4, above, pl.ds(0, length), :]
                    offset = offset + jnp.where(k < 7, count(4, 0, above), 0)
                    packed[pl.ds(offset, 8), :] = inert[0:8]
                    offset = (offset + 7) // 8 * 8
            return offset

        def gather_usual():
            offset = 0
            for k in range(8):
                offset = gather_level(k, offset, USUAL)
            return offset

        def gather_any():
            def level(k, offset):
                for c in sides:
                    pick(c, k, 128, picked.at[c])
                return gather_level(k, offset, {t: (128,) * 4 for t in range(3)})

            return lax.fori_loop(0, 8, level, jnp.int32(0))

        end = lax.cond(count_s[8, j * 128] > 0, gather_any, gather_usual)
        packed[pl.ds(end, 32), :] = inert
        bounds[1, 8] = end

        def cell(k, _):
            first = jnp.where(k == 0, 0, bounds[0, jnp.maximum(k - 1, 0)])
            last = bounds[1, k + 1]
            table = tables.at[j * 8 + k]

            parts = (last - first + 31) // 32
            sums = (jnp.zeros((8, 128), F32),) * 3
            for size, times in ((128, parts // 4), (64, parts % 4 // 2), (32, parts % 2 // 1)):

                def chunk(i, acc, size=size):
                    at = pl.multiple_of(first + i * size, 8)
                    return add_pairs(packed[pl.ds(at, size), 0:KEYS], table, acc)

                sums = lax.fori_loop(0, times, chunk, sums)
                first = first + times * size
            for t in range(3):
                force[pl.ds((j * 8 + t) * 8 + k, 1), :] = jnp.sum(sums[t], 0, keepdims=True)
            return 0

        lax.fori_loop(0, 8, cell, 0)

    loads[2].wait()
    for j in range(2):
        fx, fy, fz = (
            force[(j * 8 + t) * 8 : (j * 8 + t) * 8 + 8, :]
            + inside[(j * 8 + t) * 8 : (j * 8 + t) * 8 + 8, :]
            for t in range(3)
        )
        fy, fz = fy + blade[j] * cos_b, fz + blade[j] * sin_b
        ox, oy, oz = (off[t, 0, j] for t in range(3))
        six = [fx, fy, fz, oy * fz - oz * fy, oz * fx - ox * fz, ox * fy - oy * fx]
        for t in range(8):
            force[(j * 8 + t) * 8 : (j * 8 + t) * 8 + 8, :] = (
                six[t] if t < 6 else jnp.zeros((8, 128), F32)
            )


def exchange_kernel(
    n_shaft,
    n_lat,
    force,
    hot_piece,
    hot_clump,
    route_rows,
    turning,
    motion_hbm,
    inverse_mass_hbm,
    table,
    motion,
    inverse_mass,
    part,
    got,
    send_sem,
    recv_sem,
    load_sem,
):
    place = Place(n_shaft, n_lat)
    n_clump = turning.shape[-1]
    place.greet()
    loads = [
        pltpu.make_async_copy(motion_hbm, motion, load_sem.at[0]),
        pltpu.make_async_copy(inverse_mass_hbm, inverse_mass, load_sem.at[1]),
    ]
    for load in loads:
        load.start()

    def sums_copy(ds, dl, slot):
        c = (ds + 1) * 3 + dl + 1
        return pltpu.make_async_remote_copy(
            src_ref=part.at[c],
            dst_ref=got.at[slot],
            send_sem=send_sem.at[0, slot],
            recv_sem=recv_sem.at[0, slot],
            device_id=place.at(ds, dl),
            device_id_type=MESH,
        )

    def table_copy(ds, dl, slot):
        return pltpu.make_async_remote_copy(
            src_ref=table.at[4],
            dst_ref=table.at[slot],
            send_sem=send_sem.at[1, slot],
            recv_sem=recv_sem.at[1, slot],
            device_id=place.at(ds, dl),
            device_id_type=MESH,
        )

    def around(act, dl):
        for ds in (-1, 0, 1):
            if (ds, dl) != (0, 0):
                act(ds, dl)

    terms = [
        rows3(force[pl.ds(j * 64 + k, 8, stride=8), :]).astype(BF16) for j in range(2) for k in range(8)
    ]
    sums = lax.dot_general(
        jnp.concatenate(terms, 1), hot_piece[...], LANES, preferred_element_type=F32
    )
    sums = rows3(sum3(sums))
    route = jnp.concatenate([route_rows[...]] * 3, 0)
    routed = jnp.concatenate([jnp.where(route == c, sums, 0.0) for c in range(9)], 0)
    sums = lax.dot_general(
        routed.astype(BF16), hot_clump[...], LANES, preferred_element_type=F32
    )
    for c in range(9):
        part[c] = sum3(sums[24 * c : 24 * c + 24])

    def clear(edge, column):
        @pl.when(place.l == edge)
        def _():
            for row in range(3):
                table[row * 3 + column] = jnp.zeros((8, n_clump), F32)
                got[row * 3 + 2 - column] = jnp.zeros((8, n_clump), F32)

    clear(0, 0)
    clear(n_lat - 1, 2)
    place.meet()
    place.lateral(
        lambda dl: around(lambda ds, d: sums_copy(ds, d, (ds + 1) * 3 + d + 1).start(), dl)
    )
    for load in loads:
        load.wait()
    place.lateral(
        lambda dl: around(lambda ds, d: sums_copy(ds, d, 8 - (ds + 1) * 3 - d - 1).wait_recv(), dl)
    )
    sums = part[4]
    for c in range(9):
        if c != 4:
            sums = sums + got[c]
    rows = []
    for t in range(3):
        pull = -GRAVITY if t == 2 else 0.0
        rows.append(motion[t, 0] + TIME_STEP * (inverse_mass[0] * sums[t : t + 1] + pull))
    torque = [sums[3 + t : 4 + t] for t in range(3)]
    order = ((0, 1, 2), (1, 3, 4), (2, 4, 5))
    for t in range(3):
        change = sum(turning[order[t][i] : order[t][i] + 1, :] * torque[i] for i in range(3))
        rows.append(motion[3 + t, 0] + change)
    table[4] = jnp.concatenate(rows + [jnp.zeros((2, n_clump), F32)], 0)
    place.lateral(
        lambda dl: around(lambda ds, d: table_copy(ds, d, 8 - (ds + 1) * 3 - d - 1).start(), dl)
    )
    place.lateral(
        lambda dl: around(lambda ds, d: table_copy(ds, d, (ds + 1) * 3 + d + 1).wait_recv(), dl)
    )
    place.lateral(
        lambda dl: around(lambda ds, d: sums_copy(ds, d, (ds + 1) * 3 + d + 1).wait_send(), dl)
    )
    place.lateral(
        lambda dl: around(lambda ds, d: table_copy(ds, d, 8 - (ds + 1) * 3 - d - 1).wait_send(), dl)
    )


def spread_kernel(
    table,
    hot_piece,
    hot_clump,
    route_rows,
    centre_hbm,
    off_hbm,
    clump_hbm,
    sphere_hbm,
    centre,
    off,
    clump_out,
    sphere_out,
    pose,
    sem,
):
    loads = [
        pltpu.make_async_copy(centre_hbm, centre, sem.at[0]),
        pltpu.make_async_copy(off_hbm, off, sem.at[1]),
    ]
    for load in loads:
        load.start()
    tables = jnp.concatenate([rows3(table[c]) for c in range(9)], 0).astype(BF16)
    found = lax.dot_general(tables, hot_clump[...], ROWS, preferred_element_type=F32)
    route = jnp.concatenate([route_rows[...]] * 3, 0)
    by_piece = found[0:24]
    for c in range(1, 9):
        by_piece = jnp.where(route == c, found[24 * c : 24 * c + 24], by_piece)
    by_sphere = sum3(
        lax.dot_general(by_piece.astype(BF16), hot_piece[...], ROWS, preferred_element_type=F32)
    )
    loads[0].wait()
    for t in range(6):
        row = table[4, t : t + 1, :]
        if t < 3:
            clump_out[t, 0] = centre[t, 0] + TIME_STEP * row
        clump_out[3 + t, 0] = row
    stores = [pltpu.make_async_copy(clump_out, clump_hbm, sem.at[2])]
    stores[0].start()
    for m in range(16):
        pose[m * 8 : m * 8 + 8, :] = by_sphere[:, m * 128 : m * 128 + 128]
    loads[1].wait()
    for j in range(2):
        vx, vy, vz, sx, sy, sz = (
            pose[pl.ds(j * 64 + t, 8, stride=8), :] for t in range(6)
        )
        bx, by, bz = (off[t, 0, j] for t in range(3))
        hx, hy, hz = (0.5 * TIME_STEP * s for s in (sx, sy, sz))
        scale = 2.0 / (1.0 + (hx * hx + hy * hy + hz * hz))
        cx, cy, cz = hy * bz - hz * by, hz * bx - hx * bz, hx * by - hy * bx
        tx = bx + scale * (cx + hy * cz - hz * cy)
        ty = by + scale * (cy + hz * cx - hx * cz)
        tz = bz + scale * (cz + hx * cy - hy * cx)
        sphere_out[0, 0, j], sphere_out[1, 0, j], sphere_out[2, 0, j] = tx, ty, tz
        sphere_out[3, 0, j] = vx + (sy * tz - sz * ty)
        sphere_out[4, 0, j] = vy + (sz * tx - sx * tz)
        sphere_out[5, 0, j] = vz + (sx * ty - sy * tx)
        stores.append(
            pltpu.make_async_copy(
                sphere_out.at[:, :, pl.ds(j, 1)], sphere_hbm.at[:, :, pl.ds(j, 1)], sem.at[3 + j]
            )
        )
        stores[-1].start()
    for store in stores:
        store.wait()


def contact_call(lat_cells, blade_phase, ext, inside, tables, off, angles, inertia, **extra):
    n_clump = angles.shape[-1]
    return pl.pallas_call(
        functools.partial(contact_kernel, lat_cells),
        out_shape=(
            jax.ShapeDtypeStruct((128, 128), F32),
            jax.ShapeDtypeStruct((8, n_clump), F32),
        ),
        in_specs=[SMEM] + [VMEM] * 3 + [HBM] * 3,
        out_specs=(VMEM, VMEM),
        scratch_shapes=[
            pltpu.VMEM(off.shape, F32),
            pltpu.VMEM(angles.shape, F32),
            pltpu.VMEM(inertia.shape, F32),
            pltpu.VMEM((144, 128), jnp.int32),
            pltpu.VMEM((16, 512), jnp.int32),
            pltpu.SMEM((16, 512), jnp.int32),
            pltpu.SMEM((2, 16), jnp.int32),
            pltpu.VMEM((9, 8, 256, 128), F32),
            pltpu.VMEM((9 * 1024 + 8 * 72 + 256, 128), F32),
            pltpu.SemaphoreType.DMA((4,)),
        ],
        compiler_params=pltpu.CompilerParams(vmem_limit_bytes=24 << 20),
        name="contact",
        **extra,
    )(blade_phase, ext, inside, tables, off, angles, inertia)


def on_device(
    n_shaft,
    n_lat,
    sphere_position,
    sphere_velocity,
    sphere_radius,
    sphere_offset,
    sphere_piece,
    piece_route,
    piece_clump,
    blade_phase,
    clump_centre,
    clump_motion,
    clump_angles,
    clump_inverse_mass,
    clump_inverse_inertia,
):
    n_piece, n_clump = piece_route.shape[-1], clump_angles.shape[-1]
    sphere_position, sphere_velocity, sphere_radius, sphere_piece, piece_route, piece_clump = (
        pltpu.with_memory_space_constraint(v, pltpu.HBM)
        for v in (
            sphere_position,
            sphere_velocity,
            sphere_radius,
            sphere_piece,
            piece_route,
            piece_clump,
        )
    )
    sphere_offset, clump_centre, clump_motion = (
        pltpu.with_memory_space_constraint(v, pltpu.HBM)
        for v in (sphere_offset, clump_centre, clump_motion)
    )
    clump_angles, clump_inverse_mass, clump_inverse_inertia = (
        pltpu.with_memory_space_constraint(v, pltpu.HBM)
        for v in (clump_angles, clump_inverse_mass, clump_inverse_inertia)
    )
    ext, hot_piece, hot_clump, route_rows, inside, tables = pl.pallas_call(
        functools.partial(halo_kernel, n_shaft, n_lat),
        out_shape=(
            jax.ShapeDtypeStruct((3, 4, 8, 8, 128), F32),
            jax.ShapeDtypeStruct((n_piece, 2048), BF16),
            jax.ShapeDtypeStruct((n_clump, n_piece), BF16),
            jax.ShapeDtypeStruct((8, n_piece), jnp.int32),
            jax.ShapeDtypeStruct((128, 128), F32),
            jax.ShapeDtypeStruct((16, KEYS, TERMS * 128), BF16),
        ),
        in_specs=[HBM] * 6,
        out_specs=(VMEM,) * 6,
        scratch_shapes=[
            pltpu.VMEM(sphere_piece.shape, jnp.int32),
            pltpu.VMEM(piece_route.shape, jnp.int32),
            pltpu.VMEM(piece_clump.shape, jnp.int32),
            pltpu.SemaphoreType.DMA((3, 4, 3)),
            pltpu.SemaphoreType.DMA((3, 4, 3)),
            pltpu.SemaphoreType.DMA((2, 3)),
            pltpu.SemaphoreType.DMA((3,)),
        ],
        compiler_params=pltpu.CompilerParams(
            collective_id=0, has_side_effects=True, vmem_limit_bytes=16 << 20
        ),
        name="halo",
    )(
        sphere_position,
        sphere_velocity,
        sphere_radius,
        sphere_piece,
        piece_route,
        piece_clump,
    )
    force, turning = contact_call(
        2 * n_lat,
        blade_phase,
        ext.reshape(768, 128),
        inside,
        tables,
        sphere_offset,
        clump_angles,
        clump_inverse_inertia,
    )
    table = pl.pallas_call(
        functools.partial(exchange_kernel, n_shaft, n_lat),
        out_shape=jax.ShapeDtypeStruct((9, 8, n_clump), F32),
        in_specs=[VMEM] * 5 + [HBM] * 2,
        out_specs=VMEM,
        scratch_shapes=[
            pltpu.VMEM(clump_motion.shape, F32),
            pltpu.VMEM(clump_inverse_mass.shape, F32),
            pltpu.VMEM((9, 8, n_clump), F32),
            pltpu.VMEM((9, 8, n_clump), F32),
            pltpu.SemaphoreType.DMA((2, 9)),
            pltpu.SemaphoreType.DMA((2, 9)),
            pltpu.SemaphoreType.DMA((2,)),
        ],
        compiler_params=pltpu.CompilerParams(
            collective_id=1, has_side_effects=True, vmem_limit_bytes=16 << 20
        ),
        name="exchange",
    )(force, hot_piece, hot_clump, route_rows, turning, clump_motion, clump_inverse_mass)
    return pl.pallas_call(
        spread_kernel,
        out_shape=(
            jax.ShapeDtypeStruct((9, 1, 1, n_clump), F32),
            jax.ShapeDtypeStruct((6, 1, 2, 8, 128), F32),
        ),
        in_specs=[VMEM] * 4 + [HBM] * 2,
        out_specs=(HBM, HBM),
        scratch_shapes=[
            pltpu.VMEM(clump_centre.shape, F32),
            pltpu.VMEM(sphere_offset.shape, F32),
            pltpu.VMEM((9, 1, 1, n_clump), F32),
            pltpu.VMEM((6, 1, 2, 8, 128), F32),
            pltpu.VMEM((128, 128), F32),
            pltpu.SemaphoreType.DMA((5,)),
        ],
        compiler_params=pltpu.CompilerParams(vmem_limit_bytes=16 << 20),
        name="spread",
    )(table, hot_piece, hot_clump, route_rows, clump_centre, sphere_offset)


def solution(mesh):
    placed = (
        P(None, "shaft", "lat", None, None),
        P(None, "shaft", "lat", None, None),
        P("shaft", "lat", None, None),
        P(None, "shaft", "lat", None, None),
        P("shaft", "lat", None),
        P("shaft", "lat", None),
        P("shaft", "lat", None),
        P(),
        P(None, "shaft", "lat", None),
        P(None, "shaft", "lat", None),
        P(None, "shaft", "lat", None),
        P("shaft", "lat", None),
        P(None, "shaft", "lat", None),
    )
    return jax.shard_map(
        functools.partial(on_device, mesh.shape["shaft"], mesh.shape["lat"]),
        mesh=mesh,
        in_specs=placed,
        out_specs=(P(None, "shaft", "lat", None), P(None, "shaft", "lat", None, None)),
        check_vma=False,
    )
```

```python
import functools
import math

import jax
import jax.numpy as jnp
from jax import lax
from jax.experimental import pallas as pl
from jax.experimental.pallas import tpu as pltpu
from jax.sharding import PartitionSpec as P

PHASES = 64
CELL_SIDE = 5.0
BLADE_STIFFNESS = 20.0
BLADE_THICKNESS = 1.0
TIME_STEP = 0.5
GRAVITY = 0.5

REACH = 0.6001
CHUNK = 64
F32 = jnp.float32
BF16 = jnp.bfloat16
MESH = pl.DeviceIdType.MESH
LANES = (((1,), (1,)), ((), ()))
ROWS = (((1,), (0,)), ((), ()))
VMEM = pl.BlockSpec(memory_space=pltpu.VMEM)
SMEM = pl.BlockSpec(memory_space=pltpu.SMEM)
HBM = pl.BlockSpec(memory_space=pltpu.HBM)


def split3(x):
    high = x.astype(BF16)
    rest = x - high.astype(F32)
    middle = rest.astype(BF16)
    low = (rest - middle.astype(F32)).astype(BF16)
    return high, middle, low


def rows3(x):
    high = x.astype(BF16).astype(F32)
    rest = x - high
    middle = rest.astype(BF16).astype(F32)
    return jnp.concatenate([high, middle, rest - middle], 0)


def sum3(x):
    return x[0:8] + x[8:16] + x[16:24]


def one_hot(rows, row):
    length = row.shape[-1]
    ids = lax.broadcasted_iota(jnp.int16, (rows, length), 0)
    return jnp.where(ids == row.astype(jnp.int16), jnp.ones((), BF16), jnp.zeros((), BF16))


class Place:
    def __init__(self, n_shaft, n_lat):
        self.n_shaft, self.n_lat = n_shaft, n_lat
        self.s, self.l = lax.axis_index("shaft"), lax.axis_index("lat")

    def at(self, ds, dl):
        return {"shaft": lax.rem(self.s + ds + self.n_shaft, self.n_shaft), "lat": self.l + dl}

    def lateral(self, act):
        pl.when(self.l > 0)(lambda: act(-1))
        pl.when(self.l < self.n_lat - 1)(lambda: act(1))
        act(0)

    def greet(self):
        sem = pltpu.get_barrier_semaphore()

        def signal(dl):
            for ds in (-1, 0, 1):
                if (ds, dl) != (0, 0):
                    pl.semaphore_signal(
                        sem, inc=1, device_id=self.at(ds, dl), device_id_type=MESH
                    )

        self.lateral(signal)

    def meet(self):
        sem = pltpu.get_barrier_semaphore()
        edge = jnp.logical_or(self.l == 0, self.l == self.n_lat - 1)
        pl.semaphore_wait(sem, jnp.where(edge, 5, 8))


def halo_kernel(
    n_shaft,
    n_lat,
    pos,
    vel,
    rad,
    piece_hbm,
    route_hbm,
    clump_hbm,
    ext,
    hot_piece,
    hot_clump,
    route_rows,
    inside,
    tables,
    piece,
    route,
    clump,
    send_sem,
    recv_sem,
    own_sem,
    load_sem,
):
    place = Place(n_shaft, n_lat)

    def parts(j, si, lj):
        return (
            (pos.at[:, 0, j], ext.at[si, lj, 0:3]),
            (vel.at[:, 0, j], ext.at[si, lj, 3:6]),
            (rad.at[0, pl.ds(j, 1)], ext.at[si, lj, 6:7]),
        )

    def remote(j, ds, dl, si, lj):
        return [
            pltpu.make_async_remote_copy(
                src_ref=src,
                dst_ref=dst,
                send_sem=send_sem.at[si, lj, t],
                recv_sem=recv_sem.at[si, lj, t],
                device_id=place.at(ds, dl),
                device_id_type=MESH,
            )
            for t, (src, dst) in enumerate(parts(j, si, lj))
        ]

    def outgoing(dl):
        found = []
        for ds in (-1, 0, 1):
            for j in (0, 1):
                lj = j - 2 * dl + 1
                if 0 <= lj <= 3 and (ds, dl) != (0, 0):
                    found += remote(j, ds, dl, 1 - ds, lj)
        return found

    def incoming(dl):
        found = []
        for ds in (-1, 0, 1):
            for lj in {0: (1, 2), -1: (0,), 1: (3,)}[dl]:
                if (ds, dl) != (0, 0):
                    found += remote(0, ds, dl, 1 + ds, lj)
        return found

    own = [
        pltpu.make_async_copy(src, dst, own_sem.at[j, t])
        for j in (0, 1)
        for t, (src, dst) in enumerate(parts(j, 1, 1 + j))
    ]
    own += [
        pltpu.make_async_copy(src, dst, load_sem.at[t])
        for t, (src, dst) in enumerate(
            ((piece_hbm, piece), (route_hbm, route), (clump_hbm, clump))
        )
    ]
    for c in own:
        c.start()
    place.greet()
    place.meet()
    place.lateral(lambda dl: [c.start() for c in outgoing(dl)] and None)
    ext[:, :, 7] = jnp.zeros((3, 4, 8, 128), F32)

    @pl.when(place.l == 0)
    def _():
        ext[:, 0, 0:7] = jnp.zeros((3, 7, 8, 128), F32)

    @pl.when(place.l == n_lat - 1)
    def _():
        ext[:, 3, 0:7] = jnp.zeros((3, 7, 8, 128), F32)

    for c in own:
        c.wait()
    sub = lax.broadcasted_iota(jnp.int32, (8, 128), 0)
    every = one_hot(128, lax.broadcasted_iota(jnp.int32, (1, 128), 1))
    inside[...] = jnp.zeros((128, 128), F32)

    def cell(m):
        j, k = m // 8, m % 8
        mine = [ext[1, 1 + j, t, pl.ds(k, 1), :] for t in range(7)]
        mine[2] = mine[2] + (CELL_SIDE * k.astype(F32) - 20.0)
        own_table(mine, sub, tables.at[m])
        value = jnp.concatenate(mine + [mine[6]], 0)
        rows = lax.dot_general(every, keyed(value, sub), LANES, preferred_element_type=F32)
        zero = jnp.zeros((8, 128), F32)
        acc = (zero, zero, zero)
        for i in range(0, 128, CHUNK):
            acc = add_pairs(rows[i : i + CHUNK], tables.at[m], acc)
        for t in range(3):
            inside[pl.ds((j * 8 + t) * 8 + k, 1), :] = jnp.sum(acc[t], 0, keepdims=True)

    def cells(i, _):
        for t in range(4):
            cell(4 * i + t)
        return 0

    lax.fori_loop(0, 4, cells, 0)
    for m in range(16):
        hot_piece[:, m * 128 : m * 128 + 128] = one_hot(
            hot_piece.shape[0], piece[0, :, m * 128 : m * 128 + 128]
        )
    hot_clump[...] = one_hot(hot_clump.shape[0], clump[0])
    route_rows[...] = jnp.broadcast_to(route[0], route_rows.shape)
    place.lateral(lambda dl: [c.wait_recv() for c in incoming(dl)] and None)
    place.lateral(lambda dl: [c.wait_send() for c in outgoing(dl)] and None)


USUAL = {0: (128, 64, 64, 64), 1: (64, 24, 40, 24), 2: (32, 16, 24, 16)}
KEYS = 32
TERMS = 9


def kind(c):
    return (c // 3 != 1) + (c % 3 != 1)


def keyed(value, sub):
    radius = value[6:7]
    value = jnp.where(sub == 7, radius * radius * 0.0625, value)
    high = value.astype(BF16).astype(F32)
    rest = value - high
    middle = rest.astype(BF16).astype(F32)
    more = jnp.where(
        sub < 3,
        1.0,
        jnp.where(sub < 5, high[6:7], jnp.where(sub == 5, middle[6:7], 0.0)),
    )
    return jnp.concatenate([high, middle, rest - middle, more], 0).astype(BF16)


def own_table(own, sub, table):
    zero = jnp.zeros((8, 128), F32)

    def split(row):
        return [p.astype(F32) for p in split3(jnp.broadcast_to(row, (8, 128)))]

    def constants(row):
        high, middle, low = split(row)
        return jnp.where(sub == 0, high, jnp.where(sub == 1, middle, jnp.where(sub == 2, low, 0.0)))

    def put(t, same, more):
        block = jnp.concatenate([same, same, same, more], 0)
        table[:, t * 128 : t * 128 + 128] = block.astype(BF16)

    for t in range(7):
        put(t, jnp.where(sub == t, 1.0 if t == 6 else -1.0, zero), constants(own[t]))
    high, middle, low = split(4.0 * own[6])
    same = jnp.where(sub == 6, high, 0.0)
    more = jnp.where(sub == 4, low, jnp.where((sub == 3) | (sub == 5), middle, 0.0))
    put(7, same, more)
    put(
        8,
        jnp.where(sub == 7, 1.0, same * 0.03125),
        more * 0.03125 + constants(own[6] * own[6] * 0.0625),
    )


def pair_sums(pair, acc):
    dx, dy, dz, du, dv, dw, radii, product, least = pair
    square = dx * dx + dy * dy + dz * dz
    clamped = jnp.maximum(square, least)
    inverse = lax.rsqrt(clamped)
    delta = jnp.maximum(radii - clamped * inverse, 0.0)
    normal_speed = (du * dx + dv * dy + dw * dz) * inverse
    speed = du * du + dv * dv + dw * dw
    unit = square * (inverse * inverse)
    sliding = speed + normal_speed * normal_speed * (unit - 2.0)
    load = product * delta
    root = load * lax.rsqrt(jnp.maximum(load * radii, 1e-30))
    root2 = root * root
    cap = 2.5 * delta
    shear = root2 * cap * lax.rsqrt(jnp.maximum(root2 * (sliding + cap * cap), 0.0) + 1e-06)
    push = root * (cap + cap - normal_speed - 0.25)
    along = (push + shear * normal_speed) * inverse
    return (
        acc[0] + (along * dx - shear * du),
        acc[1] + (along * dy - shear * dv),
        acc[2] + (along * dz - shear * dw),
    )


def add_pairs(rows, table, acc):
    pairs = lax.dot_general(rows.astype(BF16), table[...], ROWS, preferred_element_type=F32)
    for g in range(0, rows.shape[0], 8):
        acc = pair_sums([pairs[g : g + 8, t * 128 : t * 128 + 128] for t in range(TERMS)], acc)
    return acc


def contact_kernel(
    lat_cells,
    phase,
    ext,
    inside,
    tables,
    off_hbm,
    force,
    off,
    dest,
    count_v,
    count_s,
    bounds,
    picked,
    packed,
    copy_sem,
):
    loads = [
        pltpu.make_async_copy(src, dst, copy_sem.at[1 + t])
        for t, (src, dst) in enumerate(
            ((off_hbm, off),)
        )
    ]
    for load in loads:
        load.start()
    sub = lax.broadcasted_iota(jnp.int32, (8, 128), 0)

    before = jnp.where(
        lax.broadcasted_iota(jnp.int32, (128, 128), 0)
        < lax.broadcasted_iota(jnp.int32, (128, 128), 1),
        1.0,
        0.0,
    ).astype(BF16)
    ones = jnp.ones((128, 128), BF16)
    for j in range(2):
        masks = []
        for c in range(9):
            di, dj = c // 3 - 1, c % 3 - 1
            base = ((1 + di) * 4 + 1 + j + dj) * 64
            x, y, z = (ext[base + 8 * t : base + 8 * t + 8, :] for t in range(3))
            radius = ext[base + 48 : base + 56, :]
            keep = radius > 0.0
            near = radius + REACH
            away = [v if d > 0 else CELL_SIDE - v for v, d in ((x, di), (y, dj)) if d]
            up, square = CELL_SIDE - z, near * near
            low, high = z < near, up < near
            if away:
                flat = sum(v * v for v in away)
                keep &= flat < square
                low, high = flat + z * z < square, flat + up * up < square
            kept = jnp.where(keep, 1.0, 0.0)
            low_f = jnp.where(low, kept, 0.0)
            high_f = jnp.where(high, kept, 0.0)
            mid_f = jnp.zeros((8, 128), F32) if c == 4 else kept - low_f - high_f
            masks += [low_f, mid_f, high_f]
        mask = jnp.concatenate(masks, 0).astype(BF16)
        prefix = lax.dot_general(mask, before, ROWS, preferred_element_type=F32)
        total = lax.dot_general(mask, ones, ROWS, preferred_element_type=F32)
        counts = lax.dot_general(ones[0:8], mask, LANES, preferred_element_type=F32)
        count_v[0:8, j * 256 : j * 256 + 216] = counts.astype(jnp.int32)
        over = jnp.full((8, 128), -1.0, F32)
        for c in range(9):
            a = c * 24
            low_p, mid_p, high_p = (prefix[a + 8 * t : a + 8 * t + 8] for t in range(3))
            low_n, mid_n, high_n = (total[a + 8 * t : a + 8 * t + 8] for t in range(3))
            spot = (
                masks[3 * c] * low_p
                + masks[3 * c + 1] * (low_n + mid_p)
                + masks[3 * c + 2] * (low_n + mid_n + high_p)
            )
            any_of = masks[3 * c] + masks[3 * c + 1] + masks[3 * c + 2]
            spot = jnp.where(any_of > 0.0, spot, -1.0).astype(jnp.int32)
            dest[(j * 9 + c) * 8 : (j * 9 + c) * 8 + 8, :] = spot
            sizes = (low_n + mid_n + high_n, low_n, mid_n, high_n)
            for size, usual in zip(sizes, USUAL[kind(c)]):
                over = jnp.maximum(over, size - usual)
        over = jnp.broadcast_to(jnp.max(over, 0, keepdims=True), (8, 128))
        count_v[8:16, j * 128 : j * 128 + 128] = over.astype(jnp.int32)
    copy = pltpu.make_async_copy(count_v, count_s, copy_sem.at[0])
    copy.start()

    angle = jnp.full((8, 128), phase[0].astype(F32) * (2.0 * math.pi / PHASES), F32)
    cos_b, sin_b = jnp.cos(angle), jnp.sin(angle)
    height_cells = 8
    centre_y, centre_z = 0.5 * CELL_SIDE * lat_cells, 0.5 * CELL_SIDE * height_cells
    reach = 0.45 * CELL_SIDE * min(lat_cells, height_cells)
    shaft_id = lax.axis_index("shaft").astype(F32)
    lat_id = (lax.axis_index("lat") * 2).astype(F32)
    up_id = sub.astype(F32)
    blade = []
    for j in range(2):
        base = (5 + j) * 64
        x, y, z = (ext[base + 8 * t : base + 8 * t + 8, :] for t in range(3))
        radius = ext[base + 48 : base + 56, :]
        x = CELL_SIDE * shaft_id + x
        y = CELL_SIDE * (lat_id + j) + y - centre_y
        z = CELL_SIDE * up_id + z - centre_z
        across = y * cos_b + z * sin_b
        radial = z * cos_b - y * sin_b
        depth = jnp.maximum(jnp.minimum(radius - across, radius + BLADE_THICKNESS + across), 0.0)
        window = jnp.maximum(radial * (reach - radial), 0.0) * (4.0 / (reach * reach))
        gate = jnp.maximum(jnp.cos(x * (2.0 * math.pi / (2.0 * CELL_SIDE))), 0.0)
        size = BLADE_STIFFNESS * depth * window * gate
        blade.append(size)

    lane = lax.broadcasted_iota(jnp.int32, (32, 128), 1)
    inert = jnp.where((lane >= 24) & (lane < 27), 1.0, 0.0)
    for j in range(2):

        def count(c, t, k):
            return count_s[0, j * 256 + (c * 3 + t) * 8 + k]

        def pick(c, k, rows, into):
            di, dj = c // 3 - 1, c % 3 - 1
            base = ((1 + di) * 4 + 1 + j + dj) * 64
            rise = CELL_SIDE * k.astype(F32) - 20.0
            shift = jnp.where(
                sub == 0,
                CELL_SIDE * di,
                jnp.where(sub == 1, CELL_SIDE * dj, jnp.where(sub == 2, rise, 0.0)),
            )
            value = ext[pl.ds(base + k, 8, stride=8), :] + shift
            spot = dest[pl.ds((j * 9 + c) * 8 + k, 1), :]
            keys = jnp.concatenate([keyed(value, sub), jnp.zeros((128 - KEYS, 128), BF16)], 0)
            into[k, 0:rows, :] = lax.dot_general(
                one_hot(rows, spot), keys, LANES, preferred_element_type=F32
            )

        sides = [c for c in range(9) if c != 4]

        def pick_some(i, _):
            for k in (4 * i, 4 * i + 1, 4 * i + 2, 4 * i + 3):
                for c in range(9):
                    pick(c, k, USUAL[kind(c)][0], picked.at[c])
            return 0

        lax.fori_loop(0, 2, pick_some, 0)
        if j == 0:
            copy.wait()

        def gather_level(k, offset, sizes):
            for t in range(3):
                start_of_part = offset
                if t == 2:
                    bounds[0, k] = offset
                for c in sides:
                    start = 0 if t == 0 else count(c, 0, k)
                    if t == 2:
                        start = start + count(c, 1, k)
                    length = sizes[kind(c)][1 + t]
                    packed[pl.ds(offset, length), :] = picked[c, k, pl.ds(start, length), :]
                    offset = offset + count(c, t, k)
                if t == 0:
                    bounds[1, k] = offset
                if t == 1:
                    packed[pl.ds(offset, 32), :] = inert
                    offset = jnp.maximum(offset, start_of_part + 32)
                    below, above = (k + 7) % 8, (k + 1) % 8
                    length = sizes[0][1]
                    start = count(4, 0, below)
                    packed[pl.ds(offset, length), :] = picked[4, below, pl.ds(start, length), :]
                    offset = offset + jnp.where(k > 0, count(4, 2, below), 0)
                    packed[pl.ds(offset, length), :] = picked[4, above, pl.ds(0, length), :]
                    offset = offset + jnp.where(k < 7, count(4, 0, above), 0)
                    packed[pl.ds(offset, 8), :] = inert[0:8]
                    offset = (offset + 7) // 8 * 8
            return offset

        def gather_usual():
            offset = 0
            for k in range(8):
                offset = gather_level(k, offset, USUAL)
            return offset

        def gather_any():
            def level(k, offset):
                for c in sides:
                    pick(c, k, 128, picked.at[c])
                return gather_level(k, offset, {t: (128,) * 4 for t in range(3)})

            return lax.fori_loop(0, 8, level, jnp.int32(0))

        end = lax.cond(count_s[8, j * 128] > 0, gather_any, gather_usual)
        packed[pl.ds(end, 32), :] = inert
        bounds[1, 8] = end

        def cell(k, _):
            first = jnp.where(k == 0, 0, bounds[0, jnp.maximum(k - 1, 0)])
            last = bounds[1, k + 1]
            table = tables.at[j * 8 + k]

            parts = (last - first + 31) // 32
            sums = (jnp.zeros((8, 128), F32),) * 3
            for size, times in ((128, parts // 4), (64, parts % 4 // 2), (32, parts % 2 // 1)):

                def chunk(i, acc, size=size):
                    at = pl.multiple_of(first + i * size, 8)
                    return add_pairs(packed[pl.ds(at, size), 0:KEYS], table, acc)

                sums = lax.fori_loop(0, times, chunk, sums)
                first = first + times * size
            for t in range(3):
                force[pl.ds((j * 8 + t) * 8 + k, 1), :] = jnp.sum(sums[t], 0, keepdims=True)
            return 0

        lax.fori_loop(0, 8, cell, 0)

    loads[0].wait()
    for j in range(2):
        fx, fy, fz = (
            force[(j * 8 + t) * 8 : (j * 8 + t) * 8 + 8, :]
            + inside[(j * 8 + t) * 8 : (j * 8 + t) * 8 + 8, :]
            for t in range(3)
        )
        fy, fz = fy + blade[j] * cos_b, fz + blade[j] * sin_b
        ox, oy, oz = (off[t, 0, j] for t in range(3))
        six = [fx, fy, fz, oy * fz - oz * fy, oz * fx - ox * fz, ox * fy - oy * fx]
        for t in range(8):
            force[(j * 8 + t) * 8 : (j * 8 + t) * 8 + 8, :] = (
                six[t] if t < 6 else jnp.zeros((8, 128), F32)
            )


def exchange_kernel(
    n_shaft,
    n_lat,
    force,
    hot_piece,
    hot_clump,
    route_rows,
    motion_hbm,
    inverse_mass_hbm,
    angles_hbm,
    inertia_hbm,
    table,
    motion,
    inverse_mass,
    angles,
    inertia,
    part,
    got,
    send_sem,
    recv_sem,
    load_sem,
):
    place = Place(n_shaft, n_lat)
    n_clump = table.shape[-1]
    place.greet()
    loads = [
        pltpu.make_async_copy(motion_hbm, motion, load_sem.at[0]),
        pltpu.make_async_copy(inverse_mass_hbm, inverse_mass, load_sem.at[1]),
        pltpu.make_async_copy(angles_hbm, angles, load_sem.at[2]),
        pltpu.make_async_copy(inertia_hbm, inertia, load_sem.at[3]),
    ]
    for load in loads:
        load.start()

    def sums_copy(ds, dl, slot):
        c = (ds + 1) * 3 + dl + 1
        return pltpu.make_async_remote_copy(
            src_ref=part.at[c],
            dst_ref=got.at[slot],
            send_sem=send_sem.at[0, slot],
            recv_sem=recv_sem.at[0, slot],
            device_id=place.at(ds, dl),
            device_id_type=MESH,
        )

    def table_copy(ds, dl, slot):
        return pltpu.make_async_remote_copy(
            src_ref=table.at[4],
            dst_ref=table.at[slot],
            send_sem=send_sem.at[1, slot],
            recv_sem=recv_sem.at[1, slot],
            device_id=place.at(ds, dl),
            device_id_type=MESH,
        )

    def around(act, dl):
        for ds in (-1, 0, 1):
            if (ds, dl) != (0, 0):
                act(ds, dl)

    terms = [
        rows3(force[pl.ds(j * 64 + k, 8, stride=8), :]).astype(BF16) for j in range(2) for k in range(8)
    ]
    sums = lax.dot_general(
        jnp.concatenate(terms, 1), hot_piece[...], LANES, preferred_element_type=F32
    )
    sums = rows3(sum3(sums))
    route = jnp.concatenate([route_rows[...]] * 3, 0)
    routed = jnp.concatenate([jnp.where(route == c, sums, 0.0) for c in range(9)], 0)
    sums = lax.dot_general(
        routed.astype(BF16), hot_clump[...], LANES, preferred_element_type=F32
    )
    for c in range(9):
        part[c] = sum3(sums[24 * c : 24 * c + 24])

    def clear(edge, column):
        @pl.when(place.l == edge)
        def _():
            for row in range(3):
                table[row * 3 + column] = jnp.zeros((8, n_clump), F32)
                got[row * 3 + 2 - column] = jnp.zeros((8, n_clump), F32)

    clear(0, 0)
    clear(n_lat - 1, 2)
    place.meet()
    place.lateral(
        lambda dl: around(lambda ds, d: sums_copy(ds, d, (ds + 1) * 3 + d + 1).start(), dl)
    )
    for load in loads:
        load.wait()
    cos_z, cos_y, cos_x = (jnp.cos(angles[t, 0]) for t in range(3))
    sin_z, sin_y, sin_x = (jnp.sin(angles[t, 0]) for t in range(3))
    rotation = [
        [
            cos_z * cos_y,
            cos_z * sin_y * sin_x - sin_z * cos_x,
            cos_z * sin_y * cos_x + sin_z * sin_x,
        ],
        [
            sin_z * cos_y,
            sin_z * sin_y * sin_x + cos_z * cos_x,
            sin_z * sin_y * cos_x - cos_z * sin_x,
        ],
        [-sin_y, cos_y * sin_x, cos_y * cos_x],
    ]
    turning = [
        TIME_STEP * sum(rotation[a][i] * inertia[i, 0] * rotation[b][i] for i in range(3))
        for a, b in ((0, 0), (0, 1), (0, 2), (1, 1), (1, 2), (2, 2))
    ]
    place.lateral(
        lambda dl: around(lambda ds, d: sums_copy(ds, d, 8 - (ds + 1) * 3 - d - 1).wait_recv(), dl)
    )
    sums = part[4]
    for c in range(9):
        if c != 4:
            sums = sums + got[c]
    rows = []
    for t in range(3):
        pull = -GRAVITY if t == 2 else 0.0
        rows.append(motion[t, 0] + TIME_STEP * (inverse_mass[0] * sums[t : t + 1] + pull))
    torque = [sums[3 + t : 4 + t] for t in range(3)]
    order = ((0, 1, 2), (1, 3, 4), (2, 4, 5))
    for t in range(3):
        change = sum(turning[order[t][i]] * torque[i] for i in range(3))
        rows.append(motion[3 + t, 0] + change)
    table[4] = jnp.concatenate(rows + [jnp.zeros((2, n_clump), F32)], 0)
    place.lateral(
        lambda dl: around(lambda ds, d: table_copy(ds, d, 8 - (ds + 1) * 3 - d - 1).start(), dl)
    )
    place.lateral(
        lambda dl: around(lambda ds, d: table_copy(ds, d, (ds + 1) * 3 + d + 1).wait_recv(), dl)
    )
    place.lateral(
        lambda dl: around(lambda ds, d: sums_copy(ds, d, (ds + 1) * 3 + d + 1).wait_send(), dl)
    )
    place.lateral(
        lambda dl: around(lambda ds, d: table_copy(ds, d, 8 - (ds + 1) * 3 - d - 1).wait_send(), dl)
    )


def spread_kernel(
    table,
    hot_piece,
    hot_clump,
    route_rows,
    centre_hbm,
    off_hbm,
    clump_hbm,
    sphere_hbm,
    centre,
    off,
    clump_out,
    sphere_out,
    pose,
    sem,
):
    loads = [
        pltpu.make_async_copy(centre_hbm, centre, sem.at[0]),
        pltpu.make_async_copy(off_hbm, off, sem.at[1]),
    ]
    for load in loads:
        load.start()
    tables = jnp.concatenate([rows3(table[c]) for c in range(9)], 0).astype(BF16)
    found = lax.dot_general(tables, hot_clump[...], ROWS, preferred_element_type=F32)
    route = jnp.concatenate([route_rows[...]] * 3, 0)
    by_piece = found[0:24]
    for c in range(1, 9):
        by_piece = jnp.where(route == c, found[24 * c : 24 * c + 24], by_piece)
    by_sphere = sum3(
        lax.dot_general(by_piece.astype(BF16), hot_piece[...], ROWS, preferred_element_type=F32)
    )
    loads[0].wait()
    for t in range(6):
        row = table[4, t : t + 1, :]
        if t < 3:
            clump_out[t, 0] = centre[t, 0] + TIME_STEP * row
        clump_out[3 + t, 0] = row
    stores = [pltpu.make_async_copy(clump_out, clump_hbm, sem.at[2])]
    stores[0].start()
    for m in range(16):
        pose[m * 8 : m * 8 + 8, :] = by_sphere[:, m * 128 : m * 128 + 128]
    loads[1].wait()
    for j in range(2):
        vx, vy, vz, sx, sy, sz = (
            pose[pl.ds(j * 64 + t, 8, stride=8), :] for t in range(6)
        )
        bx, by, bz = (off[t, 0, j] for t in range(3))
        hx, hy, hz = (0.5 * TIME_STEP * s for s in (sx, sy, sz))
        scale = 2.0 / (1.0 + (hx * hx + hy * hy + hz * hz))
        cx, cy, cz = hy * bz - hz * by, hz * bx - hx * bz, hx * by - hy * bx
        tx = bx + scale * (cx + hy * cz - hz * cy)
        ty = by + scale * (cy + hz * cx - hx * cz)
        tz = bz + scale * (cz + hx * cy - hy * cx)
        sphere_out[0, 0, j], sphere_out[1, 0, j], sphere_out[2, 0, j] = tx, ty, tz
        sphere_out[3, 0, j] = vx + (sy * tz - sz * ty)
        sphere_out[4, 0, j] = vy + (sz * tx - sx * tz)
        sphere_out[5, 0, j] = vz + (sx * ty - sy * tx)
        stores.append(
            pltpu.make_async_copy(
                sphere_out.at[:, :, pl.ds(j, 1)], sphere_hbm.at[:, :, pl.ds(j, 1)], sem.at[3 + j]
            )
        )
        stores[-1].start()
    for store in stores:
        store.wait()


def contact_call(lat_cells, blade_phase, ext, inside, tables, off, **extra):
    return pl.pallas_call(
        functools.partial(contact_kernel, lat_cells),
        out_shape=jax.ShapeDtypeStruct((128, 128), F32),
        in_specs=[SMEM] + [VMEM] * 3 + [HBM],
        out_specs=VMEM,
        scratch_shapes=[
            pltpu.VMEM(off.shape, F32),
            pltpu.VMEM((144, 128), jnp.int32),
            pltpu.VMEM((16, 512), jnp.int32),
            pltpu.SMEM((16, 512), jnp.int32),
            pltpu.SMEM((2, 16), jnp.int32),
            pltpu.VMEM((9, 8, 256, 128), F32),
            pltpu.VMEM((9 * 1024 + 8 * 72 + 256, 128), F32),
            pltpu.SemaphoreType.DMA((4,)),
        ],
        compiler_params=pltpu.CompilerParams(vmem_limit_bytes=24 << 20),
        name="contact",
        **extra,
    )(blade_phase, ext, inside, tables, off)


def on_device(
    n_shaft,
    n_lat,
    sphere_position,
    sphere_velocity,
    sphere_radius,
    sphere_offset,
    sphere_piece,
    piece_route,
    piece_clump,
    blade_phase,
    clump_centre,
    clump_motion,
    clump_angles,
    clump_inverse_mass,
    clump_inverse_inertia,
):
    n_piece, n_clump = piece_route.shape[-1], clump_angles.shape[-1]
    sphere_position, sphere_velocity, sphere_radius, sphere_piece, piece_route, piece_clump = (
        pltpu.with_memory_space_constraint(v, pltpu.HBM)
        for v in (
            sphere_position,
            sphere_velocity,
            sphere_radius,
            sphere_piece,
            piece_route,
            piece_clump,
        )
    )
    sphere_offset, clump_centre, clump_motion = (
        pltpu.with_memory_space_constraint(v, pltpu.HBM)
        for v in (sphere_offset, clump_centre, clump_motion)
    )
    clump_angles, clump_inverse_mass, clump_inverse_inertia = (
        pltpu.with_memory_space_constraint(v, pltpu.HBM)
        for v in (clump_angles, clump_inverse_mass, clump_inverse_inertia)
    )
    ext, hot_piece, hot_clump, route_rows, inside, tables = pl.pallas_call(
        functools.partial(halo_kernel, n_shaft, n_lat),
        out_shape=(
            jax.ShapeDtypeStruct((3, 4, 8, 8, 128), F32),
            jax.ShapeDtypeStruct((n_piece, 2048), BF16),
            jax.ShapeDtypeStruct((n_clump, n_piece), BF16),
            jax.ShapeDtypeStruct((8, n_piece), jnp.int32),
            jax.ShapeDtypeStruct((128, 128), F32),
            jax.ShapeDtypeStruct((16, KEYS, TERMS * 128), BF16),
        ),
        in_specs=[HBM] * 6,
        out_specs=(VMEM,) * 6,
        scratch_shapes=[
            pltpu.VMEM(sphere_piece.shape, jnp.int32),
            pltpu.VMEM(piece_route.shape, jnp.int32),
            pltpu.VMEM(piece_clump.shape, jnp.int32),
            pltpu.SemaphoreType.DMA((3, 4, 3)),
            pltpu.SemaphoreType.DMA((3, 4, 3)),
            pltpu.SemaphoreType.DMA((2, 3)),
            pltpu.SemaphoreType.DMA((3,)),
        ],
        compiler_params=pltpu.CompilerParams(
            collective_id=0, has_side_effects=True, vmem_limit_bytes=16 << 20
        ),
        name="halo",
    )(
        sphere_position,
        sphere_velocity,
        sphere_radius,
        sphere_piece,
        piece_route,
        piece_clump,
    )
    force = contact_call(
        2 * n_lat,
        blade_phase,
        ext.reshape(768, 128),
        inside,
        tables,
        sphere_offset,
    )
    table = pl.pallas_call(
        functools.partial(exchange_kernel, n_shaft, n_lat),
        out_shape=jax.ShapeDtypeStruct((9, 8, n_clump), F32),
        in_specs=[VMEM] * 4 + [HBM] * 4,
        out_specs=VMEM,
        scratch_shapes=[
            pltpu.VMEM(clump_motion.shape, F32),
            pltpu.VMEM(clump_inverse_mass.shape, F32),
            pltpu.VMEM(clump_angles.shape, F32),
            pltpu.VMEM(clump_inverse_inertia.shape, F32),
            pltpu.VMEM((9, 8, n_clump), F32),
            pltpu.VMEM((9, 8, n_clump), F32),
            pltpu.SemaphoreType.DMA((2, 9)),
            pltpu.SemaphoreType.DMA((2, 9)),
            pltpu.SemaphoreType.DMA((4,)),
        ],
        compiler_params=pltpu.CompilerParams(
            collective_id=1, has_side_effects=True, vmem_limit_bytes=16 << 20
        ),
        name="exchange",
    )(
        force,
        hot_piece,
        hot_clump,
        route_rows,
        clump_motion,
        clump_inverse_mass,
        clump_angles,
        clump_inverse_inertia,
    )
    return pl.pallas_call(
        spread_kernel,
        out_shape=(
            jax.ShapeDtypeStruct((9, 1, 1, n_clump), F32),
            jax.ShapeDtypeStruct((6, 1, 2, 8, 128), F32),
        ),
        in_specs=[VMEM] * 4 + [HBM] * 2,
        out_specs=(HBM, HBM),
        scratch_shapes=[
            pltpu.VMEM(clump_centre.shape, F32),
            pltpu.VMEM(sphere_offset.shape, F32),
            pltpu.VMEM((9, 1, 1, n_clump), F32),
            pltpu.VMEM((6, 1, 2, 8, 128), F32),
            pltpu.VMEM((128, 128), F32),
            pltpu.SemaphoreType.DMA((5,)),
        ],
        compiler_params=pltpu.CompilerParams(vmem_limit_bytes=16 << 20),
        name="spread",
    )(table, hot_piece, hot_clump, route_rows, clump_centre, sphere_offset)


def solution(mesh):
    placed = (
        P(None, "shaft", "lat", None, None),
        P(None, "shaft", "lat", None, None),
        P("shaft", "lat", None, None),
        P(None, "shaft", "lat", None, None),
        P("shaft", "lat", None),
        P("shaft", "lat", None),
        P("shaft", "lat", None),
        P(),
        P(None, "shaft", "lat", None),
        P(None, "shaft", "lat", None),
        P(None, "shaft", "lat", None),
        P("shaft", "lat", None),
        P(None, "shaft", "lat", None),
    )
    return jax.shard_map(
        functools.partial(on_device, mesh.shape["shaft"], mesh.shape["lat"]),
        mesh=mesh,
        in_specs=placed,
        out_specs=(P(None, "shaft", "lat", None), P(None, "shaft", "lat", None, None)),
        check_vma=False,
    )
```
